32 devices in a mesh: wide: 8 (over y, x, core), narrow: 4 (over z).
Axes of the slice: x: 2, y: 2, z: 4, core: 2. Of those that a mesh axis runs over, the one named last changes fastest.
Arguments:
- tokens: float32 [4488, 768], P('wide'), may hold values from -6 to 6
- region: int32 [4488], P('wide'), may hold values from 0 to 59, as said below
- order_rank: int32 [4488], P('wide'), may hold values from 0 to 559, as said below
- box_coords: int32 [2, 4488], P(None, 'wide'), may hold values from 0 to 127
- w_query: float32 [768, 768], P(None, 'narrow'), may hold values from -0.21875 to 0.21875
- b_query: float32 [768], P('narrow'), may hold values from -3 to 3
- w_key: float32 [768, 768], P(None, 'narrow'), may hold values from -0.21875 to 0.21875
- w_value: float32 [768, 768], P(None, 'narrow'), may hold values from -0.21875 to 0.21875
- b_value: float32 [768], P('narrow'), may hold values from -0.18 to 0.18
- w_out: float32 [768, 768], P('narrow'), may hold values from -2 to 2
- b_out: float32 [768], replicated, may hold values from -2 to 2
- ln1_gain: float32 [768], replicated, may hold values from 0.1 to 1.9
- ln1_bias: float32 [768], replicated, may hold values from -2 to 2
- w_in: float32 [768, 3072], P(None, 'narrow'), may hold values from -0.21875 to 0.21875
- b_in: float32 [3072], P('narrow'), may hold values from -2 to 2
- w_down: float32 [3072, 768], P('narrow'), may hold values from -0.109375 to 0.109375
- b_down: float32 [768], replicated, may hold values from -2 to 2
- ln2_gain: float32 [768], replicated, may hold values from 0.1 to 1.9
- ln2_bias: float32 [768], replicated, may hold values from -2 to 2
- rel_order: float32 [12, 32], P('narrow'), may hold values from -3 to 3
- rel_x: float32 [12, 64], P('narrow'), may hold values from -3 to 3
- rel_y: float32 [12, 64], P('narrow'), may hold values from -3 to 3
- cotangent: float32 [4488, 768], P('wide'), may hold values from -6 to 6
Outputs:
- output: float32 [4488, 768], P('wide')
- grad_input: float32 [4488, 768], P('wide')
- grad_w_query: float32 [768, 768], P(None, 'narrow')
- grad_b_query: float32 [768], P('narrow')
- grad_w_key: float32 [768, 768], P(None, 'narrow')
- grad_w_value: float32 [768, 768], P(None, 'narrow')
- grad_b_value: float32 [768], P('narrow')
- grad_w_out: float32 [768, 768], P('narrow')
- grad_b_out: float32 [768], replicated
- grad_ln1_gain: float32 [768], replicated
- grad_ln1_bias: float32 [768], replicated
- grad_w_in: float32 [768, 3072], P(None, 'narrow')
- grad_b_in: float32 [3072], P('narrow')
- grad_w_down: float32 [3072, 768], P('narrow')
- grad_b_down: float32 [768], replicated
- grad_ln2_gain: float32 [768], replicated
- grad_ln2_bias: float32 [768], replicated
- grad_rel_order: float32 [12, 32], P('narrow')
- grad_rel_x: float32 [12, 64], P('narrow')
- grad_rel_y: float32 [12, 64], P('narrow')
The draws below stay inside these ranges and needn't reach their ends.
Inputs may be any that keep to these rules, and one draw needn't show every extreme that they name: Each page's region ids take every value from 0 to its region count minus 1; region counts run from 2 to min(60, 561), and one page has the most. `order_rank`: within each region of a page the ranks are 0, 1, and so on up to its size minus 1, each once; no region holds more than 560 tokens, and one page has a region of exactly 560 tokens.
All inputs are finite; a program needn't handle non-finite values.
Results may differ from the reference program's by a relative error of at most 0.015.
The reference program's roundings to bfloat16 on the way count: a program that leaves them out, or rounds other values in their place, can miss the bound.
Values sent between devices are 32-bit elements; how exact they have to be, the bound alone decides.
A program may use at most 128 MiB of HBM per device.

```python
import math
import jax
import jax.numpy as jnp
from jax import lax

D = 768
HEADS = 12
HEAD_DIM = 64
FF = 3072
BINS1 = 32
BINS2 = 64
MAX_ORDER = 128
MAX_LAYOUT = 256
COORD = 128
PAGE = 561
PAGES = 8
TOKENS = 4488


def reading_layout(key):
    count_key, cut_key, place_key = jax.random.split(jax.random.fold_in(key, 11), 3)
    cut_limit = min(59, PAGE - 1)
    page_index = jnp.arange(PAGES)
    region_count = jax.random.randint(count_key, (PAGES,), 2, cut_limit + 2)
    region_count = jnp.where(page_index == 0, cut_limit + 1, region_count)
    region_count = jnp.where(page_index == PAGES - 1, 2, region_count)
    cut_keys = jax.random.split(cut_key, PAGES)
    cut_points = jax.vmap(lambda one_key: jax.random.permutation(one_key, PAGE - 1))(cut_keys)[:, :cut_limit] + 1
    first_slot = jnp.arange(cut_limit)[None, :] == 0
    last_page = (page_index == PAGES - 1)[:, None]
    cut_points = jnp.where(first_slot & last_page, 1, cut_points)
    in_use = jnp.arange(cut_limit)[None, :] < region_count[:, None] - 1
    place_keys = jax.random.split(place_key, PAGES)
    read_place = jax.vmap(lambda one_key: jax.random.permutation(one_key, PAGE))(place_keys)
    passed = in_use[:, None, :] & (cut_points[:, None, :] <= read_place[:, :, None])
    region = jnp.sum(passed.astype(jnp.int32), axis=2)
    region_start = jnp.max(jnp.where(passed, cut_points[:, None, :], 0), axis=2)
    order_rank = read_place - region_start
    return (region.reshape(-1).astype(jnp.int32), order_rank.reshape(-1).astype(jnp.int32))


def draw_region(key, part):
    return reading_layout(key)[0]


def draw_order_rank(key, part):
    return reading_layout(key)[1]


def place_ends(entries, own_key, least, top_value):
    extent = entries.shape
    place = [jax.random.randint(jax.random.fold_in(own_key, axis), (), 0, extent[axis]) for axis in range(len(extent))]
    entries = entries.at[tuple(place)].set(least)
    longest = extent.index(max(extent))
    place[longest] = (place[longest] + 1) % extent[longest]
    return entries.at[tuple(place)].set(top_value)


def steps_of(own_key, dims, shards, smallest, high):
    def one(axis_at, shards_of):
        steps = jax.random.uniform(jax.random.fold_in(jax.random.fold_in(own_key, 6), axis_at), (shards_of,), jnp.float32, smallest / len(shards), high / len(shards))
        return jnp.repeat(jnp.exp(steps), dims[axis_at] // shards_of).reshape((-1,) + (1,) * (len(dims) - axis_at - 1))

    loudness = one(*shards[0])
    for cut in shards[1:]:
        loudness = loudness * one(*cut)
    return loudness


def bell_draw(rng, shape, deviation, limit, cuts=(), kind=jnp.bfloat16):
    gain = steps_of(rng, shape, cuts, -0.22, 0.18) if cuts else 1.0
    values = jax.random.normal(rng, shape, jnp.float32) * deviation * gain
    return jnp.minimum(jnp.maximum(values, -limit), limit).astype(kind)


def setup_inputs(seed: int = 0) -> dict:
    splits = jax.random.split(jax.random.key(seed), 24)
    tokens = bell_draw(splits[0], (TOKENS, D), 1.0, 6.0, ((0, 8),), jnp.float32)
    region = draw_region(jax.random.fold_in(splits[23], 71), 0)
    order_rank = draw_order_rank(jax.random.fold_in(splits[23], 71), 0)
    box_coords = place_ends(jax.random.randint(splits[3], (2, TOKENS), 0, COORD), jax.random.fold_in(splits[3], 1), 0, COORD - 1).astype(jnp.int32)
    w_query = bell_draw(splits[4], (D, D), D ** -0.5, 0.21875, ((1, 4),), jnp.float32)
    b_query = bell_draw(splits[5], (D,), 0.5, 3.0, ((0, 4),), jnp.float32)
    w_key = bell_draw(splits[6], (D, D), D ** -0.5, 0.21875, ((1, 4),), jnp.float32)
    w_value = bell_draw(splits[7], (D, D), D ** -0.5, 0.21875, ((1, 4),), jnp.float32)
    b_value = bell_draw(splits[8], (D,), 0.03, 0.18, ((0, 4),), jnp.float32)
    w_out = bell_draw(splits[9], (D, D), 8 ** -0.5, 2.0, ((0, 4),), jnp.float32)
    b_out = bell_draw(splits[10], (D,), 0.3, 2.0, (), jnp.float32)
    ln1_gain = jnp.clip(1.0 + 0.18 * jax.random.normal(splits[11], (D,), jnp.float32), 0.1, 1.9)
    ln1_bias = bell_draw(splits[12], (D,), 0.3, 2.0, (), jnp.float32)
    w_in = bell_draw(splits[13], (D, FF), D ** -0.5, 0.21875, ((1, 4),), jnp.float32)
    b_in = bell_draw(splits[14], (FF,), 0.3, 2.0, ((0, 4),), jnp.float32)
    w_down = bell_draw(splits[15], (FF, D), FF ** -0.5, 0.109375, ((0, 4),), jnp.float32)
    b_down = bell_draw(splits[16], (D,), 0.3, 2.0, (), jnp.float32)
    ln2_gain = jnp.clip(1.0 + 0.18 * jax.random.normal(splits[17], (D,), jnp.float32), 0.1, 1.9)
    ln2_bias = bell_draw(splits[18], (D,), 0.3, 2.0, (), jnp.float32)
    rel_order = bell_draw(splits[19], (HEADS, BINS1), 0.5, 3.0, ((0, 4),), jnp.float32)
    rel_x = bell_draw(splits[20], (HEADS, BINS2), 0.5, 3.0, ((0, 4),), jnp.float32)
    rel_y = bell_draw(splits[21], (HEADS, BINS2), 0.5, 3.0, ((0, 4),), jnp.float32)
    cotangent = bell_draw(splits[22], (TOKENS, D), 1.0, 6.0, ((0, 8),), jnp.float32)
    return {"tokens": tokens, "region": region, "order_rank": order_rank, "box_coords": box_coords, "w_query": w_query, "b_query": b_query, "w_key": w_key, "w_value": w_value, "b_value": b_value, "w_out": w_out, "b_out": b_out, "ln1_gain": ln1_gain, "ln1_bias": ln1_bias, "w_in": w_in, "b_in": b_in, "w_down": w_down, "b_down": b_down, "ln2_gain": ln2_gain, "ln2_bias": ln2_bias, "rel_order": rel_order, "rel_x": rel_x, "rel_y": rel_y, "cotangent": cotangent}


@jax.custom_vjp
def low(v):
    return lax.optimization_barrier(v.astype(jnp.bfloat16)).astype(jnp.float32)

@jax.custom_vjp
def low_back(v):
    return v

def low_keep(v):
    return (low(v), None)

def low_pass(kept, grad):
    return (grad,)

def back_keep(v):
    return (v, None)

def back_low(kept, grad):
    return (low(grad),)
low.defvjp(low_keep, low_pass)
low_back.defvjp(back_keep, back_low)
HIGHEST = lax.Precision.HIGHEST
EPSILON = 1e-05
SCORE_SCALE = 0.125

def bucket_steps(bins, reach):
    halfway = bins // 2
    exact = halfway // 2
    steps = []
    for level in range(1, halfway):
        if level < exact:
            steps.append(level)
        else:
            found = reach + 1
            for count in range(exact, reach + 2):
                value = exact + int(math.log(count / exact) / math.log(reach / exact) * (halfway - exact))
                if min(value, halfway - 1) >= level:
                    found = count
                    break
            steps.append(found)
    return steps

def bucket_of(offset_grid, bins, reach):
    halfway = bins // 2
    magnitude = jnp.abs(offset_grid)
    result = jnp.where(offset_grid > 0, halfway, 0).astype(jnp.int32)
    for level_start in bucket_steps(bins, reach):
        result = result + (magnitude >= level_start).astype(jnp.int32)
    return result

def matmul(left, right):
    return jnp.dot(left, right, precision=HIGHEST, preferred_element_type=jnp.float32)

def norm_layer(values, gain_row, shift_row):
    average = lax.optimization_barrier(jnp.mean(values, axis=-1, keepdims=True))
    centred = values - average
    second = lax.optimization_barrier(jnp.mean(centred * centred, axis=-1, keepdims=True))
    return centred * lax.rsqrt(second + EPSILON) * gain_row + shift_row

def layer_page(params, tokens, region, order_rank, box_coords):
    w_query, b_query, w_key, w_value, b_value, w_out, b_out, ln1_gain, ln1_bias, w_in, b_in, w_down, b_down, ln2_gain, ln2_bias, rel_order, rel_x, rel_y = params
    earlier = (region[None, :] < region[:, None]).astype(jnp.int32)
    read_place = (lax.optimization_barrier(jnp.sum(earlier, axis=1)) + order_rank).astype(jnp.int32)
    order_bin = bucket_of(read_place[None, :] - read_place[:, None], BINS1, MAX_ORDER)
    across_bin = bucket_of(box_coords[0][None, :] - box_coords[0][:, None], BINS2, MAX_LAYOUT)
    down_bin = bucket_of(box_coords[1][None, :] - box_coords[1][:, None], BINS2, MAX_LAYOUT)
    rel_bias = rel_order[:, order_bin] + rel_x[:, across_bin] + rel_y[:, down_bin]
    tokens_low = low(tokens)
    query_rows = low_back(low(matmul(tokens_low, low(w_query)) + b_query))
    key_rows = low_back(low(matmul(tokens_low, low(w_key))))
    value_rows = low_back(low(matmul(tokens_low, low(w_value)) + b_value))
    shape_heads = (PAGE, HEADS, HEAD_DIM)
    scores = jnp.einsum('qhe,khe->hqk', query_rows.reshape(shape_heads), key_rows.reshape(shape_heads), precision=HIGHEST) * SCORE_SCALE + rel_bias
    scores = low_back(scores)
    attention = jax.nn.softmax(scores, axis=-1)
    mixed = jnp.einsum('hqk,khe->qhe', low(attention), value_rows.reshape(shape_heads), precision=HIGHEST)
    attended = low_back(low(mixed.reshape(PAGE, D)))
    branch = low_back(matmul(attended, low(w_out)) + b_out)
    hidden = norm_layer(tokens + branch, ln1_gain, ln1_bias)
    pre_gelu = low_back(matmul(low(hidden), low(w_in)) + b_in)
    active = low(jax.nn.gelu(pre_gelu, approximate=False))
    ff_out = low_back(matmul(active, low(w_down)) + b_down)
    return norm_layer(hidden + ff_out, ln2_gain, ln2_bias)

def reference(tokens, region, order_rank, box_coords, w_query, b_query, w_key, w_value, b_value, w_out, b_out, ln1_gain, ln1_bias, w_in, b_in, w_down, b_down, ln2_gain, ln2_bias, rel_order, rel_x, rel_y, cotangent):
    params = (w_query, b_query, w_key, w_value, b_value, w_out, b_out, ln1_gain, ln1_bias, w_in, b_in, w_down, b_down, ln2_gain, ln2_bias, rel_order, rel_x, rel_y)
    group_size = math.gcd(PAGES, 4)
    rounds = PAGES // group_size
    token_groups = tokens.reshape(rounds, group_size, PAGE, D)
    region_groups = region.reshape(rounds, group_size, PAGE)
    rank_groups = order_rank.reshape(rounds, group_size, PAGE)
    box_groups = jnp.moveaxis(box_coords.reshape(2, rounds, group_size, PAGE), 0, 2)
    cot_groups = cotangent.reshape(rounds, group_size, PAGE, D)

    def one_round(running, inputs):
        token_block, region_block, rank_block, box_block, cot_block = inputs

        def run_pages(param_set, token_set):
            return jax.vmap(layer_page, in_axes=(None, 0, 0, 0, 0))(param_set, token_set, region_block, rank_block, box_block)
        page_out, back_fn = jax.vjp(run_pages, params, token_block)
        grad_params, grad_tokens = back_fn(cot_block)
        running = jax.tree.map(jnp.add, running, grad_params)
        return (running, (page_out, grad_tokens))
    start_sums = jax.tree.map(jnp.zeros_like, params)
    totals, (outputs, grad_groups) = lax.scan(one_round, start_sums, (token_groups, region_groups, rank_groups, box_groups, cot_groups))
    grad_w_query, grad_b_query, grad_w_key, grad_w_value, grad_b_value, grad_w_out, grad_b_out, grad_ln1_gain, grad_ln1_bias, grad_w_in, grad_b_in, grad_w_down, grad_b_down, grad_ln2_gain, grad_ln2_bias, grad_rel_order, grad_rel_x, grad_rel_y = totals
    return (outputs.reshape(TOKENS, D), grad_groups.reshape(TOKENS, D), grad_w_query, grad_b_query, grad_w_key, grad_w_value, grad_b_value, grad_w_out, grad_b_out, grad_ln1_gain, grad_ln1_bias, grad_w_in, grad_b_in, grad_w_down, grad_b_down, grad_ln2_gain, grad_ln2_bias, grad_rel_order, grad_rel_x, grad_rel_y)
```

```python
import math

import jax
import jax.numpy as jnp
from jax import lax
from jax.sharding import PartitionSpec as P

HEAD_DIM = 64
BINS1 = 32
BINS2 = 64
MAX_ORDER = 128
MAX_LAYOUT = 256
PAGE = 561


HIGHEST = lax.Precision.HIGHEST
EPSILON = 1e-05
SCORE_SCALE = 0.125


def bucket_steps(bins, reach):
    halfway = bins // 2
    exact = halfway // 2
    steps = []
    for level in range(1, halfway):
        if level < exact:
            steps.append(level)
        else:
            found = reach + 1
            for count in range(exact, reach + 2):
                value = exact + int(
                    math.log(count / exact) / math.log(reach / exact) * (halfway - exact)
                )
                if min(value, halfway - 1) >= level:
                    found = count
                    break
            steps.append(found)
    return steps


def bucket_of(offset_grid, bins, reach):
    halfway = bins // 2
    magnitude = jnp.abs(offset_grid)
    result = jnp.where(offset_grid > 0, halfway, 0).astype(jnp.int32)
    for level_start in bucket_steps(bins, reach):
        result = result + (magnitude >= level_start).astype(jnp.int32)
    return result


def norm_layer(values, gain_row, shift_row):
    average = jnp.mean(values, axis=-1, keepdims=True)
    centred = values - average
    second = jnp.mean(centred * centred, axis=-1, keepdims=True)
    return centred * lax.rsqrt(second + EPSILON) * gain_row + shift_row


def gelu_exact(values):
    return jax.nn.gelu(values, approximate=False)


def reading_place(region, order_rank):
    earlier = (region[:, None, :] < region[:, :, None]).astype(jnp.int32)
    return (jnp.sum(earlier, axis=2) + order_rank).astype(jnp.int32)


def page_buckets(place_row, across_row, down_row):
    order_bin = bucket_of(place_row[None, :] - place_row[:, None], BINS1, MAX_ORDER)
    across_bin = bucket_of(across_row[None, :] - across_row[:, None], BINS2, MAX_LAYOUT)
    down_bin = bucket_of(down_row[None, :] - down_row[:, None], BINS2, MAX_LAYOUT)
    return (order_bin, across_bin, down_bin)


def one_hot_of(grid, bins, dtype):
    return (grid[:, :, None] == jnp.arange(bins, dtype=jnp.int32)[None, None, :]).astype(dtype)


def relative_bias(tables, read_place, across, downward):

    def relative_one_page(inputs):
        grids = page_buckets(inputs[0], inputs[1], inputs[2])
        total = None
        for table, grid in zip(tables, grids):
            chooser = one_hot_of(grid, table.shape[1], jnp.float32)
            term = jnp.einsum(
                "hb,qkb->hqk", table, chooser, precision=HIGHEST, preferred_element_type=jnp.float32
            )
            total = term if total is None else total + term
        return total

    return lax.map(relative_one_page, (read_place, across, downward))


def table_grads(grad_scores, bins_list, read_place, across, downward):

    def table_one_page(inputs):
        grad_page = inputs[0]
        grids = page_buckets(inputs[1], inputs[2], inputs[3])
        return tuple(
            (
                jnp.einsum(
                    "hqk,qkb->hb",
                    grad_page,
                    one_hot_of(grid, bins, jnp.bfloat16),
                    preferred_element_type=jnp.float32,
                )
                for grid, bins in zip(grids, bins_list)
            )
        )

    per_page = lax.map(table_one_page, (grad_scores, read_place, across, downward))
    return tuple((jnp.sum(member, axis=0) for member in per_page))


def forward(tokens, lowered, biases, rel_bias):
    query_weight, key_weight, value_weight, out_weight, in_weight, down_weight = lowered
    b_query, b_value, b_out, ln1_gain, ln1_bias, b_in, b_down, ln2_gain, ln2_bias = biases
    page_count, head_count, length = (rel_bias.shape[0], rel_bias.shape[1], rel_bias.shape[2])
    shape_heads = (page_count, length, head_count, HEAD_DIM)
    tokens_low = tokens.astype(jnp.bfloat16)
    query_rows = (
        jnp.dot(tokens_low, query_weight, preferred_element_type=jnp.float32) + b_query
    ).astype(jnp.bfloat16)
    key_rows = jnp.dot(tokens_low, key_weight, preferred_element_type=jnp.float32).astype(
        jnp.bfloat16
    )
    value_rows = (
        jnp.dot(tokens_low, value_weight, preferred_element_type=jnp.float32) + b_value
    ).astype(jnp.bfloat16)
    scores = (
        jnp.einsum(
            "pqhe,pkhe->phqk",
            query_rows.reshape(shape_heads),
            key_rows.reshape(shape_heads),
            preferred_element_type=jnp.float32,
        )
        * SCORE_SCALE
        + rel_bias
    )
    row_top = jnp.max(scores, axis=-1, keepdims=True)
    raised = jnp.exp(scores - row_top)
    row_total = jnp.sum(raised, axis=-1, keepdims=True)
    attention = raised / row_total
    log_total = row_top + jnp.log(row_total)
    mixed = jnp.einsum(
        "phqk,pkhe->pqhe",
        attention.astype(jnp.bfloat16),
        value_rows.reshape(shape_heads),
        preferred_element_type=jnp.float32,
    )
    attended = mixed.reshape(tokens.shape[0], -1).astype(jnp.bfloat16)
    partial_value = jnp.dot(attended, out_weight, preferred_element_type=jnp.float32)
    branch = lax.psum(partial_value, "narrow") + b_out
    residual_one = tokens + branch
    hidden = norm_layer(residual_one, ln1_gain, ln1_bias)
    hidden_low = hidden.astype(jnp.bfloat16)
    pre_gelu = jnp.dot(hidden_low, in_weight, preferred_element_type=jnp.float32) + b_in
    active = gelu_exact(pre_gelu).astype(jnp.bfloat16)
    ff_part = jnp.dot(active, down_weight, preferred_element_type=jnp.float32)
    residual_two = hidden + (lax.psum(ff_part, "narrow") + b_down)
    output = norm_layer(residual_two, ln2_gain, ln2_bias)
    kept_values = (
        tokens_low,
        query_rows,
        key_rows,
        value_rows,
        log_total,
        attended,
        residual_one,
        hidden_low,
        pre_gelu,
        active,
        residual_two,
    )
    return (output, kept_values)


def local(
    tokens,
    region,
    order_rank,
    box_coords,
    w_query,
    b_query,
    w_key,
    w_value,
    b_value,
    w_out,
    b_out,
    ln1_gain,
    ln1_bias,
    w_in,
    b_in,
    w_down,
    b_down,
    ln2_gain,
    ln2_bias,
    rel_order,
    rel_x,
    rel_y,
    cotangent,
):
    length = PAGE
    page_count = tokens.shape[0] // length
    read_place = reading_place(
        region.reshape(page_count, length), order_rank.reshape(page_count, length)
    )
    corners = box_coords.reshape(2, page_count, length)
    rel_bias = relative_bias((rel_order, rel_x, rel_y), read_place, corners[0], corners[1])
    lowered = tuple(
        (weight.astype(jnp.bfloat16) for weight in (w_query, w_key, w_value, w_out, w_in, w_down))
    )
    query_weight, key_weight, value_weight, out_weight, in_weight, down_weight = lowered
    biases = (b_query, b_value, b_out, ln1_gain, ln1_bias, b_in, b_down, ln2_gain, ln2_bias)
    output, kept_values = forward(tokens, lowered, biases, rel_bias)
    (
        tokens_low,
        query_rows,
        key_rows,
        value_rows,
        log_total,
        attended,
        residual_one,
        hidden_low,
        pre_gelu,
        active,
        residual_two,
    ) = kept_values
    head_count = rel_bias.shape[1]
    shape_heads = (page_count, length, head_count, HEAD_DIM)
    head_width = head_count * HEAD_DIM
    _, second_back = jax.vjp(norm_layer, residual_two, ln2_gain, ln2_bias)
    grad_residual_two, grad_ln2_gain, grad_ln2_bias = second_back(cotangent)
    grad_ff = grad_residual_two.astype(jnp.bfloat16)
    grad_b_down = jnp.sum(grad_ff, axis=0, dtype=jnp.float32)
    grad_w_down = jnp.einsum("tf,td->fd", active, grad_ff, preferred_element_type=jnp.float32)
    grad_active = jnp.einsum("td,fd->tf", grad_ff, down_weight, preferred_element_type=jnp.float32)
    _, gelu_back = jax.vjp(gelu_exact, pre_gelu)
    grad_pre = gelu_back(grad_active)[0].astype(jnp.bfloat16)
    grad_b_in = jnp.sum(grad_pre, axis=0, dtype=jnp.float32)
    grad_w_in = jnp.einsum("td,tf->df", hidden_low, grad_pre, preferred_element_type=jnp.float32)
    hidden_part = jnp.einsum("tf,df->td", grad_pre, in_weight, preferred_element_type=jnp.float32)
    grad_hidden = grad_residual_two + lax.psum(hidden_part, "narrow")
    _, first_back = jax.vjp(norm_layer, residual_one, ln1_gain, ln1_bias)
    grad_residual_one, grad_ln1_gain, grad_ln1_bias = first_back(grad_hidden)
    grad_branch = grad_residual_one.astype(jnp.bfloat16)
    grad_b_out = jnp.sum(grad_branch, axis=0, dtype=jnp.float32)
    grad_w_out = jnp.einsum("tc,td->cd", attended, grad_branch, preferred_element_type=jnp.float32)
    grad_attended = jnp.einsum(
        "td,cd->tc", grad_branch, out_weight, preferred_element_type=jnp.float32
    ).astype(jnp.bfloat16)
    query_heads = query_rows.reshape(shape_heads)
    key_heads = key_rows.reshape(shape_heads)
    value_heads = value_rows.reshape(shape_heads)
    grad_heads = grad_attended.reshape(shape_heads)
    scores = (
        jnp.einsum("pqhe,pkhe->phqk", query_heads, key_heads, preferred_element_type=jnp.float32)
        * SCORE_SCALE
        + rel_bias
    )
    attention = jnp.exp(scores - log_total)
    grad_attention = jnp.einsum(
        "pqhe,pkhe->phqk", grad_heads, value_heads, preferred_element_type=jnp.float32
    )
    inner_sum = jnp.sum(attention * grad_attention, axis=-1, keepdims=True)
    grad_scores = (attention * (grad_attention - inner_sum)).astype(jnp.bfloat16)
    grad_rel_order, grad_rel_x, grad_rel_y = table_grads(
        grad_scores, (BINS1, BINS2, BINS2), read_place, corners[0], corners[1]
    )
    grad_query = (
        (
            jnp.einsum(
                "phqk,pkhe->pqhe", grad_scores, key_heads, preferred_element_type=jnp.float32
            )
            * SCORE_SCALE
        )
        .astype(jnp.bfloat16)
        .reshape(-1, head_width)
    )
    grad_key = (
        (
            jnp.einsum(
                "phqk,pqhe->pkhe", grad_scores, query_heads, preferred_element_type=jnp.float32
            )
            * SCORE_SCALE
        )
        .astype(jnp.bfloat16)
        .reshape(-1, head_width)
    )
    grad_value = (
        jnp.einsum(
            "phqk,pqhe->pkhe",
            attention.astype(jnp.bfloat16),
            grad_heads,
            preferred_element_type=jnp.float32,
        )
        .astype(jnp.bfloat16)
        .reshape(-1, head_width)
    )
    grad_b_query = jnp.sum(grad_query, axis=0, dtype=jnp.float32)
    grad_b_value = jnp.sum(grad_value, axis=0, dtype=jnp.float32)
    grad_w_query = jnp.einsum(
        "td,tc->dc", tokens_low, grad_query, preferred_element_type=jnp.float32
    )
    grad_w_key = jnp.einsum("td,tc->dc", tokens_low, grad_key, preferred_element_type=jnp.float32)
    grad_w_value = jnp.einsum(
        "td,tc->dc", tokens_low, grad_value, preferred_element_type=jnp.float32
    )
    input_part = jnp.einsum(
        "tc,dc->td", grad_query, query_weight, preferred_element_type=jnp.float32
    )
    input_part = input_part + jnp.einsum(
        "tc,dc->td", grad_key, key_weight, preferred_element_type=jnp.float32
    )
    input_part = input_part + jnp.einsum(
        "tc,dc->td", grad_value, value_weight, preferred_element_type=jnp.float32
    )
    grad_input = grad_residual_one + lax.psum(input_part, "narrow")
    (
        grad_w_query,
        grad_b_query,
        grad_w_key,
        grad_w_value,
        grad_b_value,
        grad_w_out,
        grad_b_out,
        grad_ln1_gain,
        grad_ln1_bias,
        grad_rel_order,
        grad_rel_x,
        grad_rel_y,
        grad_w_in,
        grad_b_in,
        grad_w_down,
        grad_b_down,
        grad_ln2_gain,
        grad_ln2_bias,
    ) = lax.psum(
        (
            grad_w_query,
            grad_b_query,
            grad_w_key,
            grad_w_value,
            grad_b_value,
            grad_w_out,
            grad_b_out,
            grad_ln1_gain,
            grad_ln1_bias,
            grad_rel_order,
            grad_rel_x,
            grad_rel_y,
            grad_w_in,
            grad_b_in,
            grad_w_down,
            grad_b_down,
            grad_ln2_gain,
            grad_ln2_bias,
        ),
        "wide",
    )
    return (
        output,
        grad_input,
        grad_w_query,
        grad_b_query,
        grad_w_key,
        grad_w_value,
        grad_b_value,
        grad_w_out,
        grad_b_out,
        grad_ln1_gain,
        grad_ln1_bias,
        grad_w_in,
        grad_b_in,
        grad_w_down,
        grad_b_down,
        grad_ln2_gain,
        grad_ln2_bias,
        grad_rel_order,
        grad_rel_x,
        grad_rel_y,
    )


def solution(mesh):
    in_specs = (
        P("wide", None),
        P("wide"),
        P("wide"),
        P(None, "wide"),
        P(None, "narrow"),
        P("narrow"),
        P(None, "narrow"),
        P(None, "narrow"),
        P("narrow"),
        P("narrow", None),
        P(),
        P(),
        P(),
        P(None, "narrow"),
        P("narrow"),
        P("narrow", None),
        P(),
        P(),
        P(),
        P("narrow", None),
        P("narrow", None),
        P("narrow", None),
        P("wide", None),
    )
    out_specs = (
        P("wide", None),
        P("wide", None),
        P(None, "narrow"),
        P("narrow"),
        P(None, "narrow"),
        P(None, "narrow"),
        P("narrow"),
        P("narrow", None),
        P(),
        P(),
        P(),
        P(None, "narrow"),
        P("narrow"),
        P("narrow", None),
        P(),
        P(),
        P(),
        P("narrow", None),
        P("narrow", None),
        P("narrow", None),
    )
    return jax.shard_map(local, mesh=mesh, in_specs=in_specs, out_specs=out_specs, check_vma=False)
```

```python
import math

import jax
import jax.numpy as jnp
from jax import lax
from jax.experimental import pallas as pl
from jax.experimental.pallas import tpu as pltpu
from jax.sharding import PartitionSpec as P

HEAD_DIM = 64
BINS1 = 32
BINS2 = 64
MAX_ORDER = 128
MAX_LAYOUT = 256
PAGE = 561


HIGHEST = lax.Precision.HIGHEST
EPSILON = 1e-05
SCORE_SCALE = 0.125


def bucket_steps(bins, reach):
    halfway = bins // 2
    exact = halfway // 2
    steps = []
    for level in range(1, halfway):
        if level < exact:
            steps.append(level)
        else:
            found = reach + 1
            for count in range(exact, reach + 2):
                value = exact + int(
                    math.log(count / exact) / math.log(reach / exact) * (halfway - exact)
                )
                if min(value, halfway - 1) >= level:
                    found = count
                    break
            steps.append(found)
    return steps


def bucket_of(offset_grid, bins, reach):
    halfway = bins // 2
    magnitude = jnp.abs(offset_grid)
    result = jnp.where(offset_grid > 0, halfway, 0).astype(jnp.int32)
    for level_start in bucket_steps(bins, reach):
        result = result + (magnitude >= level_start).astype(jnp.int32)
    return result


MESH = pl.DeviceIdType.MESH
CH = 96
PC = 48


def erf_of(x):
    x = jnp.clip(x, -3.832506856900711, 3.832506856900711)
    s = x * x
    top = -2.72614225801306e-10
    for term in (2.77068142495902e-08, -2.10102402082508e-06, -5.69250639462346e-05,
                 -7.34990630326855e-04, -2.95459980854025e-03, -1.60960333262415e-02):
        top = top * s + term
    low = -1.45660718464996e-05
    for term in (-2.13374055278905e-04, -1.68282697438203e-03, -7.37332916720468e-03,
                 -1.42647390514189e-02):
        low = low * s + term
    return x * top / low


def normal_cdf(x):
    return 0.5 + 0.5 * erf_of(x * math.sqrt(0.5))


def centre(values):
    c = values - jnp.mean(values, axis=-1, keepdims=True)
    r = lax.rsqrt(jnp.mean(c * c, axis=-1, keepdims=True) + EPSILON)
    return c * r, r


def norm_back(g, n, r, gain):
    m = g * gain
    return r * (m - jnp.mean(m, axis=-1, keepdims=True) - n * jnp.mean(m * n, axis=-1, keepdims=True))


def dot_nn(a, b):
    return lax.dot_general(a, b, (((1,), (0,)), ((), ())), preferred_element_type=jnp.float32)


def dot_nt(a, b):
    return lax.dot_general(a, b, (((1,), (1,)), ((), ())), preferred_element_type=jnp.float32)


def dot_tn(a, b):
    return lax.dot_general(a, b, (((0,), (0,)), ((), ())), preferred_element_type=jnp.float32)


class LineSum:
    def __init__(self, part, rx_in, rx_mid, tot, s_in, s_mid, r_in, r_mid):
        self.part, self.rx_in, self.rx_mid, self.tot = part, rx_in, rx_mid, tot
        self.s_in, self.s_mid, self.r_in, self.r_mid = s_in, s_mid, r_in, r_mid
        w, n = lax.axis_index("wide"), lax.axis_index("narrow")
        self.end = (n == 0) | (n == 3)
        self.mid = jnp.logical_not(self.end)
        self.side = (w, n + 1 - 2 * lax.rem(n, 2))
        self.across = (w, 3 - n)
        self.pieces = part.shape[0] // PC

    def rows(self, p):
        return pl.ds(pl.multiple_of(p * PC, PC), PC)

    def copy_a(self, p):
        return pltpu.make_async_remote_copy(self.part.at[self.rows(p)], self.rx_in.at[self.rows(p)],
            self.s_in.at[p], self.r_in.at[p], device_id=self.side, device_id_type=MESH)

    def copy_b(self, p):
        return pltpu.make_async_remote_copy(self.part.at[self.rows(p)], self.rx_mid.at[self.rows(p)],
            self.s_mid.at[p], self.r_mid.at[p], device_id=self.across, device_id_type=MESH)

    def copy_t(self, p):
        return pltpu.make_async_remote_copy(self.tot.at[self.rows(p)], self.tot.at[self.rows(p)],
            self.s_in.at[p], self.r_in.at[p], device_id=self.side, device_id_type=MESH)

    def barrier(self):
        bar = pltpu.get_barrier_semaphore()
        pl.semaphore_signal(bar, inc=1, device_id=self.side, device_id_type=MESH)

        @pl.when(self.mid)
        def _():
            pl.semaphore_signal(bar, inc=1, device_id=self.across, device_id_type=MESH)

        @pl.when(self.end)
        def _():
            pl.semaphore_wait(bar, 1)

        @pl.when(self.mid)
        def _():
            pl.semaphore_wait(bar, 2)

    def free_part(self, p):
        @pl.when(self.end)
        def _():
            self.copy_a(p).wait_send()

        @pl.when(self.mid)
        def _():
            self.copy_b(p).wait_send()

    def finish(self, p, first):
        self.copy_b(p).wait_recv()
        if not first:
            self.copy_t(p).wait_send()
        self.tot[self.rows(p), :] = self.part[self.rows(p), :] + self.rx_mid[self.rows(p), :]
        self.copy_t(p).start()

    def slot(self, p, order):
        @pl.when(self.end)
        def _():
            self.copy_a(p).start()

        @pl.when(self.mid)
        def _():
            self.copy_a(p).wait_recv()
            self.part[self.rows(p), :] += self.rx_in[self.rows(p), :]
            self.copy_b(p).start()

            @pl.when(p > 0)
            def _():
                self.finish(p - 1, order == 0)

            if order > 0:
                @pl.when(p == 0)
                def _():
                    self.finish(self.pieces - 1, order == 1)

    def last(self, first):
        @pl.when(self.mid)
        def _():
            self.finish(self.pieces - 1, first)

    def want(self, p):
        @pl.when(self.end)
        def _():
            self.copy_t(p).wait_recv()

    def drain(self):
        def one(p, c):
            self.free_part(p)

            @pl.when(self.mid)
            def _():
                self.copy_t(p).wait_send()
            return c
        lax.fori_loop(0, self.pieces, one, 0)


def middle_kernel(tok_ref, cot_ref, att_ref, w_out_ref, w_in_ref, w_down_ref, vec_ref,
                  out_ref, gres_ref, dwin_ref, dwdown_ref, small_ref,
                  part, rx_in, rx_mid, tot, res, hid, pre, act, gff, hlow, gpre, wo, wi, wd,
                  s_in, s_mid, r_in, r_mid):
    line = LineSum(part, rx_in, rx_mid, tot, s_in, s_mid, r_in, r_mid)
    steps = part.shape[0] // CH
    k = CH // PC
    b_out, g1, b1, b_in = (vec_ref[i:i + 1, :] for i in range(4))
    b_down, g2, b2 = (vec_ref[i:i + 1, :] for i in range(4, 7))
    wo[...] = w_out_ref[...].astype(jnp.bfloat16)
    line.barrier()

    def rows(c):
        return pl.ds(pl.multiple_of(c * CH, CH), CH)

    def branch_step(c, carry):
        r = rows(c)
        part[r, :] = dot_nn(att_ref[r, :], wo[...])
        for j in range(k):
            line.slot(c * k + j, 0)
        return carry
    lax.fori_loop(0, steps, branch_step, 0)
    wi[...] = w_in_ref[...].astype(jnp.bfloat16)
    wd[...] = w_down_ref[...].astype(jnp.bfloat16)
    small_ref[...] = jnp.zeros_like(small_ref)

    def open_step(c):
        for j in range(k):
            line.want(c * k + j)
        for j in range(k):
            line.free_part(c * k + j)

    def forward_step(c, carry):
        r = rows(c)
        open_step(c)
        one = tok_ref[r, :] + (tot[r, :] + b_out)
        res[r, :] = one
        n, _ = centre(one)
        hidden = n * g1 + b1
        hid[r, :] = hidden
        low = hidden.astype(jnp.bfloat16)
        hlow[r, :] = low
        u = dot_nn(low, wi[...]) + b_in
        pre[r, :] = u
        a = (u * normal_cdf(u)).astype(jnp.bfloat16)
        act[r, :] = a
        part[r, :] = dot_nn(a, wd[...])
        for j in range(k):
            line.slot(c * k + j, 1)
        return carry
    lax.fori_loop(0, steps, forward_step, 0)

    def add_row(i, rows_value):
        small_ref[i:i + 1, :] += jnp.sum(rows_value, axis=0, keepdims=True)

    def back_step(c, carry):
        r = rows(c)
        open_step(c)
        two = hid[r, :] + (tot[r, :] + b_down)
        n, rs = centre(two)
        out_ref[r, :] = n * g2 + b2
        g = cot_ref[r, :]
        add_row(0, g * n)
        add_row(1, g)
        back = norm_back(g, n, rs, g2)
        hid[r, :] = back
        low = back.astype(jnp.bfloat16)
        gff[r, :] = low
        add_row(2, low.astype(jnp.float32))
        ga = dot_nt(low, wd[...])
        u = pre[r, :]
        slope = normal_cdf(u) + u * (jnp.exp(-0.5 * u * u) * (1.0 / math.sqrt(2.0 * math.pi)))
        gp = (ga * slope).astype(jnp.bfloat16)
        gpre[r, :] = gp
        add_row(3, gp.astype(jnp.float32))
        part[r, :] = dot_nt(gp, wi[...])
        for j in range(k):
            line.slot(c * k + j, 2)
        return carry
    lax.fori_loop(0, steps, back_step, 0)
    line.last(False)
    dwdown_ref[...] = dot_tn(act[...], gff[...])
    dwin_ref[...] = dot_tn(hlow[...], gpre[...])

    def close_step(c, carry):
        r = rows(c)
        for j in range(k):
            line.want(c * k + j)
        g = hid[r, :] + tot[r, :]
        n, rs = centre(res[r, :])
        add_row(4, g * n)
        add_row(5, g)
        back = norm_back(g, n, rs, g1)
        gres_ref[r, :] = back
        add_row(6, back.astype(jnp.bfloat16).astype(jnp.float32))
        return carry
    lax.fori_loop(0, steps, close_step, 0)
    line.drain()


def middle(tok, cot, att, w_out, w_in, w_down, vec):
    rows, d = tok.shape
    heads, f = w_out.shape[0], w_in.shape[1]
    pieces = rows // PC
    f32, bf = jnp.float32, jnp.bfloat16
    shapes = (jax.ShapeDtypeStruct((rows, d), f32), jax.ShapeDtypeStruct((rows, d), f32),
              jax.ShapeDtypeStruct((d, f), f32), jax.ShapeDtypeStruct((f, d), f32),
              jax.ShapeDtypeStruct((8, d), f32))
    vm = pl.BlockSpec(memory_space=pltpu.VMEM)
    big = [pltpu.VMEM((rows, d), f32) for _ in range(6)]
    return pl.pallas_call(
        middle_kernel, out_shape=shapes, in_specs=[vm] * 7, out_specs=[vm] * 5,
        scratch_shapes=big + [pltpu.VMEM((rows, f), f32), pltpu.VMEM((rows, f), bf), pltpu.VMEM((rows, d), bf),
                              pltpu.VMEM((rows, d), bf), pltpu.VMEM((rows, f), bf),
                              pltpu.VMEM((heads, d), bf), pltpu.VMEM((d, f), bf), pltpu.VMEM((f, d), bf)]
        + [pltpu.SemaphoreType.DMA((pieces,))] * 4,
        compiler_params=pltpu.CompilerParams(collective_id=0, has_side_effects=True, vmem_limit_bytes=56 << 20),
        cost_estimate=pl.CostEstimate(flops=6 * 2 * rows * d * f, bytes_accessed=20 << 20, transcendentals=rows * f),
    )(tok, cot, att, w_out, w_in, w_down, vec)


def norm_layer(values, gain_row, shift_row):
    average = jnp.mean(values, axis=-1, keepdims=True)
    centred = values - average
    second = jnp.mean(centred * centred, axis=-1, keepdims=True)
    return centred * lax.rsqrt(second + EPSILON) * gain_row + shift_row


def gelu_exact(values):
    return jax.nn.gelu(values, approximate=False)


def reading_place(region, order_rank):
    earlier = (region[:, None, :] < region[:, :, None]).astype(jnp.int32)
    return (jnp.sum(earlier, axis=2) + order_rank).astype(jnp.int32)


def page_buckets(place_row, across_row, down_row):
    order_bin = bucket_of(place_row[None, :] - place_row[:, None], BINS1, MAX_ORDER)
    across_bin = bucket_of(across_row[None, :] - across_row[:, None], BINS2, MAX_LAYOUT)
    down_bin = bucket_of(down_row[None, :] - down_row[:, None], BINS2, MAX_LAYOUT)
    return (order_bin, across_bin, down_bin)


def one_hot_of(grid, bins, dtype):
    return (grid[:, :, None] == jnp.arange(bins, dtype=jnp.int32)[None, None, :]).astype(dtype)


def relative_bias(tables, read_place, across, downward):

    def relative_one_page(inputs):
        grids = page_buckets(inputs[0], inputs[1], inputs[2])
        total = None
        for table, grid in zip(tables, grids):
            chooser = one_hot_of(grid, table.shape[1], jnp.float32)
            term = jnp.einsum(
                "hb,qkb->hqk", table, chooser, precision=HIGHEST, preferred_element_type=jnp.float32
            )
            total = term if total is None else total + term
        return total

    return lax.map(relative_one_page, (read_place, across, downward))


def table_grads(grad_scores, bins_list, read_place, across, downward):

    def table_one_page(inputs):
        grad_page = inputs[0]
        grids = page_buckets(inputs[1], inputs[2], inputs[3])
        return tuple(
            (
                jnp.einsum(
                    "hqk,qkb->hb",
                    grad_page,
                    one_hot_of(grid, bins, jnp.bfloat16),
                    preferred_element_type=jnp.float32,
                )
                for grid, bins in zip(grids, bins_list)
            )
        )

    per_page = lax.map(table_one_page, (grad_scores, read_place, across, downward))
    return tuple((jnp.sum(member, axis=0) for member in per_page))


def forward(tokens, lowered, biases, rel_bias):
    query_weight, key_weight, value_weight, out_weight, in_weight, down_weight = lowered
    b_query, b_value, b_out, ln1_gain, ln1_bias, b_in, b_down, ln2_gain, ln2_bias = biases
    page_count, head_count, length = (rel_bias.shape[0], rel_bias.shape[1], rel_bias.shape[2])
    shape_heads = (page_count, length, head_count, HEAD_DIM)
    tokens_low = tokens.astype(jnp.bfloat16)
    query_rows = (
        jnp.dot(tokens_low, query_weight, preferred_element_type=jnp.float32) + b_query
    ).astype(jnp.bfloat16)
    key_rows = jnp.dot(tokens_low, key_weight, preferred_element_type=jnp.float32).astype(
        jnp.bfloat16
    )
    value_rows = (
        jnp.dot(tokens_low, value_weight, preferred_element_type=jnp.float32) + b_value
    ).astype(jnp.bfloat16)
    scores = (
        jnp.einsum(
            "pqhe,pkhe->phqk",
            query_rows.reshape(shape_heads),
            key_rows.reshape(shape_heads),
            preferred_element_type=jnp.float32,
        )
        * SCORE_SCALE
        + rel_bias
    )
    row_top = jnp.max(scores, axis=-1, keepdims=True)
    raised = jnp.exp(scores - row_top)
    row_total = jnp.sum(raised, axis=-1, keepdims=True)
    attention = raised / row_total
    log_total = row_top + jnp.log(row_total)
    mixed = jnp.einsum(
        "phqk,pkhe->pqhe",
        attention.astype(jnp.bfloat16),
        value_rows.reshape(shape_heads),
        preferred_element_type=jnp.float32,
    )
    attended = mixed.reshape(tokens.shape[0], -1).astype(jnp.bfloat16)
    return tokens_low, query_rows, key_rows, value_rows, log_total, attended


def local(
    tokens,
    region,
    order_rank,
    box_coords,
    w_query,
    b_query,
    w_key,
    w_value,
    b_value,
    w_out,
    b_out,
    ln1_gain,
    ln1_bias,
    w_in,
    b_in,
    w_down,
    b_down,
    ln2_gain,
    ln2_bias,
    rel_order,
    rel_x,
    rel_y,
    cotangent,
):
    length = PAGE
    page_count = tokens.shape[0] // length
    read_place = reading_place(
        region.reshape(page_count, length), order_rank.reshape(page_count, length)
    )
    corners = box_coords.reshape(2, page_count, length)
    rel_bias = relative_bias((rel_order, rel_x, rel_y), read_place, corners[0], corners[1])
    lowered = tuple(
        (weight.astype(jnp.bfloat16) for weight in (w_query, w_key, w_value, w_out, w_in, w_down))
    )
    query_weight, key_weight, value_weight, out_weight, in_weight, down_weight = lowered
    biases = (b_query, b_value, b_out, ln1_gain, ln1_bias, b_in, b_down, ln2_gain, ln2_bias)
    tokens_low, query_rows, key_rows, value_rows, log_total, attended = forward(tokens, lowered, biases, rel_bias)
    extra = -length % 64
    pad = ((0, extra), (0, 0))
    vec = jnp.stack([b_out, ln1_gain, ln1_bias, b_in, b_down, ln2_gain, ln2_bias, b_down])
    output, grad_residual_one, grad_w_in, grad_w_down, small = middle(
        jnp.pad(tokens, pad), jnp.pad(cotangent, pad), jnp.pad(attended, pad), w_out, w_in, w_down, vec)
    output, grad_residual_one = output[:length], grad_residual_one[:length]
    grad_ln2_gain, grad_ln2_bias, grad_b_down, grad_b_in, grad_ln1_gain, grad_ln1_bias, grad_b_out = (small[i] for i in range(7))
    head_count = rel_bias.shape[1]
    shape_heads = (page_count, length, head_count, HEAD_DIM)
    head_width = head_count * HEAD_DIM
    grad_branch = grad_residual_one.astype(jnp.bfloat16)
    grad_w_out = jnp.einsum("tc,td->cd", attended, grad_branch, preferred_element_type=jnp.float32)
    grad_attended = jnp.einsum(
        "td,cd->tc", grad_branch, out_weight, preferred_element_type=jnp.float32
    ).astype(jnp.bfloat16)
    query_heads = query_rows.reshape(shape_heads)
    key_heads = key_rows.reshape(shape_heads)
    value_heads = value_rows.reshape(shape_heads)
    grad_heads = grad_attended.reshape(shape_heads)
    scores = (
        jnp.einsum("pqhe,pkhe->phqk", query_heads, key_heads, preferred_element_type=jnp.float32)
        * SCORE_SCALE
        + rel_bias
    )
    attention = jnp.exp(scores - log_total)
    grad_attention = jnp.einsum(
        "pqhe,pkhe->phqk", grad_heads, value_heads, preferred_element_type=jnp.float32
    )
    inner_sum = jnp.sum(attention * grad_attention, axis=-1, keepdims=True)
    grad_scores = (attention * (grad_attention - inner_sum)).astype(jnp.bfloat16)
    grad_rel_order, grad_rel_x, grad_rel_y = table_grads(
        grad_scores, (BINS1, BINS2, BINS2), read_place, corners[0], corners[1]
    )
    grad_query = (
        (
            jnp.einsum(
                "phqk,pkhe->pqhe", grad_scores, key_heads, preferred_element_type=jnp.float32
            )
            * SCORE_SCALE
        )
        .astype(jnp.bfloat16)
        .reshape(-1, head_width)
    )
    grad_key = (
        (
            jnp.einsum(
                "phqk,pqhe->pkhe", grad_scores, query_heads, preferred_element_type=jnp.float32
            )
            * SCORE_SCALE
        )
        .astype(jnp.bfloat16)
        .reshape(-1, head_width)
    )
    grad_value = (
        jnp.einsum(
            "phqk,pqhe->pkhe",
            attention.astype(jnp.bfloat16),
            grad_heads,
            preferred_element_type=jnp.float32,
        )
        .astype(jnp.bfloat16)
        .reshape(-1, head_width)
    )
    grad_b_query = jnp.sum(grad_query, axis=0, dtype=jnp.float32)
    grad_b_value = jnp.sum(grad_value, axis=0, dtype=jnp.float32)
    grad_w_query = jnp.einsum(
        "td,tc->dc", tokens_low, grad_query, preferred_element_type=jnp.float32
    )
    grad_w_key = jnp.einsum("td,tc->dc", tokens_low, grad_key, preferred_element_type=jnp.float32)
    grad_w_value = jnp.einsum(
        "td,tc->dc", tokens_low, grad_value, preferred_element_type=jnp.float32
    )
    input_part = jnp.einsum(
        "tc,dc->td", grad_query, query_weight, preferred_element_type=jnp.float32
    )
    input_part = input_part + jnp.einsum(
        "tc,dc->td", grad_key, key_weight, preferred_element_type=jnp.float32
    )
    input_part = input_part + jnp.einsum(
        "tc,dc->td", grad_value, value_weight, preferred_element_type=jnp.float32
    )
    grad_input = grad_residual_one + lax.psum(input_part, "narrow")
    (
        grad_w_query,
        grad_b_query,
        grad_w_key,
        grad_w_value,
        grad_b_value,
        grad_w_out,
        grad_b_out,
        grad_ln1_gain,
        grad_ln1_bias,
        grad_rel_order,
        grad_rel_x,
        grad_rel_y,
        grad_w_in,
        grad_b_in,
        grad_w_down,
        grad_b_down,
        grad_ln2_gain,
        grad_ln2_bias,
    ) = lax.psum(
        (
            grad_w_query,
            grad_b_query,
            grad_w_key,
            grad_w_value,
            grad_b_value,
            grad_w_out,
            grad_b_out,
            grad_ln1_gain,
            grad_ln1_bias,
            grad_rel_order,
            grad_rel_x,
            grad_rel_y,
            grad_w_in,
            grad_b_in,
            grad_w_down,
            grad_b_down,
            grad_ln2_gain,
            grad_ln2_bias,
        ),
        "wide",
    )
    return (
        output,
        grad_input,
        grad_w_query,
        grad_b_query,
        grad_w_key,
        grad_w_value,
        grad_b_value,
        grad_w_out,
        grad_b_out,
        grad_ln1_gain,
        grad_ln1_bias,
        grad_w_in,
        grad_b_in,
        grad_w_down,
        grad_b_down,
        grad_ln2_gain,
        grad_ln2_bias,
        grad_rel_order,
        grad_rel_x,
        grad_rel_y,
    )


def solution(mesh):
    in_specs = (
        P("wide", None),
        P("wide"),
        P("wide"),
        P(None, "wide"),
        P(None, "narrow"),
        P("narrow"),
        P(None, "narrow"),
        P(None, "narrow"),
        P("narrow"),
        P("narrow", None),
        P(),
        P(),
        P(),
        P(None, "narrow"),
        P("narrow"),
        P("narrow", None),
        P(),
        P(),
        P(),
        P("narrow", None),
        P("narrow", None),
        P("narrow", None),
        P("wide", None),
    )
    out_specs = (
        P("wide", None),
        P("wide", None),
        P(None, "narrow"),
        P("narrow"),
        P(None, "narrow"),
        P(None, "narrow"),
        P("narrow"),
        P("narrow", None),
        P(),
        P(),
        P(),
        P(None, "narrow"),
        P("narrow"),
        P("narrow", None),
        P(),
        P(),
        P(),
        P("narrow", None),
        P("narrow", None),
        P("narrow", None),
    )
    return jax.shard_map(local, mesh=mesh, in_specs=in_specs, out_specs=out_specs, check_vma=False)
```

```python
import functools
import math

import jax
import jax.numpy as jnp
import numpy as np
from jax import lax
from jax.experimental import pallas as pl
from jax.experimental.pallas import tpu as pltpu
from jax.sharding import PartitionSpec as P

HEAD_DIM = 64
BINS1 = 32
BINS2 = 64
MAX_ORDER = 128
MAX_LAYOUT = 256
PAGE = 561


HIGHEST = lax.Precision.HIGHEST
EPSILON = 1e-05
SCORE_SCALE = 0.125

def bucket_steps(bins, reach):
    halfway = bins // 2
    exact = halfway // 2
    steps = []
    for level in range(1, halfway):
        if level < exact:
            steps.append(level)
        else:
            found = reach + 1
            for count in range(exact, reach + 2):
                value = exact + int(
                    math.log(count / exact) / math.log(reach / exact) * (halfway - exact)
                )
                if min(value, halfway - 1) >= level:
                    found = count
                    break
            steps.append(found)
    return steps


MESH = pl.DeviceIdType.MESH
CH = 96
PC = 48


def erf_of(x):
    x = jnp.clip(x, -3.832506856900711, 3.832506856900711)
    s = x * x
    top = -2.72614225801306e-10
    for term in (2.77068142495902e-08, -2.10102402082508e-06, -5.69250639462346e-05,
                 -7.34990630326855e-04, -2.95459980854025e-03, -1.60960333262415e-02):
        top = top * s + term
    low = -1.45660718464996e-05
    for term in (-2.13374055278905e-04, -1.68282697438203e-03, -7.37332916720468e-03,
                 -1.42647390514189e-02):
        low = low * s + term
    return x * top / low


def normal_cdf(x):
    return 0.5 + 0.5 * erf_of(x * math.sqrt(0.5))


def centre(values):
    c = values - jnp.mean(values, axis=-1, keepdims=True)
    r = lax.rsqrt(jnp.mean(c * c, axis=-1, keepdims=True) + EPSILON)
    return c * r, r


def norm_back(g, n, r, gain):
    m = g * gain
    return r * (m - jnp.mean(m, axis=-1, keepdims=True) - n * jnp.mean(m * n, axis=-1, keepdims=True))


def dot_nn(a, b):
    return lax.dot_general(a, b, (((1,), (0,)), ((), ())), preferred_element_type=jnp.float32)


def dot_nt(a, b):
    return lax.dot_general(a, b, (((1,), (1,)), ((), ())), preferred_element_type=jnp.float32)


def dot_tn(a, b):
    return lax.dot_general(a, b, (((0,), (0,)), ((), ())), preferred_element_type=jnp.float32)


class LineSum:
    def __init__(self, part, rx_in, rx_mid, tot, s_in, s_mid, r_in, r_mid):
        self.part, self.rx_in, self.rx_mid, self.tot = part, rx_in, rx_mid, tot
        self.s_in, self.s_mid, self.r_in, self.r_mid = s_in, s_mid, r_in, r_mid
        w, n = lax.axis_index("wide"), lax.axis_index("narrow")
        self.end = (n == 0) | (n == 3)
        self.mid = jnp.logical_not(self.end)
        self.side = (w, n + 1 - 2 * lax.rem(n, 2))
        self.across = (w, 3 - n)
        self.pieces = part.shape[0] // PC

    def rows(self, p):
        return pl.ds(p * PC, PC) if isinstance(p, int) else pl.ds(pl.multiple_of(p * PC, PC), PC)

    def copy_a(self, p):
        return pltpu.make_async_remote_copy(self.part.at[self.rows(p)], self.rx_in.at[self.rows(p)],
            self.s_in.at[p], self.r_in.at[p], device_id=self.side, device_id_type=MESH)

    def copy_b(self, p):
        return pltpu.make_async_remote_copy(self.part.at[self.rows(p)], self.rx_mid.at[self.rows(p)],
            self.s_mid.at[p], self.r_mid.at[p], device_id=self.across, device_id_type=MESH)

    def copy_t(self, p):
        return pltpu.make_async_remote_copy(self.tot.at[self.rows(p)], self.tot.at[self.rows(p)],
            self.s_in.at[p], self.r_in.at[p], device_id=self.side, device_id_type=MESH)

    def barrier(self, others=0):
        bar = pltpu.get_barrier_semaphore()
        pl.semaphore_signal(bar, inc=1, device_id=self.side, device_id_type=MESH)

        @pl.when(self.mid)
        def _():
            pl.semaphore_signal(bar, inc=1, device_id=self.across, device_id_type=MESH)

        @pl.when(self.end)
        def _():
            pl.semaphore_wait(bar, 1 + others)

        @pl.when(self.mid)
        def _():
            pl.semaphore_wait(bar, 2 + others)

    def free_part(self, p):
        @pl.when(self.end)
        def _():
            self.copy_a(p).wait_send()

        @pl.when(self.mid)
        def _():
            self.copy_b(p).wait_send()

    def finish(self, p, first):
        self.copy_b(p).wait_recv()
        if not first:
            self.copy_t(p).wait_send()
        self.tot[self.rows(p), :] = self.part[self.rows(p), :] + self.rx_mid[self.rows(p), :]
        self.copy_t(p).start()

    def slot(self, p, order):
        @pl.when(self.end)
        def _():
            self.copy_a(p).start()

        @pl.when(self.mid)
        def _():
            self.copy_a(p).wait_recv()
            self.part[self.rows(p), :] += self.rx_in[self.rows(p), :]
            self.copy_b(p).start()

            @pl.when(p > 0)
            def _():
                self.finish(p - 1, order == 0)

            if order > 0:
                @pl.when(p == 0)
                def _():
                    self.finish(self.pieces - 1, order == 1)

    def send_end(self, p):
        @pl.when(self.end)
        def _():
            self.copy_a(p).start()

    def slot_mid(self, p):
        @pl.when(self.mid)
        def _():
            self.copy_a(p).wait_recv()
            self.part[self.rows(p), :] += self.rx_in[self.rows(p), :]
            self.copy_b(p).start()
            if p > 0:
                self.finish(p - 1, True)

    def last(self, first):
        @pl.when(self.mid)
        def _():
            self.finish(self.pieces - 1, first)

    def want(self, p):
        @pl.when(self.end)
        def _():
            self.copy_t(p).wait_recv()

    def drain(self):
        def one(p, c):
            self.free_part(p)

            @pl.when(self.mid)
            def _():
                self.copy_t(p).wait_send()
            return c
        lax.fori_loop(0, self.pieces, one, 0)


def middle_kernel(tok_ref, cot_ref, att_ref, w_out_ref, w_in_ref, w_down_ref, bo_r, g1_r, b1_r, bi_r, bd_r, g2_r, b2_r, perm,
                  out_ref, gres_ref, dwin_ref, dwdown_ref, small_ref,
                  part, rx_in, rx_mid, tot, res, hid, pre, act, gff, hlow, gpre, wo, wi, wd, outp, vec_s,
                  s_in, s_mid, r_in, r_mid):
    line = LineSum(part, rx_in, rx_mid, tot, s_in, s_mid, r_in, r_mid)
    steps = part.shape[0] // CH
    k = CH // PC
    for i, vector in enumerate((bo_r, g1_r, b1_r, bi_r, bd_r, g2_r, b2_r)):
        vec_s[i, :] = vector[...]
    b_out, g1, b1, b_in, b_down, g2, b2 = (vec_s[i:i + 1, :] for i in range(7))
    wo[...] = jnp.zeros_like(wo)
    wo[0:w_out_ref.shape[0], :] = w_out_ref[...].astype(jnp.bfloat16)
    line.barrier()

    def rows(c):
        return pl.ds(pl.multiple_of(c * CH, CH), CH)

    def branch_step(c, carry):
        r = rows(c)
        part[r, :] = dot_nn(att_ref[r, :], wo[...])
        for j in range(k):
            line.slot(c * k + j, 0)
        return carry
    lax.fori_loop(0, steps, branch_step, 0)
    wi[...] = w_in_ref[...].astype(jnp.bfloat16)
    wd[...] = w_down_ref[...].astype(jnp.bfloat16)
    small_ref[...] = jnp.zeros_like(small_ref)
    outp[...] = jnp.zeros_like(outp)

    def open_step(c):
        for j in range(k):
            line.want(c * k + j)
        for j in range(k):
            line.free_part(c * k + j)

    def forward_step(c, carry):
        r = rows(c)
        open_step(c)
        one = tok_ref[r, :] + (tot[r, :] + b_out)
        res[r, :] = one
        n, _ = centre(one)
        hidden = n * g1 + b1
        hid[r, :] = hidden
        low = hidden.astype(jnp.bfloat16)
        hlow[r, :] = low
        u = dot_nn(low, wi[...]) + b_in
        pre[r, :] = u
        a = (u * normal_cdf(u)).astype(jnp.bfloat16)
        act[r, :] = a
        part[r, :] = dot_nn(a, wd[...])
        for j in range(k):
            line.slot(c * k + j, 1)
        return carry
    lax.fori_loop(0, steps, forward_step, 0)

    def add_row(i, rows_value):
        small_ref[i:i + 1, :] += jnp.sum(rows_value, axis=0, keepdims=True)

    def back_step(c, carry):
        r = rows(c)
        open_step(c)
        two = hid[r, :] + (tot[r, :] + b_down)
        n, rs = centre(two)
        g = cot_ref[r, :]
        add_row(0, g * n)
        add_row(1, g)
        back = norm_back(g, n, rs, g2)
        hid[r, :] = back
        low = back.astype(jnp.bfloat16)
        gff[r, :] = low
        add_row(2, low.astype(jnp.float32))
        ga = dot_nt(low, wd[...])
        u = pre[r, :]
        slope = normal_cdf(u) + u * (jnp.exp(-0.5 * u * u) * (1.0 / math.sqrt(2.0 * math.pi)))
        gp = (ga * slope).astype(jnp.bfloat16)
        gpre[r, :] = gp
        add_row(3, gp.astype(jnp.float32))
        part[r, :] = dot_nt(gp, wi[...])
        for j in range(k):
            line.slot(c * k + j, 2)
        total = outp[...]
        for piece in split3(n * g2 + b2):
            total = total + dot_tn(perm[r, :], piece)
        outp[...] = total
        return carry
    lax.fori_loop(0, steps, back_step, 0)
    line.last(False)
    dwdown_ref[...] = dot_tn(act[...], gff[...])
    dwin_ref[...] = dot_tn(hlow[...], gpre[...])

    def close_step(c, carry):
        r = rows(c)
        for j in range(k):
            line.want(c * k + j)
        g = hid[r, :] + tot[r, :]
        n, rs = centre(res[r, :])
        add_row(4, g * n)
        add_row(5, g)
        back = norm_back(g, n, rs, g1)
        gres_ref[r, :] = back
        add_row(6, back.astype(jnp.bfloat16).astype(jnp.float32))
        return carry
    lax.fori_loop(0, steps, close_step, 0)
    out_ref[...] = outp[0:out_ref.shape[0], :]
    line.drain()


def middle(tok, cot, att, w_out, w_in, w_down, b_out, g1, b1, b_in, b_down, g2, b2, perm):
    rows, d = tok.shape
    f = w_in.shape[1]
    pieces = rows // PC
    f32, bf = jnp.float32, jnp.bfloat16
    shapes = (jax.ShapeDtypeStruct((PAGE, d), f32), jax.ShapeDtypeStruct((rows, d), f32),
              jax.ShapeDtypeStruct((d, f), f32), jax.ShapeDtypeStruct((f, d), f32),
              jax.ShapeDtypeStruct((8, d), f32))
    vm = pl.BlockSpec(memory_space=pltpu.VMEM)
    big = [pltpu.VMEM((rows, d), f32) for _ in range(6)]
    return pl.pallas_call(
        middle_kernel, out_shape=shapes, in_specs=[vm] * 14, out_specs=[vm] * 5,
        scratch_shapes=big + [pltpu.VMEM((rows, f), f32), pltpu.VMEM((rows, f), bf), pltpu.VMEM((rows, d), bf),
                              pltpu.VMEM((rows, d), bf), pltpu.VMEM((rows, f), bf),
                              pltpu.VMEM((256, d), bf), pltpu.VMEM((d, f), bf), pltpu.VMEM((f, d), bf),
                              pltpu.VMEM((WIDE_ROWS, d), f32), pltpu.VMEM((8, d), f32)]
        + [pltpu.SemaphoreType.DMA((pieces,))] * 4,
        compiler_params=pltpu.CompilerParams(collective_id=0, has_side_effects=True, vmem_limit_bytes=56 << 20),
        cost_estimate=pl.CostEstimate(flops=6 * 2 * rows * d * f, bytes_accessed=20 << 20, transcendentals=rows * f),
    )(tok, cot, att, w_out, w_in, w_down, b_out, g1, b1, b_in, b_down, g2, b2, perm)


WIDE_ROWS = 640
ROWS = 576


def bucket_number(offset, bins, reach):
    halfway = bins // 2
    steps = bucket_steps(bins, reach)
    return (halfway if offset > 0 else 0) + sum(1 for s in steps if abs(offset) >= s)


def choose_matrix(offsets, bins, reach):
    out = np.zeros((bins, len(offsets)), np.float32)
    for place, offset in enumerate(offsets):
        out[bucket_number(offset, bins, reach), place] = 1.0
    return out


def split3(x):
    hi = x.astype(jnp.bfloat16)
    rest = x - hi.astype(jnp.float32)
    mid = rest.astype(jnp.bfloat16)
    return hi, mid, (rest - mid.astype(jnp.float32)).astype(jnp.bfloat16)


def split2(x):
    hi = x.astype(jnp.bfloat16)
    return hi, (x - hi.astype(jnp.float32)).astype(jnp.bfloat16)


def exact_dot(a, b, dims):
    return lax.dot_general(a, b, (dims, ((), ())), precision=HIGHEST, preferred_element_type=jnp.float32)


def lanes_of(h, shape):
    lane = lax.broadcasted_iota(jnp.int32, shape, 1)
    return (lane >= h * HEAD_DIM) & (lane < (h + 1) * HEAD_DIM)


def row_blocks(body):
    full = ROWS // 128

    def step(m, carry):
        body(m, 128)
        return carry
    lax.fori_loop(0, full, step, 0)
    if ROWS % 128:
        body(full, ROWS % 128)


def block_rows(m, n):
    return pl.ds(pl.multiple_of(m * 128, 128), n)


def block_window(m):
    return pl.ds(pl.multiple_of(512 - m * 128, 128), WIDE_ROWS)


def head_kernel(tok, cot, reg, rank, box, wq, wk, wv, bq, bv, to, tx, ty, so, sxy,
                tokp, cotp, low, perm, q_ref, k_ref, v_ref, prob, att, ob, obf, ws,
                rows_s, vec_s, split_s, base, amat, ob4, att_f):
    f32, bf = jnp.float32, jnp.bfloat16
    n = PAGE
    rows_s[...] = jnp.full(rows_s.shape, 1e4, f32)
    rows_s[0, 0:n] = reg[...].astype(f32)
    rows_s[1, 0:n] = rank[...].astype(f32)
    rows_s[2:4, 0:n] = box[...].astype(f32)
    region_row, rank_row = rows_s[0:1, :], rows_s[1:2, :]
    i0 = lax.broadcasted_iota(jnp.int32, (WIDE_ROWS, WIDE_ROWS), 0)
    i1 = lax.broadcasted_iota(jnp.int32, (WIDE_ROWS, WIDE_ROWS), 1)
    region_col = jnp.sum(jnp.where(i0 == i1, region_row, 0.0), axis=1, keepdims=True)
    place = jnp.sum(jnp.where(region_col < region_row, 1.0, 0.0), axis=0, keepdims=True) + rank_row
    perm[...] = jnp.where(i0.astype(f32) == place, 1.0, 0.0).astype(bf)
    split_s[...] = jnp.zeros_like(split_s)

    def sort_rows(source, target, first):
        parts = split3(source[...])
        for i in range(3):
            split_s[i, 0:n, :] = parts[i]
        y = dot_nn(perm[...], split_s[0])
        if first is not None:
            first[...] = y.astype(bf)
        target[...] = y[0:ROWS, :]
        for i in range(1, 3):
            target[...] += dot_nn(perm[0:ROWS, :], split_s[i])
    sort_rows(tok, tokp, low)
    code = lax.broadcasted_iota(jnp.int32, (128, WIDE_ROWS), 0).astype(f32)
    for i in range(2):
        row = rows_s[2 + i:3 + i, :]
        one = dot_nt(perm[...], jnp.where(code == row, 1.0, 0.0).astype(bf)).astype(bf)
        ob[:, 128 * i:128 * (i + 1)] = one
        ob4[:, 256 * i:256 * i + 128] = one
        ob4[:, 256 * i + 128:256 * i + 256] = one
        obf[:, 128 * i:128 * (i + 1)] = dot_nt(perm[...], jnp.where(127.0 - code == row, 1.0, 0.0).astype(bf)).astype(bf)
    width = wq.shape[0]
    ws[...] = jnp.zeros_like(ws)
    for i, weight in enumerate((wq, wk, wv)):
        ws[i, 0:width, :] = weight[...].astype(bf)
    vec_s[...] = jnp.zeros_like(vec_s)
    vec_s[0, 0:width] = bq[...]
    vec_s[1, 0:width] = bv[...]
    q_ref[...] = ((dot_nt(low[...], ws[0]) + vec_s[0:1, :]).astype(bf) * SCORE_SCALE).astype(bf)
    k_ref[...] = dot_nt(low[...], ws[1]).astype(bf)
    v_ref[...] = (dot_nt(low[...], ws[2]) + vec_s[1:2, :]).astype(bf)
    row_o = exact_dot(to[...], so[...], ((1,), (0,)))
    row_xy = (exact_dot(tx[...], sxy[...], ((1,), (0,))), exact_dot(ty[...], sxy[...], ((1,), (0,))))
    heads = to.shape[0]
    for h in range(heads):
        base[...] = pltpu.roll(jnp.broadcast_to(row_o[h:h + 1, :], base.shape), 0, 1, stride=1, stride_axis=0)
        for i in range(2):
            table = pltpu.roll(jnp.broadcast_to(row_xy[i][h:h + 1, :], (128, 256)), 0, 1, stride=1, stride_axis=0)
            pair = jnp.concatenate(split2(table[:, 0:128]), axis=1)
            amat[:, 256 * i:256 * (i + 1)] = dot_nn(ob[:, 128 * i:128 * (i + 1)], pair).astype(bf)

        def block(m, rows, h=h):
            r = block_rows(m, rows)
            qh = jnp.where(lanes_of(h, (rows, 256)), q_ref[r, :], jnp.zeros((), bf))
            s = dot_nt(qh, k_ref[...]) + dot_nt(amat[r, :], ob4[...]) + base[0:rows, block_window(m)]
            s = jnp.where(lax.broadcasted_iota(jnp.int32, s.shape, 1) < n, s, -1e30)
            e = jnp.exp(s - jnp.max(s, axis=1, keepdims=True))
            p = e / jnp.sum(e, axis=1, keepdims=True)
            prob[h, r, :] = p
            pv = dot_nn(p.astype(bf), v_ref[...])
            if h > 0:
                pv = jnp.where(lanes_of(h, (rows, 256)), pv, att_f[r, :])
            att_f[r, :] = pv
        row_blocks(block)
    att[...] = jnp.zeros_like(att)
    att[0:ROWS, :] = att_f[...].astype(bf)
    sort_rows(cot, cotp, None)


def head(tok, cot, reg, rank, box, wq, wk, wv, bq, bv, to, tx, ty, so, sxy):
    f32, bf = jnp.float32, jnp.bfloat16
    d = tok.shape[1]
    heads = to.shape[0]
    sd = jax.ShapeDtypeStruct
    W, R = WIDE_ROWS, ROWS
    shapes = (sd((R, d), f32), sd((R, d), f32), sd((W, d), bf), sd((W, W), bf), sd((W, 256), bf), sd((W, 256), bf),
              sd((W, 256), bf), sd((heads, R, W), f32), sd((W, 256), bf), sd((W, 256), bf), sd((W, 256), bf), sd((3, 256, d), bf))
    vm = pl.BlockSpec(memory_space=pltpu.VMEM)
    return pl.pallas_call(
        head_kernel, out_shape=shapes, in_specs=[vm] * 15, out_specs=[vm] * 12,
        scratch_shapes=[pltpu.VMEM((8, W), f32), pltpu.VMEM((8, 256), f32),
                        pltpu.VMEM((3, W, d), bf), pltpu.VMEM((128, 1280), f32), pltpu.VMEM((W, 512), bf),
                        pltpu.VMEM((W, 512), bf), pltpu.VMEM((R, 256), f32)],
        compiler_params=pltpu.CompilerParams(vmem_limit_bytes=56 << 20),
        cost_estimate=pl.CostEstimate(flops=10 ** 10, bytes_accessed=20 << 20, transcendentals=heads * R * W),
    )(tok, cot, reg, rank, box, wq, wk, wv, bq, bv, to, tx, ty, so, sxy)


class CubeSum:
    def __init__(self, ref, rx1, rx2, rx3, rx4, rxb, ssem, rsem, free, bits):
        self.ref, self.rx1, self.rx2, self.rx3, self.rx4, self.rxb = ref, rx1, rx2, rx3, rx4, rxb
        self.ssem, self.rsem, self.free = ssem, rsem, free
        w, n = lax.axis_index("wide"), lax.axis_index("narrow")
        self.bit = [lax.rem(lax.div(w, 2 ** i), 2) for i in range(bits)]
        self.to = [(w + 2 ** i * (1 - 2 * self.bit[i]), n) for i in range(bits)]
        self.rows = ref.shape[0]
        half = self.rows // 2
        self.half, self.stream, self.eighth, self.piece = half, half // 2, half // 4, half // 8
        self.own = self.bit[0] * half
        self.axes = ((1, 2), (2, 1))
        self.extra = range(3, bits)

    def at(self, start, size):
        return pl.ds(pl.multiple_of(start, self.piece), size)

    def base1(self, s, other):
        b = self.bit[self.axes[s][0]]
        b = 1 - b if other else b
        return self.own + s * self.stream + b * self.eighth

    def base2(self, s, other):
        b = self.bit[self.axes[s][1]]
        b = 1 - b if other else b
        return self.base1(s, False) + b * self.piece

    def copy(self, src, dst, i, axis):
        return pltpu.make_async_remote_copy(src, dst, self.ssem.at[i], self.rsem.at[i], device_id=self.to[axis],
                                            device_id_type=MESH)

    def core_out(self):
        return self.copy(self.ref.at[self.at((1 - self.bit[0]) * self.half, self.half)], self.rx1, 0, 0)

    def first(self, s):
        return self.copy(self.ref.at[self.at(self.base1(s, True), self.eighth)], self.rx2.at[s], 1 + s, self.axes[s][0])

    def second(self, s):
        return self.copy(self.ref.at[self.at(self.base2(s, True), self.piece)], self.rx3.at[s], 3 + s, self.axes[s][1])

    def back2(self, s):
        r = self.at(self.base2(s, False), self.piece)
        return self.copy(self.ref.at[r], self.rxb.at[s], 5 + s, self.axes[s][1])

    def back1(self, s):
        r = self.at(self.base1(s, False), self.eighth)
        return self.copy(self.ref.at[r], self.ref.at[r], 7 + s, self.axes[s][0])

    def core_back(self):
        r = self.at(self.own, self.half)
        return self.copy(self.ref.at[r], self.ref.at[r], 9, 0)

    def more(self, e, s):
        i = e - 3
        return self.copy(self.ref.at[self.at(self.base2(s, False), self.piece)], self.rx4.at[i, s], 10 + 2 * i + s, e)

    def release(self, i, axis):
        pl.semaphore_signal(self.free.at[i], inc=1, device_id=self.to[axis], device_id_type=MESH)

    def step(self, i):
        if i == 0:
            self.core_out().start()
        if i == 1:
            self.core_out().wait_recv()
            self.ref[self.at(self.own, self.half), :] += self.rx1[...]
            for s in range(2):
                self.first(s).start()
            self.core_out().wait_send()
            self.release(0, 0)
        if i == 2:
            for s in range(2):
                self.first(s).wait()
                self.release(1 + s, self.axes[s][0])
                self.ref[self.at(self.base1(s, False), self.eighth), :] += self.rx2[s]
                self.second(s).start()
        if i == 3:
            for s in range(2):
                self.second(s).wait()
                self.ref[self.at(self.base2(s, False), self.piece), :] += self.rx3[s]
            for e in self.extra:
                for s in range(2):
                    self.more(e, s).start()
                for s in range(2):
                    self.more(e, s).wait()
                    self.ref[self.at(self.base2(s, False), self.piece), :] += self.rx4[e - 3, s]
            for s in range(2):
                self.back2(s).start()
        if i == 4:
            for s in range(2):
                self.back2(s).wait_recv()
                self.ref[self.at(self.base2(s, True), self.piece), :] = self.rxb[s]
                pl.semaphore_wait(self.free.at[1 + s], 1)
                self.back1(s).start()
        if i == 5:
            for s in range(2):
                self.back1(s).wait_recv()
            pl.semaphore_wait(self.free.at[0], 1)
            self.core_back().start()
        if i == 6:
            self.core_back().wait()
            for s in range(2):
                self.back2(s).wait_send()
                self.back1(s).wait_send()


def tail_kernel(bits, gres, small_in, dwi_in, dwd_in, wout, att, q_ref, k_ref, v_ref, prob, ob, obf, low, ws, perm, sgo, sgxy,
                gin, gat, gwi, gwd, sm,
                part, rx_in, rx_mid, tot, rx1, rx2, rx3, rx4, rxb, rxs, ds_s, pl_s, ga, gt, qt, dkt, dvt, dqf, dq, dk, dv, acc, wos, ginp,
                s_in, s_mid, r_in, r_mid, cs, cr, cf, ss, sr):
    f32, bf = jnp.float32, jnp.bfloat16
    n = PAGE
    heads = prob.shape[0]
    width = wout.shape[0]
    line = LineSum(part, rx_in, rx_mid, tot, s_in, s_mid, r_in, r_mid)
    cube = [CubeSum(ref, rx1.at[i], rx2.at[i], rx3.at[i], rx4.at[i], rxb.at[i], cs.at[i], cr.at[i], cf.at[i], bits)
            for i, ref in enumerate((gwi, gwd, gat))]
    gwi[...] = dwi_in[...]
    gwd[...] = dwd_in[...]
    bar = pltpu.get_barrier_semaphore()
    for to in cube[0].to:
        pl.semaphore_signal(bar, inc=1, device_id=to, device_id_type=MESH)
    line.barrier(bits)
    cube[0].step(0)
    cube[1].step(0)

    sm[...] = jnp.zeros_like(sm)
    sm[0:8, :] = small_in[...]
    gb = gres[...].astype(bf)
    wos[...] = jnp.zeros_like(wos)
    wos[0:width, :] = wout[...].astype(bf)
    ga[...] = jnp.zeros_like(ga)
    ga[0:ROWS, :] = dot_nt(gb, wos[...]).astype(bf)
    gt[...] = jnp.transpose(ga[...])
    qt[...] = jnp.transpose(q_ref[...])
    ds_s[...] = jnp.zeros_like(ds_s)
    pl_s[...] = jnp.zeros_like(pl_s)
    dkt[...] = jnp.zeros_like(dkt)
    dvt[...] = jnp.zeros_like(dvt)
    dqf[...] = jnp.zeros_like(dqf)
    gat[3 * width:4 * width, :] = dot_tn(att[0:ROWS, :], gb)[0:width, :]
    flip = (lax.broadcasted_iota(jnp.int32, (128, 128), 0) + lax.broadcasted_iota(jnp.int32, (128, 128), 1)) == 127
    flip = jnp.where(flip, 1.0, 0.0).astype(bf)
    for h in range(heads):
        acc[...] = jnp.zeros_like(acc)

        def block(m, rows, h=h):
            r = block_rows(m, rows)
            gh = jnp.where(lanes_of(h, (rows, 256)), ga[r, :], jnp.zeros((), bf))
            dp = dot_nt(gh, v_ref[...])
            p = prob[h, r, :]
            inner = jnp.sum(p * dp, axis=1, keepdims=True)
            ds = (p * (dp - inner)).astype(bf)
            ds_s[r, :] = ds
            pl_s[r, :] = p.astype(bf)
            dqh = dot_nn(ds, k_ref[...])
            dqf[r, :] = jnp.where(lanes_of(h, (rows, 256)), dqh, dqf[r, :])
            acc[0:rows, block_window(m)] += ds.astype(f32)
        row_blocks(block)
        hr = pl.ds(h * HEAD_DIM, HEAD_DIM)
        dkt[hr, :] = dot_nn(qt[hr, :], ds_s[...])
        dvt[hr, :] = dot_nn(gt[hr, :], pl_s[...])
        u = jnp.concatenate(split2(dot_nn(ds_s[...], ob[...])), axis=1)
        g = dot_tn(obf[...], u)
        for i in range(2):
            b = 128 * i
            both = g[b:b + 128, b:b + 128] + g[b:b + 128, 256 + b:384 + b]
            both = jnp.concatenate([both, jnp.zeros_like(both)], axis=1)
            line_sum = jnp.sum(pltpu.roll(both, 0, 1, stride=1, stride_axis=0), axis=0, keepdims=True)
            sm[13 + heads * i + h:14 + heads * i + h, 0:BINS2] = exact_dot(line_sum, sgxy[...], ((1,), (1,)))
        hi, lo = split2(acc[...])
        turned = dot_nn(flip, hi) + dot_nn(flip, lo)
        line_sum = jnp.sum(pltpu.roll(turned, 0, 1, stride=1, stride_axis=0), axis=0, keepdims=True)
        sm[10 + h:11 + h, 0:BINS1] = exact_dot(line_sum, sgo[...], ((1,), (1,)))
        if h == 1:
            cube[0].step(1)
            cube[1].step(1)
    dq[...] = jnp.zeros_like(dq)
    dq[0:ROWS, :] = (dqf[...] * SCORE_SCALE).astype(bf)
    dk[...] = jnp.transpose(dkt[...]).astype(bf)
    dv[...] = jnp.transpose(dvt[...]).astype(bf)
    sm[8:9, 0:256] = jnp.sum(dq[...].astype(f32), axis=0, keepdims=True)
    sm[9:10, 0:256] = jnp.sum(dv[...].astype(f32), axis=0, keepdims=True)
    k = CH // PC
    for c in range(ROWS // CH):
        r = slice(c * CH, (c + 1) * CH)
        part[r, :] = dot_nn(dq[r, :], ws[0]) + dot_nn(dk[r, :], ws[1]) + dot_nn(dv[r, :], ws[2])
        for j in range(k):
            line.send_end(c * k + j)

    bit_to = cube[0].to

    def small_copy(i):
        return pltpu.make_async_remote_copy(sm, rxs.at[i], ss.at[i], sr.at[i], device_id=bit_to[i], device_id_type=MESH)

    def small_step(i):
        if i > 0:
            small_copy(i - 1).wait()
            sm[...] += rxs[i - 1]
        if i < bits:
            small_copy(i).start()

    def weight_grad(i):
        gat[i * width:(i + 1) * width, :] = dot_tn((dq, dk, dv)[i][...], low[...])[0:width, :]

    ginp[...] = jnp.zeros_like(ginp)

    def consume(c):
        for j in range(k):
            line.want(c * k + j)
        r = slice(c * CH, (c + 1) * CH)
        y = gres[r, :] + tot[r, :]
        total = ginp[...]
        for piece in split3(y):
            total = total + dot_tn(perm[r, :], piece)
        ginp[...] = total

    jobs = {0: [(weight_grad, 0)], 1: [(weight_grad, 1)], 2: [(weight_grad, 2), (cube[2].step, 0), (small_step, 0)],
            3: [(cube[0].step, 2), (cube[1].step, 2)], 4: [(cube[2].step, 1), (small_step, 1)],
            5: [(cube[0].step, 3), (cube[1].step, 3)], 6: [(small_step, 2), (consume, 0)],
            7: [(cube[2].step, 2), (cube[0].step, 4), (cube[1].step, 4)], 8: [(small_step, 3), (consume, 1)],
            9: [(cube[2].step, 3)], 10: [(consume, 2)], 11: [(cube[2].step, 4), (cube[0].step, 5), (cube[1].step, 5)]}
    for p in range(line.pieces):
        line.slot_mid(p)
        for job, arg in jobs.get(p, ()):
            job(arg)
    line.last(True)
    for i in range(4, bits + 1):
        small_step(i)
    consume(3)
    consume(4)
    cube[2].step(5)
    consume(5)
    for c in cube:
        c.step(6)
    gin[...] = ginp[0:n, :]
    line.drain()


def tail(bits, gres, small_in, dwi, dwd, wout, att, q, k, v, prob, ob, obf, low, ws, perm, sgo, sgxy):
    f32, bf = jnp.float32, jnp.bfloat16
    d = gres.shape[1]
    f = dwi.shape[1]
    width = wout.shape[0]
    sd = jax.ShapeDtypeStruct
    W, R = WIDE_ROWS, ROWS
    pieces = R // PC
    more = max(bits - 3, 1)
    shapes = (sd((PAGE, d), f32), sd((4 * width, d), f32),
              sd((d, f), f32), sd((f, d), f32), sd((24, d), f32))
    vm = pl.BlockSpec(memory_space=pltpu.VMEM)
    v_ = pltpu.VMEM
    return pl.pallas_call(
        functools.partial(tail_kernel, bits), out_shape=shapes, in_specs=[vm] * 17, out_specs=[vm] * 5,
        scratch_shapes=[v_((R, d), f32)] * 4 + [v_((3, d // 2, d), f32), v_((3, 2, d // 8, d), f32),
                        v_((3, 2, d // 16, d), f32), v_((3, more, 2, d // 16, d), f32), v_((3, 2, d // 16, d), f32), v_((bits, 24, d), f32),
                        v_((W, W), bf), v_((W, W), bf), v_((W, 256), bf), v_((256, W), bf), v_((256, W), bf),
                        v_((256, W), f32), v_((256, W), f32), v_((R, 256), f32), v_((W, 256), bf), v_((W, 256), bf), v_((W, 256), bf),
                        v_((128, 1280), f32), v_((256, d), bf), v_((W, d), f32)]
        + [pltpu.SemaphoreType.DMA((pieces,))] * 4
        + [pltpu.SemaphoreType.DMA((3, 10 + 2 * more))] * 2 + [pltpu.SemaphoreType.REGULAR((3, 3))] + [pltpu.SemaphoreType.DMA((bits,))] * 2,
        compiler_params=pltpu.CompilerParams(collective_id=1, has_side_effects=True, vmem_limit_bytes=60 << 20),
        cost_estimate=pl.CostEstimate(flops=10 ** 10, bytes_accessed=20 << 20, transcendentals=0),
    )(gres, small_in, dwi, dwd, wout, att, q, k, v, prob, ob, obf, low, ws, perm, sgo, sgxy)


def finish_kernel(out_in, gin_in, gat_in, gwi_in, gwd_in, sm, out, gin, gwq, gwk, gwv, gwo, gwi, gwd, *rest):
    vectors, (b_out, b_gin, b_gat, b_gwi, b_gwd, sem_in, sem_out) = rest[:12], rest[12:]
    width = gwo.shape[0]
    heads = vectors[9].shape[0]
    whole = [(out_in, b_out, out), (gin_in, b_gin, gin), (gwi_in, b_gwi, gwi), (gwd_in, b_gwd, gwd)]
    for i, g in enumerate((gwq, gwk, gwv, gwo)):
        r = pl.ds(i * width, width)
        whole.append((gat_in.at[r], b_gat.at[r], g))
    inward = [pltpu.make_async_copy(a, b, sem_in.at[i]) for i, (a, b, _) in enumerate(whole)]
    outward = [pltpu.make_async_copy(b, c, sem_out.at[i]) for i, (_, b, c) in enumerate(whole)]
    for c in inward:
        c.start()
    for i in range(7):
        vectors[i][...] = sm[i, :]
    vectors[7][...] = sm[8, 0:width]
    vectors[8][...] = sm[9, 0:width]
    vectors[9][...] = sm[10:10 + heads, 0:BINS1]
    vectors[10][...] = sm[10 + heads:10 + 2 * heads, 0:BINS2]
    vectors[11][...] = sm[10 + 2 * heads:10 + 3 * heads, 0:BINS2]
    for c, o in zip(inward, outward):
        c.wait()
        o.start()
    for o in outward:
        o.wait()


def finish(heads, width, out, gin, gat, gwi, gwd, sm):
    f32 = jnp.float32
    sd = jax.ShapeDtypeStruct
    d = gat.shape[1]
    like = lambda x: sd(x.shape, f32)
    shapes = (like(out), like(gin)) + (sd((width, d), f32),) * 4 + (like(gwi), like(gwd)) + (sd((d,), f32),) * 7 \
        + (sd((width,), f32),) * 2 + (sd((heads, BINS1), f32), sd((heads, BINS2), f32), sd((heads, BINS2), f32))
    vm, hbm = pl.BlockSpec(memory_space=pltpu.VMEM), pl.BlockSpec(memory_space=pl.ANY)
    return pl.pallas_call(
        finish_kernel, out_shape=shapes, in_specs=[hbm] * 5 + [vm], out_specs=[hbm] * 8 + [vm] * 12,
        scratch_shapes=[pltpu.VMEM(x.shape, f32) for x in (out, gin, gat, gwi, gwd)] + [pltpu.SemaphoreType.DMA((8,))] * 2,
        compiler_params=pltpu.CompilerParams(vmem_limit_bytes=56 << 20),
    )(out, gin, gat, gwi, gwd, sm)


def local(
    bits,
    tokens,
    region,
    order_rank,
    box_coords,
    w_query,
    b_query,
    w_key,
    w_value,
    b_value,
    w_out,
    b_out,
    ln1_gain,
    ln1_bias,
    w_in,
    b_in,
    w_down,
    b_down,
    ln2_gain,
    ln2_bias,
    rel_order,
    rel_x,
    rel_y,
    cotangent,
):
    so = choose_matrix([i - 512 if i < 1152 else i - 1792 for i in range(1280)], BINS1, MAX_ORDER)
    sxy = choose_matrix([i if i < 128 else i - 256 for i in range(256)], BINS2, MAX_LAYOUT)
    sgo = choose_matrix([i - 639 for i in range(1280)], BINS1, MAX_ORDER)
    sgxy = choose_matrix([i - 127 for i in range(256)], BINS2, MAX_LAYOUT)
    width = w_out.shape[0]
    heads = rel_order.shape[0]
    tokp, cotp, low, perm, q, k, v, prob, att, ob, obf, ws = head(
        tokens, cotangent, region, order_rank, box_coords, w_query.T, w_key.T, w_value.T, b_query, b_value, rel_order, rel_x, rel_y, so, sxy)
    output, gres, dwi, dwd, small = middle(
        tokp, cotp, att, w_out, w_in, w_down, b_out, ln1_gain, ln1_bias, b_in, b_down, ln2_gain, ln2_bias, perm)
    gin, gat, gwi, gwd, sm = tail(
        bits, gres, small, dwi, dwd, w_out, att, q, k, v, prob, ob, obf, low, ws, perm, sgo, sgxy)
    (output, gin, gwq, gwk, gwv, gwo, gwi, gwd, l2g, l2b, bd, bi, l1g, l1b, bo, gbq, gbv, ro, rx, ry) = finish(
        heads, width, output, gin, gat, gwi, gwd, sm)
    return (output, gin, gwq.T, gbq, gwk.T, gwv.T, gbv, gwo, bo, l1g, l1b, gwi, bi,
            gwd, bd, l2g, l2b, ro, rx, ry)


def solution(mesh):
    in_specs = (
        P("wide", None),
        P("wide"),
        P("wide"),
        P(None, "wide"),
        P(None, "narrow"),
        P("narrow"),
        P(None, "narrow"),
        P(None, "narrow"),
        P("narrow"),
        P("narrow", None),
        P(),
        P(),
        P(),
        P(None, "narrow"),
        P("narrow"),
        P("narrow", None),
        P(),
        P(),
        P(),
        P("narrow", None),
        P("narrow", None),
        P("narrow", None),
        P("wide", None),
    )
    out_specs = (
        P("wide", None),
        P("wide", None),
        P(None, "narrow"),
        P("narrow"),
        P(None, "narrow"),
        P(None, "narrow"),
        P("narrow"),
        P("narrow", None),
        P(),
        P(),
        P(),
        P(None, "narrow"),
        P("narrow"),
        P("narrow", None),
        P(),
        P(),
        P(),
        P("narrow", None),
        P("narrow", None),
        P("narrow", None),
    )
    bits = mesh.shape["wide"].bit_length() - 1
    return jax.shard_map(functools.partial(local, bits), mesh=mesh, in_specs=in_specs, out_specs=out_specs, check_vma=False)
```

```python
import functools
import math

import jax
import jax.numpy as jnp
import numpy as np
from jax import lax
from jax.experimental import pallas as pl
from jax.experimental.pallas import tpu as pltpu
from jax.sharding import PartitionSpec as P

HEAD_DIM = 64
BINS1 = 32
BINS2 = 64
MAX_ORDER = 128
MAX_LAYOUT = 256
PAGE = 561


HIGHEST = lax.Precision.HIGHEST
EPSILON = 1e-05
SCORE_SCALE = 0.125

def bucket_steps(bins, reach):
    halfway = bins // 2
    exact = halfway // 2
    steps = []
    for level in range(1, halfway):
        if level < exact:
            steps.append(level)
        else:
            found = reach + 1
            for count in range(exact, reach + 2):
                value = exact + int(
                    math.log(count / exact) / math.log(reach / exact) * (halfway - exact)
                )
                if min(value, halfway - 1) >= level:
                    found = count
                    break
            steps.append(found)
    return steps


MESH = pl.DeviceIdType.MESH
BLOCK = 128
PC = 32
LAG = 4


def erf_of(x):
    x = jnp.clip(x, -3.832506856900711, 3.832506856900711)
    s = x * x
    top = -2.72614225801306e-10
    for term in (2.77068142495902e-08, -2.10102402082508e-06, -5.69250639462346e-05,
                 -7.34990630326855e-04, -2.95459980854025e-03, -1.60960333262415e-02):
        top = top * s + term
    low = -1.45660718464996e-05
    for term in (-2.13374055278905e-04, -1.68282697438203e-03, -7.37332916720468e-03,
                 -1.42647390514189e-02):
        low = low * s + term
    return x * top / low


def normal_cdf(x):
    return 0.5 + 0.5 * erf_of(x * math.sqrt(0.5))


def centre(values):
    c = values - jnp.mean(values, axis=-1, keepdims=True)
    r = lax.rsqrt(jnp.mean(c * c, axis=-1, keepdims=True) + EPSILON)
    return c * r, r


def norm_back(g, n, r, gain):
    m = g * gain
    return r * (m - jnp.mean(m, axis=-1, keepdims=True) - n * jnp.mean(m * n, axis=-1, keepdims=True))


def dot_nn(a, b):
    return lax.dot_general(a, b, (((1,), (0,)), ((), ())), preferred_element_type=jnp.float32)


def dot_nt(a, b):
    return lax.dot_general(a, b, (((1,), (1,)), ((), ())), preferred_element_type=jnp.float32)


def dot_tn(a, b):
    return lax.dot_general(a, b, (((0,), (0,)), ((), ())), preferred_element_type=jnp.float32)


class LineSum:
    def __init__(self, part, rx_in, rx_mid, tot, s_in, s_mid, r_in, r_mid):
        self.part, self.rx_in, self.rx_mid, self.tot = part, rx_in, rx_mid, tot
        self.s_in, self.s_mid, self.r_in, self.r_mid = s_in, s_mid, r_in, r_mid
        w, n = lax.axis_index("wide"), lax.axis_index("narrow")
        self.end = (n == 0) | (n == 3)
        self.mid = jnp.logical_not(self.end)
        self.side = (w, n + 1 - 2 * lax.rem(n, 2))
        self.across = (w, 3 - n)
        self.pieces = part.shape[0] // PC

    def rows(self, p):
        return pl.ds(p * PC, PC) if isinstance(p, int) else pl.ds(pl.multiple_of(p * PC, PC), PC)

    def copy_a(self, p):
        return pltpu.make_async_remote_copy(self.part.at[self.rows(p)], self.rx_in.at[self.rows(p)],
            self.s_in.at[p], self.r_in.at[p], device_id=self.side, device_id_type=MESH)

    def copy_b(self, p):
        return pltpu.make_async_remote_copy(self.part.at[self.rows(p)], self.rx_mid.at[self.rows(p)],
            self.s_mid.at[p], self.r_mid.at[p], device_id=self.across, device_id_type=MESH)

    def copy_t(self, p):
        return pltpu.make_async_remote_copy(self.tot.at[self.rows(p)], self.tot.at[self.rows(p)],
            self.s_in.at[p], self.r_in.at[p], device_id=self.side, device_id_type=MESH)

    def signal(self):
        bar = pltpu.get_barrier_semaphore()
        pl.semaphore_signal(bar, inc=1, device_id=self.side, device_id_type=MESH)

        @pl.when(self.mid)
        def _():
            pl.semaphore_signal(bar, inc=1, device_id=self.across, device_id_type=MESH)

    def ready(self, others):
        bar = pltpu.get_barrier_semaphore()

        @pl.when(self.end)
        def _():
            pl.semaphore_wait(bar, 1 + others)

        @pl.when(self.mid)
        def _():
            pl.semaphore_wait(bar, 2 + others)

    def free_part(self, p):
        @pl.when(self.end)
        def _():
            self.copy_a(p).wait_send()

        @pl.when(self.mid)
        def _():
            self.copy_b(p).wait_send()

    def finish(self, p, first):
        self.copy_b(p).wait_recv()
        if not first:
            self.copy_t(p).wait_send()
        self.tot[self.rows(p), :] = self.part[self.rows(p), :] + self.rx_mid[self.rows(p), :]
        self.copy_t(p).start()

    def slot(self, p, order, done=None):
        @pl.when(self.end)
        def _():
            self.copy_a(p).start()

        @pl.when(self.mid)
        def _():
            self.copy_a(p).wait_recv()
            self.part[self.rows(p), :] += self.rx_in[self.rows(p), :]
            self.copy_b(p).start()

            if done is not None:
                for q in done:
                    self.finish(q, order == 0)
                return

            @pl.when(p >= LAG)
            def _():
                self.finish(p - LAG, order == 0)

            if order > 0:
                @pl.when(p < LAG)
                def _():
                    self.finish(p + self.pieces - LAG, order == 1)

    def send_end(self, p):
        @pl.when(self.end)
        def _():
            self.copy_a(p).start()

    def slot_mid(self, p, done):
        @pl.when(self.mid)
        def _():
            self.copy_a(p).wait_recv()
            self.part[self.rows(p), :] += self.rx_in[self.rows(p), :]
            self.copy_b(p).start()
            for q in done:
                self.finish(q, False)

    def last(self, pieces):
        @pl.when(self.mid)
        def _():
            for q in pieces:
                self.finish(q, False)

    def want(self, p):
        @pl.when(self.end)
        def _():
            self.copy_t(p).wait_recv()

    def drain(self):
        def one(p, c):
            self.free_part(p)

            @pl.when(self.mid)
            def _():
                self.copy_t(p).wait_send()
            return c
        lax.fori_loop(0, self.pieces, one, 0)


WIDE_ROWS = 640
ROWS = 576


def bucket_number(offset, bins, reach):
    halfway = bins // 2
    steps = bucket_steps(bins, reach)
    return (halfway if offset > 0 else 0) + sum(1 for s in steps if abs(offset) >= s)


def choose_matrix(offsets, bins, reach):
    out = np.zeros((bins, len(offsets)), np.float32)
    for place, offset in enumerate(offsets):
        out[bucket_number(offset, bins, reach), place] = 1.0
    return out


def split3(x):
    hi = x.astype(jnp.bfloat16)
    rest = x - hi.astype(jnp.float32)
    mid = rest.astype(jnp.bfloat16)
    return hi, mid, (rest - mid.astype(jnp.float32)).astype(jnp.bfloat16)


def split2(x):
    hi = x.astype(jnp.bfloat16)
    return hi, (x - hi.astype(jnp.float32)).astype(jnp.bfloat16)


def exact_dot(a, b, dims):
    return lax.dot_general(a, b, (dims, ((), ())), precision=HIGHEST, preferred_element_type=jnp.float32)


def lanes_of(h, shape):
    lane = lax.broadcasted_iota(jnp.int32, shape, 1)
    return (lane >= h * HEAD_DIM) & (lane < (h + 1) * HEAD_DIM)


def block_rows(m, n):
    return pl.ds(m * BLOCK, n) if isinstance(m, int) else pl.ds(pl.multiple_of(m * BLOCK, BLOCK), n)


def block_window(m):
    start = 512 - m * BLOCK
    return pl.ds(start if isinstance(m, int) else pl.multiple_of(start, 128), WIDE_ROWS)


class CubeSum:
    def __init__(self, ref, rx1, rx2, rx3, rx4, rxb, ssem, rsem, free, bits):
        self.ref, self.rx1, self.rx2, self.rx3, self.rx4, self.rxb = ref, rx1, rx2, rx3, rx4, rxb
        self.ssem, self.rsem, self.free = ssem, rsem, free
        w, n = lax.axis_index("wide"), lax.axis_index("narrow")
        self.bit = [lax.rem(lax.div(w, 2 ** i), 2) for i in range(bits)]
        self.to = [(w + 2 ** i * (1 - 2 * self.bit[i]), n) for i in range(bits)]
        self.rows = ref.shape[0]
        half = self.rows // 2
        self.half, self.stream, self.eighth, self.piece = half, half // 2, half // 4, half // 8
        self.own = self.bit[0] * half
        self.axes = ((1, 2), (2, 1))
        self.extra = range(3, bits)

    def at(self, start, size):
        return pl.ds(pl.multiple_of(start, self.piece), size)

    def base1(self, s, other):
        b = self.bit[self.axes[s][0]]
        b = 1 - b if other else b
        return self.own + s * self.stream + b * self.eighth

    def base2(self, s, other):
        b = self.bit[self.axes[s][1]]
        b = 1 - b if other else b
        return self.base1(s, False) + b * self.piece

    def copy(self, src, dst, i, axis):
        return pltpu.make_async_remote_copy(src, dst, self.ssem.at[i], self.rsem.at[i], device_id=self.to[axis],
                                            device_id_type=MESH)

    def core_out(self):
        return self.copy(self.ref.at[self.at((1 - self.bit[0]) * self.half, self.half)], self.rx1, 0, 0)

    def first(self, s):
        return self.copy(self.ref.at[self.at(self.base1(s, True), self.eighth)], self.rx2[s], 1 + s, self.axes[s][0])

    def second(self, s):
        return self.copy(self.ref.at[self.at(self.base2(s, True), self.piece)], self.rx3[s], 3 + s, self.axes[s][1])

    def back2(self, s):
        r = self.at(self.base2(s, False), self.piece)
        return self.copy(self.ref.at[r], self.rxb[s], 5 + s, self.axes[s][1])

    def back1(self, s):
        r = self.at(self.base1(s, False), self.eighth)
        return self.copy(self.ref.at[r], self.ref.at[r], 7 + s, self.axes[s][0])

    def core_back(self):
        r = self.at(self.own, self.half)
        return self.copy(self.ref.at[r], self.ref.at[r], 9, 0)

    def more(self, e, s):
        i = e - 3
        return self.copy(self.ref.at[self.at(self.base2(s, False), self.piece)], self.rx4.at[i, s], 10 + 2 * i + s, e)

    def release(self, i, axis):
        pl.semaphore_signal(self.free.at[i], inc=1, device_id=self.to[axis], device_id_type=MESH)

    def step(self, i):
        if i == 0:
            self.core_out().start()
        if i == 1:
            self.core_out().wait_recv()
            self.ref[self.at(self.own, self.half), :] += self.rx1[...]
            for s in range(2):
                self.first(s).start()
            self.core_out().wait_send()
            self.release(0, 0)
        if i == 2:
            for s in range(2):
                self.first(s).wait()
                self.release(1 + s, self.axes[s][0])
                self.ref[self.at(self.base1(s, False), self.eighth), :] += self.rx2[s][...]
                self.second(s).start()
        if i == 3:
            for s in range(2):
                self.second(s).wait()
                self.ref[self.at(self.base2(s, False), self.piece), :] += self.rx3[s][...]
            for e in self.extra:
                for s in range(2):
                    self.more(e, s).start()
                for s in range(2):
                    self.more(e, s).wait()
                    self.ref[self.at(self.base2(s, False), self.piece), :] += self.rx4[e - 3, s]
            for s in range(2):
                self.back2(s).start()
        if i == 4:
            for s in range(2):
                self.back2(s).wait_recv()
                self.ref[self.at(self.base2(s, True), self.piece), :] = self.rxb[s][...]
                pl.semaphore_wait(self.free.at[1 + s], 1)
                self.back1(s).start()
        if i == 5:
            for s in range(2):
                self.back1(s).wait_recv()
            pl.semaphore_wait(self.free.at[0], 1)
            self.core_back().start()
        if i == 6:
            self.core_back().wait()
            for s in range(2):
                self.back2(s).wait_send()
                self.back1(s).wait_send()


def layer_kernel(bits, tok_h, cot_h, wq_h, wk_h, wv_h, wo_h, wi_h, wd_h, reg, rank, box, bq, bv, bo_r, g1_r, b1_r, bi_r, bd_r, g2_r, b2_r,
                 to, tx, ty, so, sxy, sgo, sgxy,
                 out_h, gin_h, gat_h, gwi_h, gwd_h, sm,
                 out, gin, gat, gwi, gwd, part, rx_in, rx_mid, tot, res, cotp, hid, pre, act, gff, hlow, gpre, low, perm,
                 q_s, k_s, v_s, prob, att, ob, obf, pairs, ob4, split_s, base, ga, gt, qt, dkt, dvt, dq, dk, dv, gacc,
                 ws, wo, wi, wd, outp, rows_s, vec_s, rx1, rx2, rx3, rx4, rxb, rxs,
                 s_in, s_mid, r_in, r_mid, cs, cr, cf, ss, sr, ls):
    f32, bf = jnp.float32, jnp.bfloat16
    n = PAGE
    width = wo_h.shape[0]
    heads = to.shape[0]
    block_pieces = BLOCK // PC
    line = LineSum(part, rx_in, rx_mid, tot, s_in, s_mid, r_in, r_mid)
    pieces = line.pieces
    closing = {p: [p - LAG] for p in range(LAG, pieces)}
    closing[pieces - 2] = [pieces - 6, pieces - 5]
    closing[pieces - 1] = [pieces - 4, pieces - 3]
    rest1, rest2, rest3, restb = pre.at[pl.ds(0, 384)], pre.at[pl.ds(384, 192)], cotp.at[pl.ds(0, 96)], cotp.at[pl.ds(96, 96)]
    cube = [CubeSum(gwi, rx1.at[0], [rx2.at[0, s] for s in range(2)], [rx3.at[0, s] for s in range(2)], rx4.at[0],
                    [rxb.at[0, s] for s in range(2)], cs.at[0], cr.at[0], cf.at[0], bits),
            CubeSum(gwd, rx1.at[1], [rx2.at[1, s] for s in range(2)], [rx3.at[1, s] for s in range(2)], rx4.at[1],
                    [rxb.at[1, s] for s in range(2)], cs.at[1], cr.at[1], cf.at[1], bits),
            CubeSum(gat, rest1, [pre.at[pl.ds(384 + 96 * s, 96)] for s in range(2)],
                    [cotp.at[pl.ds(48 * s, 48)] for s in range(2)], rx4.at[2],
                    [cotp.at[pl.ds(96 + 48 * s, 48)] for s in range(2)], cs.at[2], cr.at[2], cf.at[2], bits)]

    def load(i, src, dst):
        return pltpu.make_async_copy(src, dst, ls.at[i])
    loads = [load(0, tok_h, out)]
    loads += [load(1 + i, src, gat.at[pl.ds(i * width, width)]) for i, src in enumerate((wq_h, wk_h, wv_h, wo_h))]
    loads += [load(5, wi_h, gwi), load(6, wd_h, gwd), load(7, cot_h, gin)]
    for c in loads:
        c.start()
    bar = pltpu.get_barrier_semaphore()
    for peer in cube[0].to:
        pl.semaphore_signal(bar, inc=1, device_id=peer, device_id_type=MESH)
    line.signal()

    rows_s[...] = jnp.full(rows_s.shape, 1e4, f32)
    rows_s[0, 0:n] = reg[...].astype(f32)
    rows_s[1, 0:n] = rank[...].astype(f32)
    rows_s[2:4, 0:n] = box[...].astype(f32)
    region_row, rank_row = rows_s[0:1, :], rows_s[1:2, :]
    i0 = lax.broadcasted_iota(jnp.int32, (WIDE_ROWS, WIDE_ROWS), 0)
    i1 = lax.broadcasted_iota(jnp.int32, (WIDE_ROWS, WIDE_ROWS), 1)
    region_col = jnp.sum(jnp.where(i0 == i1, region_row, 0.0), axis=1, keepdims=True)
    place = jnp.sum(jnp.where(region_col < region_row, 1.0, 0.0), axis=0, keepdims=True) + rank_row
    perm[...] = jnp.where(i0.astype(f32) == place, 1.0, 0.0).astype(bf)
    split_s[...] = jnp.zeros_like(split_s)
    for i, vector in enumerate((bo_r, g1_r, b1_r, bi_r, bd_r, g2_r, b2_r)):
        vec_s[i, :] = vector[...]
    vec_s[7:9, :] = jnp.zeros((2, vec_s.shape[1]), f32)
    vec_s[7, 0:width] = bq[...]
    vec_s[8, 0:width] = bv[...]
    b_out, g1, b1, b_in, b_down, g2, b2 = (vec_s[i:i + 1, :] for i in range(7))

    def sort_first(source, target, first):
        split_s[0:n, :] = source[...].astype(bf)
        y = dot_nn(perm[...], split_s[...])
        if first is not None:
            first[...] = y.astype(bf)
        target[...] = y[0:ROWS, :]

    def sort_rest(source, target):
        for i in range(1, 3):
            split_s[0:n, :] = split3(source[...])[i]
            target[...] += dot_nn(perm[0:ROWS, :], split_s[...])

    loads[0].wait()
    sort_first(out, res, low)
    code = lax.broadcasted_iota(jnp.int32, (128, WIDE_ROWS), 0).astype(f32)
    for i in range(2):
        row = rows_s[2 + i:3 + i, :]
        one = dot_nt(perm[...], jnp.where(code == row, 1.0, 0.0).astype(bf)).astype(bf)
        ob[:, 128 * i:128 * (i + 1)] = one
        ob4[:, 256 * i:256 * i + 128] = one
        ob4[:, 256 * i + 128:256 * i + 256] = one
        obf[:, 128 * i:128 * (i + 1)] = dot_nt(perm[...], jnp.where(127.0 - code == row, 1.0, 0.0).astype(bf)).astype(bf)
    ws[...] = jnp.zeros_like(ws)
    for i in range(3):
        loads[1 + i].wait()
        ws[i, 0:width, :] = gat[i * width:(i + 1) * width, :].astype(bf)
    q_s[...] = ((dot_nt(low[...], ws[0]) + vec_s[7:8, 0:256]).astype(bf) * SCORE_SCALE).astype(bf)
    k_s[...] = dot_nt(low[...], ws[1]).astype(bf)
    v_s[...] = (dot_nt(low[...], ws[2]) + vec_s[8:9, 0:256]).astype(bf)
    wo[...] = jnp.zeros_like(wo)
    loads[4].wait()
    wo[0:width, :] = gat[3 * width:4 * width, :].astype(bf)
    row_o = exact_dot(to[...], so[...], ((1,), (0,)))
    row_xy = (exact_dot(tx[...], sxy[...], ((1,), (0,))), exact_dot(ty[...], sxy[...], ((1,), (0,))))
    for h in range(heads):
        base[h] = pltpu.roll(jnp.broadcast_to(row_o[h:h + 1, :], (128, 1280)), 0, 1, stride=1, stride_axis=0)
        for i in range(2):
            table = pltpu.roll(jnp.broadcast_to(row_xy[i][h:h + 1, :], (128, 256)), 0, 1, stride=1, stride_axis=0)
            pairs[h, i] = jnp.concatenate(split2(table[:, 0:128]), axis=1)
    line.ready(bits)

    def blocks(body, start=0):
        full = ROWS // BLOCK

        def step(m, carry):
            body(m, BLOCK)
            return carry
        lax.fori_loop(start, full, step, 0)
        if ROWS % BLOCK:
            body(full, ROWS % BLOCK)

    def sends(m, rows, order):
        for j in range(rows // PC):
            p = m * block_pieces + j
            line.slot(p, order, closing[p] if order == 2 and isinstance(p, int) else None)

    def attend(m, rows):
        r = block_rows(m, rows)
        mixed = None
        for h in range(heads):
            qh = jnp.where(lanes_of(h, (rows, 256)), q_s[r, :], jnp.zeros((), bf))
            bias = jnp.concatenate([dot_nn(ob[r, 128 * i:128 * (i + 1)], pairs[h, i]).astype(bf) for i in range(2)], axis=1)
            s = dot_nt(qh, k_s[...]) + dot_nt(bias, ob4[...]) + base[h, 0:rows, block_window(m)]
            s = jnp.where(lax.broadcasted_iota(jnp.int32, s.shape, 1) < n, s, -1e30)
            e = jnp.exp(s - jnp.max(s, axis=1, keepdims=True))
            p = e / jnp.sum(e, axis=1, keepdims=True)
            prob[h, r, :] = p
            pv = dot_nn(p.astype(bf), v_s[...])
            mixed = pv if h == 0 else jnp.where(lanes_of(h, (rows, 256)), pv, mixed)
        mixed = mixed.astype(bf)
        att[r, :] = mixed
        part[r, :] = dot_nn(mixed, wo[...])
        sends(m, rows, 0)
    blocks(attend)

    sort_rest(out, res)
    loads[5].wait()
    wi[...] = gwi[...].astype(bf)
    loads[6].wait()
    wd[...] = gwd[...].astype(bf)
    sm[...] = jnp.zeros_like(sm)

    def open_block(m, rows):
        for j in range(rows // PC):
            line.want(m * block_pieces + j)
        for j in range(rows // PC):
            line.free_part(m * block_pieces + j)

    def forward(m, rows):
        r = block_rows(m, rows)
        open_block(m, rows)
        one = res[r, :] + (tot[r, :] + b_out)
        res[r, :] = one
        c, _ = centre(one)
        hidden = c * g1 + b1
        hid[r, :] = hidden
        hl = hidden.astype(bf)
        hlow[r, :] = hl
        u = dot_nn(hl, wi[...]) + b_in
        pre[r, :] = u
        a = (u * normal_cdf(u)).astype(bf)
        act[r, :] = a
        part[r, :] = dot_nn(a, wd[...])
        sends(m, rows, 1)
    blocks(forward)

    loads[7].wait()
    sort_first(gin, cotp, None)
    sort_rest(gin, cotp)
    outp[...] = jnp.zeros_like(outp)
    qt[...] = jnp.transpose(q_s[...])
    dkt[...] = jnp.zeros_like(dkt)
    dvt[...] = jnp.zeros_like(dvt)
    base[...] = jnp.zeros_like(base)
    gacc[...] = jnp.zeros_like(gacc)
    ga[...] = jnp.zeros_like(ga)
    dq[...] = jnp.zeros_like(dq)
    gat[3 * width:4 * width, :] = jnp.zeros((width, gat.shape[1]), f32)

    def add_row(i, value):
        sm[i:i + 1, :] += jnp.sum(value, axis=0, keepdims=True)

    def put_back(r, y):
        total = outp[...]
        for piece in split3(y):
            total = total + dot_tn(perm[r, :], piece)
        outp[...] = total

    def back(m, rows):
        r = block_rows(m, rows)
        open_block(m, rows)
        two = hid[r, :] + (tot[r, :] + b_down)
        c, rs = centre(two)
        g = cotp[r, :]
        add_row(0, g * c)
        add_row(1, g)
        gradient = norm_back(g, c, rs, g2)
        hid[r, :] = gradient
        gl = gradient.astype(bf)
        gff[r, :] = gl
        add_row(2, gl.astype(f32))
        slope_in = dot_nt(gl, wd[...])
        u = pre[r, :]
        slope = normal_cdf(u) + u * (jnp.exp(-0.5 * u * u) * (1.0 / math.sqrt(2.0 * math.pi)))
        gp = (slope_in * slope).astype(bf)
        gpre[r, :] = gp
        add_row(3, gp.astype(f32))
        part[r, :] = dot_nt(gp, wi[...])
        sends(m, rows, 2)
        put_back(r, c * g2 + b2)

    def attend_back(m, rows):
        r = block_rows(m, rows)
        for j in range(rows // PC):
            line.want(m * block_pieces + j)
        g = hid[r, :] + tot[r, :]
        c, rs = centre(res[r, :])
        add_row(4, g * c)
        add_row(5, g)
        gradient = norm_back(g, c, rs, g1)
        hid[r, :] = gradient
        gb = gradient.astype(bf)
        add_row(6, gb.astype(f32))
        gat[3 * width:4 * width, :] += dot_tn(att[r, :], gb)[0:width, :]
        gab = dot_nt(gb, wo[...]).astype(bf)
        ga[0:rows, :] = gab
        gt[...] = jnp.transpose(ga[...])
        cols = pl.ds(pl.multiple_of(m * BLOCK, BLOCK), rows)
        query_grad = None
        for h in range(heads):
            gh = jnp.where(lanes_of(h, (rows, 256)), gab, jnp.zeros((), bf))
            dp = dot_nt(gh, v_s[...])
            p = prob[h, r, :]
            inner = jnp.sum(p * dp, axis=1, keepdims=True)
            ds = (p * (dp - inner)).astype(bf)
            dqh = dot_nn(ds, k_s[...])
            query_grad = dqh if h == 0 else jnp.where(lanes_of(h, (rows, 256)), dqh, query_grad)
            base[h, 0:rows, block_window(m)] += ds.astype(f32)
            hr = pl.ds(h * HEAD_DIM, HEAD_DIM)
            dkt[hr, :] += dot_nn(qt[hr, cols], ds)
            dvt[hr, :] += dot_nn(gt[hr, 0:rows], p.astype(bf))
            u = jnp.concatenate(split2(dot_nn(ds, ob[...])), axis=1)
            gg = dot_tn(obf[r, :], u)
            for i in range(2):
                b = 128 * i
                gacc[h, i] += gg[b:b + 128, b:b + 128] + gg[b:b + 128, 256 + b:384 + b]
        dq[r, :] = jnp.where(lax.broadcasted_iota(jnp.int32, (rows, 256), 1) < width, query_grad * SCORE_SCALE, 0.0).astype(bf)

    def back_step(m, carry):
        back(m, BLOCK)

        @pl.when(m == ROWS // BLOCK - 1)
        def _():
            attend_back(0, BLOCK)
        return carry
    lax.fori_loop(0, ROWS // BLOCK, back_step, 0)
    back(ROWS // BLOCK, ROWS % BLOCK)

    def late_step(m, carry):
        @pl.when(m == 2)
        def _():
            line.last([pieces - 2, pieces - 1])
            gwd[...] = dot_tn(act[...], gff[...])
            cube[1].step(0)
            gwi[...] = dot_tn(hlow[...], gpre[...])
            cube[0].step(0)
        attend_back(m, BLOCK)
        return carry
    lax.fori_loop(1, ROWS // BLOCK, late_step, 0)
    out[...] = outp[0:n, :]
    store_out = [pltpu.make_async_copy(a, b, ls.at[i]) for i, (a, b) in enumerate(((out, out_h), (gwd, gwd_h), (gwi, gwi_h), (gat, gat_h), (gin, gin_h)))]
    store_out[0].start()
    outp[...] = jnp.zeros_like(outp)
    attend_back(ROWS // BLOCK, ROWS % BLOCK)
    dk[...] = jnp.transpose(dkt[...]).astype(bf)
    dv[...] = jnp.transpose(dvt[...]).astype(bf)
    cube[1].step(1)
    cube[0].step(1)

    def produce(m, rows):
        r = block_rows(m, rows)
        for j in range(rows // PC):
            line.free_part(m * block_pieces + j)
        part[r, :] = dot_nn(dq[r, :], ws[0]) + dot_nn(dk[r, :], ws[1]) + dot_nn(dv[r, :], ws[2])
        for j in range(rows // PC):
            line.send_end(m * block_pieces + j)
    blocks(produce)

    def table_sums(h):
        for i in range(2):
            both = jnp.concatenate([gacc[h, i], jnp.zeros((128, 128), f32)], axis=1)
            line_sum = jnp.sum(pltpu.roll(both, 0, 1, stride=1, stride_axis=0), axis=0, keepdims=True)
            sm[10 + heads * (i + 1) + h:11 + heads * (i + 1) + h, 0:BINS2] = exact_dot(line_sum, sgxy[...], ((1,), (1,)))
        flip = (lax.broadcasted_iota(jnp.int32, (128, 128), 0) + lax.broadcasted_iota(jnp.int32, (128, 128), 1)) == 127
        flip = jnp.where(flip, 1.0, 0.0).astype(bf)
        hi, lo = split2(base[h])
        turned = dot_nn(flip, hi) + dot_nn(flip, lo)
        line_sum = jnp.sum(pltpu.roll(turned, 0, 1, stride=1, stride_axis=0), axis=0, keepdims=True)
        sm[10 + h:11 + h, 0:BINS1] = exact_dot(line_sum, sgo[...], ((1,), (1,)))

    def bias_sums(_):
        sm[8:9, 0:256] = jnp.sum(dq[...].astype(f32), axis=0, keepdims=True)
        sm[9:10, 0:256] = jnp.sum(dv[...].astype(f32), axis=0, keepdims=True)

    bit_to = cube[0].to

    def small_copy(i):
        return pltpu.make_async_remote_copy(sm, rxs.at[i], ss.at[i], sr.at[i], device_id=bit_to[i], device_id_type=MESH)

    def small_step(i):
        if i > 0:
            small_copy(i - 1).wait()
            sm[...] += rxs[i - 1]
        if i < bits:
            small_copy(i).start()

    def weight_grad(i):
        gat[i * width:(i + 1) * width, :] = dot_tn((dq, dk, dv)[i][...], low[...])[0:width, :]

    def consume(m):
        rows = min(BLOCK, ROWS - m * BLOCK)
        for j in range(rows // PC):
            line.want(m * block_pieces + j)
        r = slice(m * BLOCK, m * BLOCK + rows)
        put_back(r, hid[r, :] + tot[r, :])

    def both_step(i):
        cube[1].step(i)
        cube[0].step(i)
    jobs = {0: [(weight_grad, 0)], 1: [(weight_grad, 1)], 2: [(weight_grad, 2)], 3: [(cube[2].step, 0)], 4: [(both_step, 2), (bias_sums, 0)],
            5: [(cube[2].step, 1), (table_sums, 0)], 6: [(table_sums, 1)], 7: [(table_sums, 2), (small_step, 0)],
            8: [(both_step, 3)], 9: [(cube[2].step, 2), (small_step, 1)], 10: [(consume, 0)], 11: [(both_step, 4), (small_step, 2)],
            12: [(cube[2].step, 3)], 13: [(small_step, 3)], 14: [(consume, 1), (cube[2].step, 4)], 17: [(both_step, 5)]}
    ending = {p: [p - LAG] for p in range(LAG, pieces - 4)}
    ending.update({pieces - 4: [pieces - 8, pieces - 7], pieces - 3: [pieces - 6], pieces - 2: [pieces - 5, pieces - 4],
                   pieces - 1: [pieces - 3, pieces - 2]})
    for p in range(pieces):
        line.slot_mid(p, ending.get(p, ()))
        for job, arg in jobs.get(p, ()):
            job(arg)
    line.last([pieces - 1])
    for i in range(4, bits + 1):
        small_step(i)
    consume(2)
    cube[2].step(5)
    consume(3)
    both_step(6)
    store_out[1].start()
    store_out[2].start()
    cube[2].step(6)
    store_out[3].start()
    consume(4)
    gin[...] = outp[0:n, :]
    store_out[4].start()
    line.drain()
    for c in store_out:
        c.wait()


def layer(bits, tok, cot, wq, wk, wv, wo, wi, wd, *small_args):
    f32, bf = jnp.float32, jnp.bfloat16
    d = tok.shape[1]
    f = wi.shape[1]
    width = wo.shape[0]
    heads = small_args[12].shape[0]
    sd = jax.ShapeDtypeStruct
    W, R = WIDE_ROWS, ROWS
    pieces = R // PC
    more = max(bits - 3, 1)
    vm, hbm = pl.BlockSpec(memory_space=pltpu.VMEM), pl.BlockSpec(memory_space=pl.ANY)
    v_ = pltpu.VMEM
    shapes = (sd((PAGE, d), f32), sd((PAGE, d), f32), sd((4 * width, d), f32), sd((d, f), f32), sd((f, d), f32), sd((24, d), f32))
    scratch = [v_(s.shape, f32) for s in shapes[:5]]
    scratch += [v_((R, d), f32)] * 7 + [v_((R, f), f32), v_((R, f), bf), v_((R, d), bf), v_((R, d), bf), v_((R, f), bf)]
    scratch += [v_((W, d), bf), v_((W, W), bf)] + [v_((W, 256), bf)] * 3 + [v_((heads, R, W), f32)] + [v_((W, 256), bf)] * 3
    scratch += [v_((heads, 2, 128, 256), bf), v_((W, 512), bf), v_((W, d), bf), v_((heads, 128, 1280), f32)]
    scratch += [v_((BLOCK, 256), bf), v_((256, BLOCK), bf), v_((256, W), bf), v_((256, W), f32), v_((256, W), f32)]
    scratch += [v_((W, 256), bf)] * 3 + [v_((heads, 2, 128, 128), f32)]
    scratch += [v_((3, 256, d), bf), v_((256, d), bf), v_((d, f), bf), v_((f, d), bf), v_((W, d), f32), v_((8, W), f32), v_((16, d), f32)]
    scratch += [v_((2, d // 2, d), f32), v_((2, 2, d // 8, d), f32), v_((2, 2, d // 16, d), f32), v_((3, more, 2, d // 16, d), f32),
                v_((2, 2, d // 16, d), f32), v_((bits, 24, d), f32)]
    scratch += [pltpu.SemaphoreType.DMA((pieces,))] * 4 + [pltpu.SemaphoreType.DMA((3, 10 + 2 * more))] * 2
    scratch += [pltpu.SemaphoreType.REGULAR((3, 3))] + [pltpu.SemaphoreType.DMA((bits,))] * 2 + [pltpu.SemaphoreType.DMA((8,))]
    return pl.pallas_call(
        functools.partial(layer_kernel, bits), out_shape=shapes, in_specs=[hbm] * 8 + [vm] * 19, out_specs=[hbm] * 5 + [vm],
        scratch_shapes=scratch,
        compiler_params=pltpu.CompilerParams(collective_id=0, has_side_effects=True, vmem_limit_bytes=62 << 20),
        cost_estimate=pl.CostEstimate(flops=3 * 10 ** 10, bytes_accessed=20 << 20, transcendentals=heads * R * W),
    )(tok, cot, wq, wk, wv, wo, wi, wd, *small_args)


def finish_kernel(out_in, gin_in, gat_in, gwi_in, gwd_in, sm, out, gin, gwq, gwk, gwv, gwo, gwi, gwd, *rest):
    vectors, (b_out, b_gin, b_gat, b_gwi, b_gwd, sem_in, sem_out) = rest[:12], rest[12:]
    width = gwo.shape[0]
    heads = vectors[9].shape[0]
    whole = [(out_in, b_out, out), (gin_in, b_gin, gin), (gwi_in, b_gwi, gwi), (gwd_in, b_gwd, gwd)]
    for i, g in enumerate((gwq, gwk, gwv, gwo)):
        r = pl.ds(i * width, width)
        whole.append((gat_in.at[r], b_gat.at[r], g))
    inward = [pltpu.make_async_copy(a, b, sem_in.at[i]) for i, (a, b, _) in enumerate(whole)]
    outward = [pltpu.make_async_copy(b, c, sem_out.at[i]) for i, (_, b, c) in enumerate(whole)]
    for c in inward:
        c.start()
    for i in range(7):
        vectors[i][...] = sm[i, :]
    vectors[7][...] = sm[8, 0:width]
    vectors[8][...] = sm[9, 0:width]
    vectors[9][...] = sm[10:10 + heads, 0:BINS1]
    vectors[10][...] = sm[10 + heads:10 + 2 * heads, 0:BINS2]
    vectors[11][...] = sm[10 + 2 * heads:10 + 3 * heads, 0:BINS2]
    for c, o in zip(inward, outward):
        c.wait()
        o.start()
    for o in outward:
        o.wait()


def finish(heads, width, out, gin, gat, gwi, gwd, sm):
    f32 = jnp.float32
    sd = jax.ShapeDtypeStruct
    d = gat.shape[1]
    like = lambda x: sd(x.shape, f32)
    shapes = (like(out), like(gin)) + (sd((width, d), f32),) * 4 + (like(gwi), like(gwd)) + (sd((d,), f32),) * 7 \
        + (sd((width,), f32),) * 2 + (sd((heads, BINS1), f32), sd((heads, BINS2), f32), sd((heads, BINS2), f32))
    vm, hbm = pl.BlockSpec(memory_space=pltpu.VMEM), pl.BlockSpec(memory_space=pl.ANY)
    return pl.pallas_call(
        finish_kernel, out_shape=shapes, in_specs=[hbm] * 5 + [vm], out_specs=[hbm] * 8 + [vm] * 12,
        scratch_shapes=[pltpu.VMEM(x.shape, f32) for x in (out, gin, gat, gwi, gwd)] + [pltpu.SemaphoreType.DMA((8,))] * 2,
        compiler_params=pltpu.CompilerParams(vmem_limit_bytes=56 << 20),
    )(out, gin, gat, gwi, gwd, sm)


def local(
    bits,
    tokens,
    region,
    order_rank,
    box_coords,
    w_query,
    b_query,
    w_key,
    w_value,
    b_value,
    w_out,
    b_out,
    ln1_gain,
    ln1_bias,
    w_in,
    b_in,
    w_down,
    b_down,
    ln2_gain,
    ln2_bias,
    rel_order,
    rel_x,
    rel_y,
    cotangent,
):
    so = choose_matrix([i - 512 if i < 1152 else i - 1792 for i in range(1280)], BINS1, MAX_ORDER)
    sxy = choose_matrix([i if i < 128 else i - 256 for i in range(256)], BINS2, MAX_LAYOUT)
    sgo = choose_matrix([i - 639 for i in range(1280)], BINS1, MAX_ORDER)
    sgxy = choose_matrix([i - 127 for i in range(256)], BINS2, MAX_LAYOUT)
    width = w_out.shape[0]
    heads = rel_order.shape[0]
    output, gin, gat, gwi, gwd, sm = layer(
        bits, tokens, cotangent, w_query.T, w_key.T, w_value.T, w_out, w_in, w_down, region, order_rank, box_coords, b_query, b_value,
        b_out, ln1_gain, ln1_bias, b_in, b_down, ln2_gain, ln2_bias, rel_order, rel_x, rel_y, so, sxy, sgo, sgxy)
    (output, gin, gwq, gwk, gwv, gwo, gwi, gwd, l2g, l2b, bd, bi, l1g, l1b, bo, gbq, gbv, ro, rx, ry) = finish(
        heads, width, output, gin, gat, gwi, gwd, sm)
    return (output, gin, gwq.T, gbq, gwk.T, gwv.T, gbv, gwo, bo, l1g, l1b, gwi, bi,
            gwd, bd, l2g, l2b, ro, rx, ry)


def solution(mesh):
    in_specs = (
        P("wide", None),
        P("wide"),
        P("wide"),
        P(None, "wide"),
        P(None, "narrow"),
        P("narrow"),
        P(None, "narrow"),
        P(None, "narrow"),
        P("narrow"),
        P("narrow", None),
        P(),
        P(),
        P(),
        P(None, "narrow"),
        P("narrow"),
        P("narrow", None),
        P(),
        P(),
        P(),
        P("narrow", None),
        P("narrow", None),
        P("narrow", None),
        P("wide", None),
    )
    out_specs = (
        P("wide", None),
        P("wide", None),
        P(None, "narrow"),
        P("narrow"),
        P(None, "narrow"),
        P(None, "narrow"),
        P("narrow"),
        P("narrow", None),
        P(),
        P(),
        P(),
        P(None, "narrow"),
        P("narrow"),
        P("narrow", None),
        P(),
        P(),
        P(),
        P("narrow", None),
        P("narrow", None),
        P("narrow", None),
    )
    bits = mesh.shape["wide"].bit_length() - 1
    return jax.shard_map(functools.partial(local, bits), mesh=mesh, in_specs=in_specs, out_specs=out_specs, check_vma=False)
```

```python
import functools
import math

import jax
import jax.numpy as jnp
import numpy as np
from jax import lax
from jax.experimental import pallas as pl
from jax.experimental.pallas import tpu as pltpu
from jax.sharding import PartitionSpec as P

HEAD_DIM = 64
BINS1 = 32
BINS2 = 64
MAX_ORDER = 128
MAX_LAYOUT = 256
PAGE = 561


HIGHEST = lax.Precision.HIGHEST
EPSILON = 1e-05
SCORE_SCALE = 0.125

def bucket_steps(bins, reach):
    halfway = bins // 2
    exact = halfway // 2
    steps = []
    for level in range(1, halfway):
        if level < exact:
            steps.append(level)
        else:
            found = reach + 1
            for count in range(exact, reach + 2):
                value = exact + int(
                    math.log(count / exact) / math.log(reach / exact) * (halfway - exact)
                )
                if min(value, halfway - 1) >= level:
                    found = count
                    break
            steps.append(found)
    return steps


MESH = pl.DeviceIdType.MESH
BLOCK = 128
PC = 32
LAG = 4


def erf_of(x):
    x = jnp.clip(x, -3.832506856900711, 3.832506856900711)
    s = x * x
    top = -2.72614225801306e-10
    for term in (2.77068142495902e-08, -2.10102402082508e-06, -5.69250639462346e-05,
                 -7.34990630326855e-04, -2.95459980854025e-03, -1.60960333262415e-02):
        top = top * s + term
    low = -1.45660718464996e-05
    for term in (-2.13374055278905e-04, -1.68282697438203e-03, -7.37332916720468e-03,
                 -1.42647390514189e-02):
        low = low * s + term
    return x * top / low


def normal_cdf(x):
    return 0.5 + 0.5 * erf_of(x * math.sqrt(0.5))


def centre(values):
    c = values - jnp.mean(values, axis=-1, keepdims=True)
    r = lax.rsqrt(jnp.mean(c * c, axis=-1, keepdims=True) + EPSILON)
    return c * r, r


def norm_back(g, n, r, gain):
    m = g * gain
    return r * (m - jnp.mean(m, axis=-1, keepdims=True) - n * jnp.mean(m * n, axis=-1, keepdims=True))


def dot_nn(a, b):
    return lax.dot_general(a, b, (((1,), (0,)), ((), ())), preferred_element_type=jnp.float32)


def dot_nt(a, b):
    return lax.dot_general(a, b, (((1,), (1,)), ((), ())), preferred_element_type=jnp.float32)


def dot_tn(a, b):
    return lax.dot_general(a, b, (((0,), (0,)), ((), ())), preferred_element_type=jnp.float32)


class LineSum:
    def __init__(self, part, rx_in, rx_mid, tot, s_in, s_mid, r_in, r_mid):
        self.part, self.rx_in, self.rx_mid, self.tot = part, rx_in, rx_mid, tot
        self.s_in, self.s_mid, self.r_in, self.r_mid = s_in, s_mid, r_in, r_mid
        w, n = lax.axis_index("wide"), lax.axis_index("narrow")
        self.end = (n == 0) | (n == 3)
        self.mid = jnp.logical_not(self.end)
        self.side = (w, n + 1 - 2 * lax.rem(n, 2))
        self.across = (w, 3 - n)
        self.pieces = part.shape[0] // PC

    def rows(self, p):
        return pl.ds(p * PC, PC) if isinstance(p, int) else pl.ds(pl.multiple_of(p * PC, PC), PC)

    def copy_a(self, p):
        return pltpu.make_async_remote_copy(self.part.at[self.rows(p)], self.rx_in.at[self.rows(p)],
            self.s_in.at[p], self.r_in.at[p], device_id=self.side, device_id_type=MESH)

    def copy_b(self, p):
        return pltpu.make_async_remote_copy(self.part.at[self.rows(p)], self.rx_mid.at[self.rows(p)],
            self.s_mid.at[p], self.r_mid.at[p], device_id=self.across, device_id_type=MESH)

    def copy_t(self, p):
        return pltpu.make_async_remote_copy(self.tot.at[self.rows(p)], self.tot.at[self.rows(p)],
            self.s_in.at[p], self.r_in.at[p], device_id=self.side, device_id_type=MESH)

    def signal(self):
        bar = pltpu.get_barrier_semaphore()
        pl.semaphore_signal(bar, inc=1, device_id=self.side, device_id_type=MESH)

        @pl.when(self.mid)
        def _():
            pl.semaphore_signal(bar, inc=1, device_id=self.across, device_id_type=MESH)

    def ready(self, others):
        bar = pltpu.get_barrier_semaphore()

        @pl.when(self.end)
        def _():
            pl.semaphore_wait(bar, 1 + others)

        @pl.when(self.mid)
        def _():
            pl.semaphore_wait(bar, 2 + others)

    def free_part(self, p):
        @pl.when(self.end)
        def _():
            self.copy_a(p).wait_send()

        @pl.when(self.mid)
        def _():
            self.copy_b(p).wait_send()

    def finish(self, p, first):
        self.copy_b(p).wait_recv()
        if not first:
            self.copy_t(p).wait_send()
        self.tot[self.rows(p), :] = self.part[self.rows(p), :] + self.rx_mid[self.rows(p), :]
        self.copy_t(p).start()

    def slot(self, p, order, done=None):
        @pl.when(self.end)
        def _():
            self.copy_a(p).start()

        @pl.when(self.mid)
        def _():
            self.copy_a(p).wait_recv()
            self.part[self.rows(p), :] += self.rx_in[self.rows(p), :]
            self.copy_b(p).start()

            if done is not None:
                for q in done:
                    self.finish(q, order == 0)
                return

            @pl.when(p >= LAG)
            def _():
                self.finish(p - LAG, order == 0)

            if order > 0:
                @pl.when(p < LAG)
                def _():
                    self.finish(p + self.pieces - LAG, order == 1)

    def send_end(self, p):
        @pl.when(self.end)
        def _():
            self.copy_a(p).start()

    def slot_mid(self, p, done):
        @pl.when(self.mid)
        def _():
            self.copy_a(p).wait_recv()
            self.part[self.rows(p), :] += self.rx_in[self.rows(p), :]
            self.copy_b(p).start()
            for q in done:
                self.finish(q, False)

    def last(self, pieces):
        @pl.when(self.mid)
        def _():
            for q in pieces:
                self.finish(q, False)

    def want(self, p):
        @pl.when(self.end)
        def _():
            self.copy_t(p).wait_recv()

    def drain(self):
        def one(p, c):
            self.free_part(p)

            @pl.when(self.mid)
            def _():
                self.copy_t(p).wait_send()
            return c
        lax.fori_loop(0, self.pieces, one, 0)


WIDE_ROWS = 640
ROWS = 576


def bucket_number(offset, bins, reach):
    halfway = bins // 2
    steps = bucket_steps(bins, reach)
    return (halfway if offset > 0 else 0) + sum(1 for s in steps if abs(offset) >= s)


def choose_matrix(offsets, bins, reach):
    out = np.zeros((bins, len(offsets)), np.float32)
    for place, offset in enumerate(offsets):
        out[bucket_number(offset, bins, reach), place] = 1.0
    return out


def split3(x):
    hi = x.astype(jnp.bfloat16)
    rest = x - hi.astype(jnp.float32)
    mid = rest.astype(jnp.bfloat16)
    return hi, mid, (rest - mid.astype(jnp.float32)).astype(jnp.bfloat16)


def split2(x):
    hi = x.astype(jnp.bfloat16)
    return hi, (x - hi.astype(jnp.float32)).astype(jnp.bfloat16)


def exact_dot(a, b, dims):
    return lax.dot_general(a, b, (dims, ((), ())), precision=HIGHEST, preferred_element_type=jnp.float32)


def lanes_of(h, shape):
    lane = lax.broadcasted_iota(jnp.int32, shape, 1)
    return (lane >= h * HEAD_DIM) & (lane < (h + 1) * HEAD_DIM)


def block_rows(m, n):
    return pl.ds(m * BLOCK, n) if isinstance(m, int) else pl.ds(pl.multiple_of(m * BLOCK, BLOCK), n)


def block_window(m):
    start = 512 - m * BLOCK
    return pl.ds(start if isinstance(m, int) else pl.multiple_of(start, 128), WIDE_ROWS)


class CubeSum:
    def __init__(self, ref, rx1, rx2, rx3, rx4, rxb, ssem, rsem, free, bits):
        self.ref, self.rx1, self.rx2, self.rx3, self.rx4, self.rxb = ref, rx1, rx2, rx3, rx4, rxb
        self.ssem, self.rsem, self.free = ssem, rsem, free
        w, n = lax.axis_index("wide"), lax.axis_index("narrow")
        self.bit = [lax.rem(lax.div(w, 2 ** i), 2) for i in range(bits)]
        self.to = [(w + 2 ** i * (1 - 2 * self.bit[i]), n) for i in range(bits)]
        self.rows = ref.shape[0]
        half = self.rows // 2
        self.half, self.stream, self.eighth, self.piece = half, half // 2, half // 4, half // 8
        self.own = self.bit[0] * half
        self.axes = ((1, 2), (2, 1))
        self.extra = range(3, bits)

    def at(self, start, size):
        return pl.ds(pl.multiple_of(start, self.piece), size)

    def base1(self, s, other):
        b = self.bit[self.axes[s][0]]
        b = 1 - b if other else b
        return self.own + s * self.stream + b * self.eighth

    def base2(self, s, other):
        b = self.bit[self.axes[s][1]]
        b = 1 - b if other else b
        return self.base1(s, False) + b * self.piece

    def copy(self, src, dst, i, axis):
        return pltpu.make_async_remote_copy(src, dst, self.ssem.at[i], self.rsem.at[i], device_id=self.to[axis],
                                            device_id_type=MESH)

    def core_out(self):
        return self.copy(self.ref.at[self.at((1 - self.bit[0]) * self.half, self.half)], self.rx1, 0, 0)

    def first(self, s):
        return self.copy(self.ref.at[self.at(self.base1(s, True), self.eighth)], self.rx2[s], 1 + s, self.axes[s][0])

    def second(self, s):
        return self.copy(self.ref.at[self.at(self.base2(s, True), self.piece)], self.rx3[s], 3 + s, self.axes[s][1])

    def back2(self, s):
        r = self.at(self.base2(s, False), self.piece)
        return self.copy(self.ref.at[r], self.rxb[s], 5 + s, self.axes[s][1])

    def back1(self, s):
        r = self.at(self.base1(s, False), self.eighth)
        return self.copy(self.ref.at[r], self.ref.at[r], 7 + s, self.axes[s][0])

    def core_back(self):
        r = self.at(self.own, self.half)
        return self.copy(self.ref.at[r], self.ref.at[r], 9, 0)

    def more(self, e, s):
        i = e - 3
        return self.copy(self.ref.at[self.at(self.base2(s, False), self.piece)], self.rx4.at[i, s], 10 + 2 * i + s, e)

    def release(self, i, axis):
        pl.semaphore_signal(self.free.at[i], inc=1, device_id=self.to[axis], device_id_type=MESH)

    def step(self, i):
        if i == 0:
            self.core_out().start()
        if i == 1:
            self.core_out().wait_recv()
            self.ref[self.at(self.own, self.half), :] += self.rx1[...]
            for s in range(2):
                self.first(s).start()
            self.core_out().wait_send()
            self.release(0, 0)
        if i == 2:
            for s in range(2):
                self.first(s).wait()
                self.release(1 + s, self.axes[s][0])
                self.ref[self.at(self.base1(s, False), self.eighth), :] += self.rx2[s][...]
                self.second(s).start()
        if i == 3:
            for s in range(2):
                self.second(s).wait()
                self.ref[self.at(self.base2(s, False), self.piece), :] += self.rx3[s][...]
            for e in self.extra:
                for s in range(2):
                    self.more(e, s).start()
                for s in range(2):
                    self.more(e, s).wait()
                    self.ref[self.at(self.base2(s, False), self.piece), :] += self.rx4[e - 3, s]
            for s in range(2):
                self.back2(s).start()
        if i == 4:
            for s in range(2):
                self.back2(s).wait_recv()
                self.ref[self.at(self.base2(s, True), self.piece), :] = self.rxb[s][...]
                pl.semaphore_wait(self.free.at[1 + s], 1)
                self.back1(s).start()
        if i == 5:
            for s in range(2):
                self.back1(s).wait_recv()
            pl.semaphore_wait(self.free.at[0], 1)
            self.core_back().start()
        if i == 6:
            self.core_back().wait()
            for s in range(2):
                self.back2(s).wait_send()
                self.back1(s).wait_send()


def layer_kernel(bits, tok_h, cot_h, wq_h, wk_h, wv_h, wo_h, wi_h, wd_h, reg, rank, box, bq, bv, bo_r, g1_r, b1_r, bi_r, bd_r, g2_r, b2_r,
                 to, tx, ty, so, sxy, sgo, sgxy,
                 out, gin, gat, gwi, gwd, sm,
                 part, rx_in, rx_mid, tot, res, cotp, hid, pre, act, gff, hlow, gpre, low, perm,
                 q_s, k_s, v_s, prob, att, ob, obf, pairs, ob4, split_s, base, ga, gt, qt, dkt, dvt, dq, dk, dv, gacc,
                 ws, wo, wi, wd, outp, rows_s, vec_s, rx1, rx2, rx3, rx4, rxb, rxs,
                 s_in, s_mid, r_in, r_mid, cs, cr, cf, ss, sr, ls):
    f32, bf = jnp.float32, jnp.bfloat16
    n = PAGE
    width = wo_h.shape[0]
    heads = to.shape[0]
    block_pieces = BLOCK // PC
    line = LineSum(part, rx_in, rx_mid, tot, s_in, s_mid, r_in, r_mid)
    pieces = line.pieces
    closing = {p: [p - LAG] for p in range(LAG, pieces)}
    closing[pieces - 2] = [pieces - 6, pieces - 5]
    closing[pieces - 1] = [pieces - 4, pieces - 3]
    rest1, rest2, rest3, restb = pre.at[pl.ds(0, 384)], pre.at[pl.ds(384, 192)], cotp.at[pl.ds(0, 96)], cotp.at[pl.ds(96, 96)]
    cube = [CubeSum(gwi, rx1.at[0], [rx2.at[0, s] for s in range(2)], [rx3.at[0, s] for s in range(2)], rx4.at[0],
                    [rxb.at[0, s] for s in range(2)], cs.at[0], cr.at[0], cf.at[0], bits),
            CubeSum(gwd, rx1.at[1], [rx2.at[1, s] for s in range(2)], [rx3.at[1, s] for s in range(2)], rx4.at[1],
                    [rxb.at[1, s] for s in range(2)], cs.at[1], cr.at[1], cf.at[1], bits),
            CubeSum(gat, rest1, [pre.at[pl.ds(384 + 96 * s, 96)] for s in range(2)],
                    [cotp.at[pl.ds(48 * s, 48)] for s in range(2)], rx4.at[2],
                    [cotp.at[pl.ds(96 + 48 * s, 48)] for s in range(2)], cs.at[2], cr.at[2], cf.at[2], bits)]

    def load(i, src, dst):
        return pltpu.make_async_copy(src, dst, ls.at[i])
    loads = [load(0, tok_h, out)]
    loads += [load(1 + i, src, gat.at[pl.ds(i * width, width)]) for i, src in enumerate((wq_h, wk_h, wv_h, wo_h))]
    loads += [load(5, wi_h, gwi), load(6, wd_h, gwd), load(7, cot_h, gin)]
    for c in loads:
        c.start()
    bar = pltpu.get_barrier_semaphore()
    for peer in cube[0].to:
        pl.semaphore_signal(bar, inc=1, device_id=peer, device_id_type=MESH)
    line.signal()

    rows_s[...] = jnp.full(rows_s.shape, 1e4, f32)
    rows_s[0, 0:n] = reg[...].astype(f32)
    rows_s[1, 0:n] = rank[...].astype(f32)
    rows_s[2:4, 0:n] = box[...].astype(f32)
    region_row, rank_row = rows_s[0:1, :], rows_s[1:2, :]
    i0 = lax.broadcasted_iota(jnp.int32, (WIDE_ROWS, WIDE_ROWS), 0)
    i1 = lax.broadcasted_iota(jnp.int32, (WIDE_ROWS, WIDE_ROWS), 1)
    region_col = jnp.sum(jnp.where(i0 == i1, region_row, 0.0), axis=1, keepdims=True)
    place = jnp.sum(jnp.where(region_col < region_row, 1.0, 0.0), axis=0, keepdims=True) + rank_row
    perm[...] = jnp.where(i0.astype(f32) == place, 1.0, 0.0).astype(bf)
    split_s[...] = jnp.zeros_like(split_s)
    for i, vector in enumerate((bo_r, g1_r, b1_r, bi_r, bd_r, g2_r, b2_r)):
        vec_s[i, :] = vector[...]
    vec_s[7:9, :] = jnp.zeros((2, vec_s.shape[1]), f32)
    vec_s[7, 0:width] = bq[...]
    vec_s[8, 0:width] = bv[...]
    b_out, g1, b1, b_in, b_down, g2, b2 = (vec_s[i:i + 1, :] for i in range(7))

    def sort_first(source, target, first):
        split_s[0:n, :] = source[...].astype(bf)
        y = dot_nn(perm[...], split_s[...])
        if first is not None:
            first[...] = y.astype(bf)
        target[...] = y[0:ROWS, :]

    def sort_rest(source, target):
        for i in range(1, 3):
            split_s[0:n, :] = split3(source[...])[i]
            target[...] += dot_nn(perm[0:ROWS, :], split_s[...])

    loads[0].wait()
    sort_first(out, res, low)
    code = lax.broadcasted_iota(jnp.int32, (128, WIDE_ROWS), 0).astype(f32)
    for i in range(2):
        row = rows_s[2 + i:3 + i, :]
        one = dot_nt(perm[...], jnp.where(code == row, 1.0, 0.0).astype(bf)).astype(bf)
        ob[:, 128 * i:128 * (i + 1)] = one
        ob4[:, 256 * i:256 * i + 128] = one
        ob4[:, 256 * i + 128:256 * i + 256] = one
        obf[:, 128 * i:128 * (i + 1)] = dot_nt(perm[...], jnp.where(127.0 - code == row, 1.0, 0.0).astype(bf)).astype(bf)
    ws[...] = jnp.zeros_like(ws)
    for i in range(3):
        loads[1 + i].wait()
        ws[i, 0:width, :] = gat[i * width:(i + 1) * width, :].astype(bf)
    q_s[...] = ((dot_nt(low[...], ws[0]) + vec_s[7:8, 0:256]).astype(bf) * SCORE_SCALE).astype(bf)
    k_s[...] = dot_nt(low[...], ws[1]).astype(bf)
    v_s[...] = (dot_nt(low[...], ws[2]) + vec_s[8:9, 0:256]).astype(bf)
    wo[...] = jnp.zeros_like(wo)
    loads[4].wait()
    wo[0:width, :] = gat[3 * width:4 * width, :].astype(bf)
    row_o = exact_dot(to[...], so[...], ((1,), (0,)))
    row_xy = (exact_dot(tx[...], sxy[...], ((1,), (0,))), exact_dot(ty[...], sxy[...], ((1,), (0,))))
    for h in range(heads):
        base[h] = pltpu.roll(jnp.broadcast_to(row_o[h:h + 1, :], (128, 1280)), 0, 1, stride=1, stride_axis=0)
        for i in range(2):
            table = pltpu.roll(jnp.broadcast_to(row_xy[i][h:h + 1, :], (128, 256)), 0, 1, stride=1, stride_axis=0)
            pairs[h, i] = jnp.concatenate(split2(table[:, 0:128]), axis=1)
    line.ready(bits)

    def blocks(body, start=0):
        full = ROWS // BLOCK

        def step(m, carry):
            body(m, BLOCK)
            return carry
        lax.fori_loop(start, full, step, 0)
        if ROWS % BLOCK:
            body(full, ROWS % BLOCK)

    def sends(m, rows, order):
        for j in range(rows // PC):
            p = m * block_pieces + j
            line.slot(p, order, closing[p] if order == 2 and isinstance(p, int) else None)

    def attend(m, rows):
        r = block_rows(m, rows)
        mixed = None
        for h in range(heads):
            qh = jnp.where(lanes_of(h, (rows, 256)), q_s[r, :], jnp.zeros((), bf))
            bias = jnp.concatenate([dot_nn(ob[r, 128 * i:128 * (i + 1)], pairs[h, i]).astype(bf) for i in range(2)], axis=1)
            s = dot_nt(qh, k_s[...]) + dot_nt(bias, ob4[...]) + base[h, 0:rows, block_window(m)]
            s = jnp.where(lax.broadcasted_iota(jnp.int32, s.shape, 1) < n, s, -1e30)
            e = jnp.exp(s - jnp.max(s, axis=1, keepdims=True))
            p = e / jnp.sum(e, axis=1, keepdims=True)
            prob[h, r, :] = p
            pv = dot_nn(p.astype(bf), v_s[...])
            mixed = pv if h == 0 else jnp.where(lanes_of(h, (rows, 256)), pv, mixed)
        mixed = mixed.astype(bf)
        att[r, :] = mixed
        part[r, :] = dot_nn(mixed, wo[...])
        sends(m, rows, 0)
    blocks(attend)

    sort_rest(out, res)
    loads[5].wait()
    wi[...] = gwi[...].astype(bf)
    loads[6].wait()
    wd[...] = gwd[...].astype(bf)
    sm[...] = jnp.zeros_like(sm)

    def open_block(m, rows):
        for j in range(rows // PC):
            line.want(m * block_pieces + j)
        for j in range(rows // PC):
            line.free_part(m * block_pieces + j)

    def forward(m, rows):
        r = block_rows(m, rows)
        open_block(m, rows)
        one = res[r, :] + (tot[r, :] + b_out)
        res[r, :] = one
        c, _ = centre(one)
        hidden = c * g1 + b1
        hid[r, :] = hidden
        hl = hidden.astype(bf)
        hlow[r, :] = hl
        u = dot_nn(hl, wi[...]) + b_in
        pre[r, :] = u
        a = (u * normal_cdf(u)).astype(bf)
        act[r, :] = a
        part[r, :] = dot_nn(a, wd[...])
        sends(m, rows, 1)
    blocks(forward)

    loads[7].wait()
    sort_first(gin, cotp, None)
    sort_rest(gin, cotp)
    outp[...] = jnp.zeros_like(outp)
    qt[...] = jnp.transpose(q_s[...])
    dkt[...] = jnp.zeros_like(dkt)
    dvt[...] = jnp.zeros_like(dvt)
    base[...] = jnp.zeros_like(base)
    gacc[...] = jnp.zeros_like(gacc)
    ga[...] = jnp.zeros_like(ga)
    dq[...] = jnp.zeros_like(dq)
    gat[3 * width:4 * width, :] = jnp.zeros((width, gat.shape[1]), f32)

    def add_row(i, value):
        sm[i:i + 1, :] += jnp.sum(value, axis=0, keepdims=True)

    def put_back(r, y):
        total = outp[...]
        for piece in split3(y):
            total = total + dot_tn(perm[r, :], piece)
        outp[...] = total

    def back(m, rows):
        r = block_rows(m, rows)
        open_block(m, rows)
        two = hid[r, :] + (tot[r, :] + b_down)
        c, rs = centre(two)
        g = cotp[r, :]
        add_row(0, g * c)
        add_row(1, g)
        gradient = norm_back(g, c, rs, g2)
        hid[r, :] = gradient
        gl = gradient.astype(bf)
        gff[r, :] = gl
        add_row(2, gl.astype(f32))
        slope_in = dot_nt(gl, wd[...])
        u = pre[r, :]
        slope = normal_cdf(u) + u * (jnp.exp(-0.5 * u * u) * (1.0 / math.sqrt(2.0 * math.pi)))
        gp = (slope_in * slope).astype(bf)
        gpre[r, :] = gp
        add_row(3, gp.astype(f32))
        part[r, :] = dot_nt(gp, wi[...])
        sends(m, rows, 2)
        put_back(r, c * g2 + b2)

    def attend_back(m, rows):
        r = block_rows(m, rows)
        for j in range(rows // PC):
            line.want(m * block_pieces + j)
        g = hid[r, :] + tot[r, :]
        c, rs = centre(res[r, :])
        add_row(4, g * c)
        add_row(5, g)
        gradient = norm_back(g, c, rs, g1)
        hid[r, :] = gradient
        gb = gradient.astype(bf)
        add_row(6, gb.astype(f32))
        gat[3 * width:4 * width, :] += dot_tn(att[r, :], gb)[0:width, :]
        gab = dot_nt(gb, wo[...]).astype(bf)
        ga[0:rows, :] = gab
        gt[...] = jnp.transpose(ga[...])
        cols = pl.ds(pl.multiple_of(m * BLOCK, BLOCK), rows)
        query_grad = None
        for h in range(heads):
            gh = jnp.where(lanes_of(h, (rows, 256)), gab, jnp.zeros((), bf))
            dp = dot_nt(gh, v_s[...])
            p = prob[h, r, :]
            inner = jnp.sum(p * dp, axis=1, keepdims=True)
            ds = (p * (dp - inner)).astype(bf)
            dqh = dot_nn(ds, k_s[...])
            query_grad = dqh if h == 0 else jnp.where(lanes_of(h, (rows, 256)), dqh, query_grad)
            base[h, 0:rows, block_window(m)] += ds.astype(f32)
            hr = pl.ds(h * HEAD_DIM, HEAD_DIM)
            dkt[hr, :] += dot_nn(qt[hr, cols], ds)
            dvt[hr, :] += dot_nn(gt[hr, 0:rows], p.astype(bf))
            u = jnp.concatenate(split2(dot_nn(ds, ob[...])), axis=1)
            gg = dot_tn(obf[r, :], u)
            for i in range(2):
                b = 128 * i
                gacc[h, i] += gg[b:b + 128, b:b + 128] + gg[b:b + 128, 256 + b:384 + b]
        dq[r, :] = jnp.where(lax.broadcasted_iota(jnp.int32, (rows, 256), 1) < width, query_grad * SCORE_SCALE, 0.0).astype(bf)

    def back_step(m, carry):
        back(m, BLOCK)

        @pl.when(m == ROWS // BLOCK - 1)
        def _():
            attend_back(0, BLOCK)
        return carry
    lax.fori_loop(0, ROWS // BLOCK, back_step, 0)
    back(ROWS // BLOCK, ROWS % BLOCK)

    gwd[...] = dot_tn(act[...], gff[...])
    cube[1].step(0)
    gwi[...] = dot_tn(hlow[...], gpre[...])
    cube[0].step(0)
    line.last([pieces - 2, pieces - 1])

    def late_step(m, carry):
        attend_back(m, BLOCK)

        @pl.when(m == 1)
        def _():
            cube[1].step(1)

        @pl.when(m == 2)
        def _():
            cube[0].step(1)
        return carry
    lax.fori_loop(1, ROWS // BLOCK, late_step, 0)
    out[...] = outp[0:n, :]
    outp[...] = jnp.zeros_like(outp)
    attend_back(ROWS // BLOCK, ROWS % BLOCK)
    dk[...] = jnp.transpose(dkt[...]).astype(bf)
    dv[...] = jnp.transpose(dvt[...]).astype(bf)

    def produce(m, rows):
        r = block_rows(m, rows)
        for j in range(rows // PC):
            line.free_part(m * block_pieces + j)
        part[r, :] = dot_nn(dq[r, :], ws[0]) + dot_nn(dk[r, :], ws[1]) + dot_nn(dv[r, :], ws[2])
        for j in range(rows // PC):
            line.send_end(m * block_pieces + j)
    blocks(produce)

    def table_sums(h):
        for i in range(2):
            both = jnp.concatenate([gacc[h, i], jnp.zeros((128, 128), f32)], axis=1)
            line_sum = jnp.sum(pltpu.roll(both, 0, 1, stride=1, stride_axis=0), axis=0, keepdims=True)
            sm[10 + heads * (i + 1) + h:11 + heads * (i + 1) + h, 0:BINS2] = exact_dot(line_sum, sgxy[...], ((1,), (1,)))
        flip = (lax.broadcasted_iota(jnp.int32, (128, 128), 0) + lax.broadcasted_iota(jnp.int32, (128, 128), 1)) == 127
        flip = jnp.where(flip, 1.0, 0.0).astype(bf)
        hi, lo = split2(base[h])
        turned = dot_nn(flip, hi) + dot_nn(flip, lo)
        line_sum = jnp.sum(pltpu.roll(turned, 0, 1, stride=1, stride_axis=0), axis=0, keepdims=True)
        sm[10 + h:11 + h, 0:BINS1] = exact_dot(line_sum, sgo[...], ((1,), (1,)))

    def bias_sums(_):
        sm[8:9, 0:256] = jnp.sum(dq[...].astype(f32), axis=0, keepdims=True)
        sm[9:10, 0:256] = jnp.sum(dv[...].astype(f32), axis=0, keepdims=True)

    bit_to = cube[0].to

    def small_copy(i):
        return pltpu.make_async_remote_copy(sm, rxs.at[i], ss.at[i], sr.at[i], device_id=bit_to[i], device_id_type=MESH)

    def small_step(i):
        if i > 0:
            small_copy(i - 1).wait()
            sm[...] += rxs[i - 1]
        if i < bits:
            small_copy(i).start()

    def weight_grad(i):
        gat[i * width:(i + 1) * width, :] = dot_tn((dq, dk, dv)[i][...], low[...])[0:width, :]

    def consume(m):
        rows = min(BLOCK, ROWS - m * BLOCK)
        for j in range(rows // PC):
            line.want(m * block_pieces + j)
        r = slice(m * BLOCK, m * BLOCK + rows)
        put_back(r, hid[r, :] + tot[r, :])

    def both_step(i):
        cube[1].step(i)
        cube[0].step(i)
    jobs = {0: [(both_step, 2)], 1: [(cube[2].step, 1)], 2: [(bias_sums, 0), (table_sums, 0)], 3: [(table_sums, 1)],
            4: [(table_sums, 2), (small_step, 0)], 6: [(both_step, 3), (small_step, 1)], 7: [(cube[2].step, 2)], 8: [(small_step, 2)],
            9: [(consume, 0)], 10: [(small_step, 3)], 11: [(both_step, 4), (cube[2].step, 3)], 13: [(consume, 1)],
            14: [(cube[2].step, 4)]}
    for i in range(3):
        weight_grad(i)
    cube[2].step(0)
    ending = {p: [p - LAG] for p in range(LAG, pieces - 4)}
    ending.update({pieces - 4: [pieces - 8, pieces - 7], pieces - 3: [pieces - 6], pieces - 2: [pieces - 5, pieces - 4],
                   pieces - 1: [pieces - 3, pieces - 2]})
    for p in range(pieces):
        line.slot_mid(p, ending.get(p, ()))
        for job, arg in jobs.get(p, ()):
            job(arg)
    line.last([pieces - 1])
    for i in range(4, bits + 1):
        small_step(i)
    consume(2)
    both_step(5)
    cube[2].step(5)
    consume(3)
    consume(4)
    both_step(6)
    cube[2].step(6)
    gin[...] = outp[0:n, :]
    line.drain()


def layer(bits, tok, cot, wq, wk, wv, wo, wi, wd, *small_args):
    f32, bf = jnp.float32, jnp.bfloat16
    d = tok.shape[1]
    f = wi.shape[1]
    width = wo.shape[0]
    heads = small_args[12].shape[0]
    sd = jax.ShapeDtypeStruct
    W, R = WIDE_ROWS, ROWS
    pieces = R // PC
    more = max(bits - 3, 1)
    vm, hbm = pl.BlockSpec(memory_space=pltpu.VMEM), pl.BlockSpec(memory_space=pl.ANY)
    v_ = pltpu.VMEM
    shapes = (v_((PAGE, d), f32), v_((PAGE, d), f32), v_((4 * width, d), f32), v_((d, f), f32), v_((f, d), f32), v_((24, d), f32))
    scratch = [v_((R, d), f32)] * 7 + [v_((R, f), f32), v_((R, f), bf), v_((R, d), bf), v_((R, d), bf), v_((R, f), bf)]
    scratch += [v_((W, d), bf), v_((W, W), bf)] + [v_((W, 256), bf)] * 3 + [v_((heads, R, W), f32)] + [v_((W, 256), bf)] * 3
    scratch += [v_((heads, 2, 128, 256), bf), v_((W, 512), bf), v_((W, d), bf), v_((heads, 128, 1280), f32)]
    scratch += [v_((BLOCK, 256), bf), v_((256, BLOCK), bf), v_((256, W), bf), v_((256, W), f32), v_((256, W), f32)]
    scratch += [v_((W, 256), bf)] * 3 + [v_((heads, 2, 128, 128), f32)]
    scratch += [v_((3, 256, d), bf), v_((256, d), bf), v_((d, f), bf), v_((f, d), bf), v_((W, d), f32), v_((8, W), f32), v_((16, d), f32)]
    scratch += [v_((2, d // 2, d), f32), v_((2, 2, d // 8, d), f32), v_((2, 2, d // 16, d), f32), v_((3, more, 2, d // 16, d), f32),
                v_((2, 2, d // 16, d), f32), v_((bits, 24, d), f32)]
    scratch += [pltpu.SemaphoreType.DMA((pieces,))] * 4 + [pltpu.SemaphoreType.DMA((3, 10 + 2 * more))] * 2
    scratch += [pltpu.SemaphoreType.REGULAR((3, 3))] + [pltpu.SemaphoreType.DMA((bits,))] * 2 + [pltpu.SemaphoreType.DMA((8,))]
    return pl.pallas_call(
        functools.partial(layer_kernel, bits), out_shape=shapes, in_specs=[hbm] * 8 + [vm] * 19, out_specs=[vm] * 6,
        scratch_shapes=scratch,
        compiler_params=pltpu.CompilerParams(collective_id=0, has_side_effects=True, vmem_limit_bytes=52 << 20),
        cost_estimate=pl.CostEstimate(flops=3 * 10 ** 10, bytes_accessed=20 << 20, transcendentals=heads * R * W),
    )(tok, cot, wq, wk, wv, wo, wi, wd, *small_args)


def finish_kernel(out_in, gin_in, gat_in, gwi_in, gwd_in, sm, out, gin, gwq, gwk, gwv, gwo, gwi, gwd, *rest):
    vectors, sem = rest[:12], rest[12]
    width = gwo.shape[0]
    heads = vectors[9].shape[0]
    pairs = [(out_in, out), (gin_in, gin), (gwi_in, gwi), (gwd_in, gwd)]
    pairs += [(gat_in.at[pl.ds(i * width, width)], g) for i, g in enumerate((gwq, gwk, gwv, gwo))]
    copies = [pltpu.make_async_copy(a, b, sem.at[i]) for i, (a, b) in enumerate(pairs)]
    for c in copies:
        c.start()
    for i in range(7):
        vectors[i][...] = sm[i, :]
    vectors[7][...] = sm[8, 0:width]
    vectors[8][...] = sm[9, 0:width]
    vectors[9][...] = sm[10:10 + heads, 0:BINS1]
    vectors[10][...] = sm[10 + heads:10 + 2 * heads, 0:BINS2]
    vectors[11][...] = sm[10 + 2 * heads:10 + 3 * heads, 0:BINS2]
    for c in copies:
        c.wait()


def finish(heads, width, out, gin, gat, gwi, gwd, sm):
    f32 = jnp.float32
    sd = jax.ShapeDtypeStruct
    d = gat.shape[1]
    like = lambda x: sd(x.shape, f32)
    shapes = (like(out), like(gin)) + (sd((width, d), f32),) * 4 + (like(gwi), like(gwd)) + (sd((d,), f32),) * 7 \
        + (sd((width,), f32),) * 2 + (sd((heads, BINS1), f32), sd((heads, BINS2), f32), sd((heads, BINS2), f32))
    vm, hbm = pl.BlockSpec(memory_space=pltpu.VMEM), pl.BlockSpec(memory_space=pl.ANY)
    return pl.pallas_call(
        finish_kernel, out_shape=shapes, in_specs=[vm] * 6, out_specs=[hbm] * 8 + [vm] * 12,
        scratch_shapes=[pltpu.SemaphoreType.DMA((8,))],
        compiler_params=pltpu.CompilerParams(vmem_limit_bytes=4 << 20),
    )(*(pltpu.with_memory_space_constraint(x, pltpu.VMEM) for x in (out, gin, gat, gwi, gwd, sm)))


def local(
    bits,
    tokens,
    region,
    order_rank,
    box_coords,
    w_query,
    b_query,
    w_key,
    w_value,
    b_value,
    w_out,
    b_out,
    ln1_gain,
    ln1_bias,
    w_in,
    b_in,
    w_down,
    b_down,
    ln2_gain,
    ln2_bias,
    rel_order,
    rel_x,
    rel_y,
    cotangent,
):
    so = choose_matrix([i - 512 if i < 1152 else i - 1792 for i in range(1280)], BINS1, MAX_ORDER)
    sxy = choose_matrix([i if i < 128 else i - 256 for i in range(256)], BINS2, MAX_LAYOUT)
    sgo = choose_matrix([i - 639 for i in range(1280)], BINS1, MAX_ORDER)
    sgxy = choose_matrix([i - 127 for i in range(256)], BINS2, MAX_LAYOUT)
    width = w_out.shape[0]
    heads = rel_order.shape[0]
    output, gin, gat, gwi, gwd, sm = layer(
        bits, tokens, cotangent, w_query.T, w_key.T, w_value.T, w_out, w_in, w_down, region, order_rank, box_coords, b_query, b_value,
        b_out, ln1_gain, ln1_bias, b_in, b_down, ln2_gain, ln2_bias, rel_order, rel_x, rel_y, so, sxy, sgo, sgxy)
    (output, gin, gwq, gwk, gwv, gwo, gwi, gwd, l2g, l2b, bd, bi, l1g, l1b, bo, gbq, gbv, ro, rx, ry) = finish(
        heads, width, output, gin, gat, gwi, gwd, sm)
    return (output, gin, gwq.T, gbq, gwk.T, gwv.T, gbv, gwo, bo, l1g, l1b, gwi, bi,
            gwd, bd, l2g, l2b, ro, rx, ry)


def solution(mesh):
    in_specs = (
        P("wide", None),
        P("wide"),
        P("wide"),
        P(None, "wide"),
        P(None, "narrow"),
        P("narrow"),
        P(None, "narrow"),
        P(None, "narrow"),
        P("narrow"),
        P("narrow", None),
        P(),
        P(),
        P(),
        P(None, "narrow"),
        P("narrow"),
        P("narrow", None),
        P(),
        P(),
        P(),
        P("narrow", None),
        P("narrow", None),
        P("narrow", None),
        P("wide", None),
    )
    out_specs = (
        P("wide", None),
        P("wide", None),
        P(None, "narrow"),
        P("narrow"),
        P(None, "narrow"),
        P(None, "narrow"),
        P("narrow"),
        P("narrow", None),
        P(),
        P(),
        P(),
        P(None, "narrow"),
        P("narrow"),
        P("narrow", None),
        P(),
        P(),
        P(),
        P("narrow", None),
        P("narrow", None),
        P("narrow", None),
    )
    bits = mesh.shape["wide"].bit_length() - 1
    return jax.shard_map(functools.partial(local, bits), mesh=mesh, in_specs=in_specs, out_specs=out_specs, check_vma=False)
```

```python
import functools
import math

import jax
import jax.numpy as jnp
import numpy as np
from jax import lax
from jax.experimental import pallas as pl
from jax.experimental.pallas import tpu as pltpu
from jax.sharding import PartitionSpec as P

HEAD_DIM = 64
BINS1 = 32
BINS2 = 64
MAX_ORDER = 128
MAX_LAYOUT = 256
PAGE = 561


HIGHEST = lax.Precision.HIGHEST
EPSILON = 1e-05
SCORE_SCALE = 0.125

def bucket_steps(bins, reach):
    halfway = bins // 2
    exact = halfway // 2
    steps = []
    for level in range(1, halfway):
        if level < exact:
            steps.append(level)
        else:
            found = reach + 1
            for count in range(exact, reach + 2):
                value = exact + int(
                    math.log(count / exact) / math.log(reach / exact) * (halfway - exact)
                )
                if min(value, halfway - 1) >= level:
                    found = count
                    break
            steps.append(found)
    return steps


MESH = pl.DeviceIdType.MESH
BLOCK = 128
PC = 32
END_PC = 32
SENT = -(-PAGE // 8) * 8
LAG = 4


def erf_of(x):
    x = jnp.clip(x, -3.832506856900711, 3.832506856900711)
    s = x * x
    top = -2.72614225801306e-10
    for term in (2.77068142495902e-08, -2.10102402082508e-06, -5.69250639462346e-05,
                 -7.34990630326855e-04, -2.95459980854025e-03, -1.60960333262415e-02):
        top = top * s + term
    low = -1.45660718464996e-05
    for term in (-2.13374055278905e-04, -1.68282697438203e-03, -7.37332916720468e-03,
                 -1.42647390514189e-02):
        low = low * s + term
    return x * top / low


def normal_cdf(x):
    return 0.5 + 0.5 * erf_of(x * math.sqrt(0.5))


def centre(values):
    c = values - jnp.mean(values, axis=-1, keepdims=True)
    r = lax.rsqrt(jnp.mean(c * c, axis=-1, keepdims=True) + EPSILON)
    return c * r, r


def norm_back(g, n, r, gain):
    m = g * gain
    return r * (m - jnp.mean(m, axis=-1, keepdims=True) - n * jnp.mean(m * n, axis=-1, keepdims=True))


def dot_nn(a, b):
    return lax.dot_general(a, b, (((1,), (0,)), ((), ())), preferred_element_type=jnp.float32)


def dot_nt(a, b):
    return lax.dot_general(a, b, (((1,), (1,)), ((), ())), preferred_element_type=jnp.float32)


def dot_tn(a, b):
    return lax.dot_general(a, b, (((0,), (0,)), ((), ())), preferred_element_type=jnp.float32)


class LineSum:
    def __init__(self, part, rx_in, rx_mid, tot, s_in, s_mid, r_in, r_mid):
        self.part, self.rx_in, self.rx_mid, self.tot = part, rx_in, rx_mid, tot
        self.s_in, self.s_mid, self.r_in, self.r_mid = s_in, s_mid, r_in, r_mid
        w, n = lax.axis_index("wide"), lax.axis_index("narrow")
        self.end = (n == 0) | (n == 3)
        self.mid = jnp.logical_not(self.end)
        self.side = (w, n + 1 - 2 * lax.rem(n, 2))
        self.across = (w, 3 - n)
        self.body = part.shape[0] // BLOCK * BLOCK // PC
        self.pieces = self.body + part.shape[0] % BLOCK // END_PC

    def rows(self, p):
        if not isinstance(p, int):
            return pl.ds(pl.multiple_of(p * PC, PC), PC)
        if p < self.body:
            return pl.ds(p * PC, PC)
        start = self.body * PC + (p - self.body) * END_PC
        return pl.ds(start, min(END_PC, SENT - start))

    def copy_a(self, p):
        return pltpu.make_async_remote_copy(self.part.at[self.rows(p)], self.rx_in.at[self.rows(p)],
            self.s_in.at[p], self.r_in.at[p], device_id=self.side, device_id_type=MESH)

    def copy_b(self, p):
        return pltpu.make_async_remote_copy(self.part.at[self.rows(p)], self.rx_mid.at[self.rows(p)],
            self.s_mid.at[p], self.r_mid.at[p], device_id=self.across, device_id_type=MESH)

    def copy_t(self, p):
        return pltpu.make_async_remote_copy(self.tot.at[self.rows(p)], self.tot.at[self.rows(p)],
            self.s_in.at[p], self.r_in.at[p], device_id=self.side, device_id_type=MESH)

    def signal(self):
        bar = pltpu.get_barrier_semaphore()
        pl.semaphore_signal(bar, inc=1, device_id=self.side, device_id_type=MESH)

        @pl.when(self.mid)
        def _():
            pl.semaphore_signal(bar, inc=1, device_id=self.across, device_id_type=MESH)

    def ready(self, others):
        bar = pltpu.get_barrier_semaphore()

        @pl.when(self.end)
        def _():
            pl.semaphore_wait(bar, 1 + others)

        @pl.when(self.mid)
        def _():
            pl.semaphore_wait(bar, 2 + others)

    def free_part(self, p):
        @pl.when(self.end)
        def _():
            self.copy_a(p).wait_send()

        @pl.when(self.mid)
        def _():
            self.copy_b(p).wait_send()

    def finish(self, p, first):
        self.copy_b(p).wait_recv()
        if not first:
            self.copy_t(p).wait_send()
        self.tot[self.rows(p), :] = self.part[self.rows(p), :] + self.rx_mid[self.rows(p), :]
        self.copy_t(p).start()

    def slot(self, p, order, done=None):
        @pl.when(self.end)
        def _():
            self.copy_a(p).start()

        @pl.when(self.mid)
        def _():
            self.copy_a(p).wait_recv()
            self.part[self.rows(p), :] += self.rx_in[self.rows(p), :]
            self.copy_b(p).start()

            if done is not None:
                for q in done:
                    self.finish(q, order == 0)
                return

            if isinstance(p, int):
                self.finish(p - LAG, order == 0)
                return

            @pl.when(p >= LAG)
            def _():
                self.finish(p - LAG, order == 0)

            if order > 0:
                for i in range(LAG):
                    @pl.when(p == i)
                    def _(i=i):
                        self.finish(i + self.pieces - LAG, order == 1)

    def send_end(self, p):
        @pl.when(self.end)
        def _():
            self.copy_a(p).start()

    def slot_mid(self, p, done):
        @pl.when(self.mid)
        def _():
            self.copy_a(p).wait_recv()
            self.part[self.rows(p), :] += self.rx_in[self.rows(p), :]
            self.copy_b(p).start()
            for q in done:
                self.finish(q, False)

    def last(self, pieces):
        @pl.when(self.mid)
        def _():
            for q in pieces:
                self.finish(q, False)

    def want(self, p):
        @pl.when(self.end)
        def _():
            self.copy_t(p).wait_recv()

    def drain(self):
        def one(p, c):
            self.free_part(p)

            @pl.when(self.mid)
            def _():
                self.copy_t(p).wait_send()
            return c
        lax.fori_loop(0, self.body, one, 0)
        for p in range(self.body, self.pieces):
            one(p, 0)


WIDE_ROWS = 640
ROWS = 576


def bucket_number(offset, bins, reach):
    halfway = bins // 2
    steps = bucket_steps(bins, reach)
    return (halfway if offset > 0 else 0) + sum(1 for s in steps if abs(offset) >= s)


def choose_matrix(offsets, bins, reach):
    out = np.zeros((bins, len(offsets)), np.float32)
    for place, offset in enumerate(offsets):
        out[bucket_number(offset, bins, reach), place] = 1.0
    return out


def split3(x):
    hi = x.astype(jnp.bfloat16)
    rest = x - hi.astype(jnp.float32)
    mid = rest.astype(jnp.bfloat16)
    return hi, mid, (rest - mid.astype(jnp.float32)).astype(jnp.bfloat16)


def split2(x):
    hi = x.astype(jnp.bfloat16)
    return hi, (x - hi.astype(jnp.float32)).astype(jnp.bfloat16)


def exact_dot(a, b, dims):
    return lax.dot_general(a, b, (dims, ((), ())), precision=HIGHEST, preferred_element_type=jnp.float32)


def lanes_of(h, shape):
    lane = lax.broadcasted_iota(jnp.int32, shape, 1)
    return (lane >= h * HEAD_DIM) & (lane < (h + 1) * HEAD_DIM)


def block_rows(m, n):
    return pl.ds(m * BLOCK, n) if isinstance(m, int) else pl.ds(pl.multiple_of(m * BLOCK, BLOCK), n)


def block_window(m):
    start = 512 - m * BLOCK
    return pl.ds(start if isinstance(m, int) else pl.multiple_of(start, 128), WIDE_ROWS)


class CubeSum:
    def __init__(self, ref, rx1, rx2, rx3, rxb, ssem, rsem, free, bits):
        self.ref, self.rx1, self.rx2, self.rx3, self.rxb = ref, rx1, rx2, rx3, rxb
        self.ssem, self.rsem, self.free = ssem, rsem, free
        w, n = lax.axis_index("wide"), lax.axis_index("narrow")
        self.bit = [lax.rem(lax.div(w, 2 ** i), 2) for i in range(bits)]
        self.to = [(w + 2 ** i * (1 - 2 * self.bit[i]), n) for i in range(bits)]
        self.rows = ref.shape[0]
        half = self.rows // 2
        self.half, self.stream, self.eighth, self.piece = half, half // 2, half // 4, half // 8
        self.own = self.bit[0] * half
        self.axes = ((1, 2), (2, 1))
        self.extra = range(3, bits)

    def at(self, start, size):
        return pl.ds(pl.multiple_of(start, self.piece), size)

    def base1(self, s, other):
        b = self.bit[self.axes[s][0]]
        b = 1 - b if other else b
        return self.own + s * self.stream + b * self.eighth

    def base2(self, s, other):
        b = self.bit[self.axes[s][1]]
        b = 1 - b if other else b
        return self.base1(s, False) + b * self.piece

    def copy(self, src, dst, i, axis):
        return pltpu.make_async_remote_copy(src, dst, self.ssem.at[i], self.rsem.at[i], device_id=self.to[axis],
                                            device_id_type=MESH)

    def core_out(self):
        return self.copy(self.ref.at[self.at((1 - self.bit[0]) * self.half, self.half)], self.rx1, 0, 0)

    def first(self, s):
        return self.copy(self.ref.at[self.at(self.base1(s, True), self.eighth)], self.rx2[s], 1 + s, self.axes[s][0])

    def second(self, s):
        return self.copy(self.ref.at[self.at(self.base2(s, True), self.piece)], self.rx3[s], 3 + s, self.axes[s][1])

    def back2(self, s):
        r = self.at(self.base2(s, False), self.piece)
        return self.copy(self.ref.at[r], self.rxb[s], 5 + s, self.axes[s][1])

    def back1(self, s):
        r = self.at(self.base1(s, False), self.eighth)
        return self.copy(self.ref.at[r], self.ref.at[r], 7 + s, self.axes[s][0])

    def core_back(self):
        r = self.at(self.own, self.half)
        return self.copy(self.ref.at[r], self.ref.at[r], 9, 0)

    def spare(self, e, s):
        return pl.ds((2 * (e - 3) + s) * self.piece, self.piece)

    def more(self, e, s):
        return self.copy(self.ref.at[self.at(self.base2(s, False), self.piece)], self.rx1.at[self.spare(e, s)],
                         10 + 2 * (e - 3) + s, e)

    def release(self, i, axis):
        pl.semaphore_signal(self.free.at[i], inc=1, device_id=self.to[axis], device_id_type=MESH)

    def step(self, i):
        if i == 0:
            self.core_out().start()
        if i == 1:
            self.core_out().wait_recv()
            self.ref[self.at(self.own, self.half), :] += self.rx1[...]
            for s in range(2):
                self.first(s).start()
            self.core_out().wait_send()
            self.release(0, 0)
            for e in self.extra:
                self.release(e, e)
        if i == 2:
            for s in range(2):
                self.first(s).wait()
                self.release(1 + s, self.axes[s][0])
                self.ref[self.at(self.base1(s, False), self.eighth), :] += self.rx2[s][...]
                self.second(s).start()
        if i == 3:
            for s in range(2):
                self.second(s).wait()
                self.ref[self.at(self.base2(s, False), self.piece), :] += self.rx3[s][...]
            for e in self.extra:
                pl.semaphore_wait(self.free.at[e], 1)
                for s in range(2):
                    self.more(e, s).start()
                for s in range(2):
                    self.more(e, s).wait()
                    self.ref[self.at(self.base2(s, False), self.piece), :] += self.rx1[self.spare(e, s), :]
            for s in range(2):
                self.back2(s).start()
        if i == 4:
            for s in range(2):
                self.back2(s).wait_recv()
                self.ref[self.at(self.base2(s, True), self.piece), :] = self.rxb[s][...]
                pl.semaphore_wait(self.free.at[1 + s], 1)
                self.back1(s).start()
        if i == 5:
            for s in range(2):
                self.back1(s).wait_recv()
            pl.semaphore_wait(self.free.at[0], 1)
            self.core_back().start()
        if i == 6:
            self.core_back().wait()
            for s in range(2):
                self.back2(s).wait_send()
                self.back1(s).wait_send()


def layer_kernel(bits, tok_h, cot_h, wq_h, wk_h, wv_h, wo_h, wi_h, wd_h, reg, rank, box, bq, bv, bo_r, g1_r, b1_r, bi_r, bd_r, g2_r, b2_r,
                 to, tx, ty, so, sxy, sgo, sgxy,
                 out, gin, gat, gwi, gwd, sm,
                 part, rx_in, rx_mid, tot, res, cotp, hid, pre, act, gff, hlow, gpre, low, perm,
                 q_s, k_s, v_s, prob, att, ob, obf, pairs, ob4, split_s, base, ga, gt, qt, dkt, dvt, dq, dk, dv, gacc,
                 ws, wo, wi, wd, outp, rows_s, vec_s, rx1, rx2, rx3, rxb, rxs,
                 s_in, s_mid, r_in, r_mid, cs, cr, cf, ss, sr, ls):
    f32, bf = jnp.float32, jnp.bfloat16
    n = PAGE
    width = wo_h.shape[0]
    heads = to.shape[0]
    block_pieces = BLOCK // PC
    tail_pieces = ROWS % BLOCK // END_PC

    def pieces_of(m, rows):
        return [m * block_pieces + j for j in range(block_pieces if rows == BLOCK else tail_pieces)]
    line = LineSum(part, rx_in, rx_mid, tot, s_in, s_mid, r_in, r_mid)
    pieces = line.pieces
    closing = {pieces - 2: [pieces - 6, pieces - 5], pieces - 1: [pieces - 4, pieces - 3]}
    rest1, rest2, rest3, restb = pre.at[pl.ds(0, 384)], pre.at[pl.ds(384, 192)], cotp.at[pl.ds(0, 96)], cotp.at[pl.ds(96, 96)]
    cube = [CubeSum(gwi, rx1.at[0], [rx2.at[0, s] for s in range(2)], [rx3.at[0, s] for s in range(2)],
                    [rxb.at[0, s] for s in range(2)], cs.at[0], cr.at[0], cf.at[0], bits),
            CubeSum(gwd, rx1.at[1], [rx2.at[1, s] for s in range(2)], [rx3.at[1, s] for s in range(2)],
                    [rxb.at[1, s] for s in range(2)], cs.at[1], cr.at[1], cf.at[1], bits),
            CubeSum(gat, rest1, [pre.at[pl.ds(384 + 96 * s, 96)] for s in range(2)],
                    [cotp.at[pl.ds(48 * s, 48)] for s in range(2)],
                    [cotp.at[pl.ds(96 + 48 * s, 48)] for s in range(2)], cs.at[2], cr.at[2], cf.at[2], bits)]

    def load(i, src, dst):
        return pltpu.make_async_copy(src, dst, ls.at[i])
    loads = [load(0, tok_h, out)]
    loads += [load(1 + i, src, gat.at[pl.ds(i * width, width)]) for i, src in enumerate((wq_h, wk_h, wv_h, wo_h))]
    loads += [load(5, wi_h, gwi), load(6, wd_h, gwd), load(7, cot_h, gin)]
    for c in loads:
        c.start()
    bar = pltpu.get_barrier_semaphore()
    for peer in cube[0].to:
        pl.semaphore_signal(bar, inc=1, device_id=peer, device_id_type=MESH)
    line.signal()
    tot[SENT:ROWS, :] = jnp.zeros((ROWS - SENT, tot.shape[1]), f32)

    rows_s[...] = jnp.full(rows_s.shape, 1e4, f32)
    rows_s[0, 0:n] = reg[...].astype(f32)
    rows_s[1, 0:n] = rank[...].astype(f32)
    rows_s[2:4, 0:n] = box[...].astype(f32)
    region_row, rank_row = rows_s[0:1, :], rows_s[1:2, :]
    i0 = lax.broadcasted_iota(jnp.int32, (WIDE_ROWS, WIDE_ROWS), 0)
    i1 = lax.broadcasted_iota(jnp.int32, (WIDE_ROWS, WIDE_ROWS), 1)
    region_col = jnp.sum(jnp.where(i0 == i1, region_row, 0.0), axis=1, keepdims=True)
    place = jnp.sum(jnp.where(region_col < region_row, 1.0, 0.0), axis=0, keepdims=True) + rank_row
    perm[...] = jnp.where(i0.astype(f32) == place, 1.0, 0.0).astype(bf)
    split_s[...] = jnp.zeros_like(split_s)
    for i, vector in enumerate((bo_r, g1_r, b1_r, bi_r, bd_r, g2_r, b2_r)):
        vec_s[i, :] = vector[...]
    vec_s[7:9, :] = jnp.zeros((2, vec_s.shape[1]), f32)
    vec_s[7, 0:width] = bq[...]
    vec_s[8, 0:width] = bv[...]
    b_out, g1, b1, b_in, b_down, g2, b2 = (vec_s[i:i + 1, :] for i in range(7))

    def sort_first(source, target, first):
        split_s[0:n, :] = source[...].astype(bf)
        y = dot_nn(perm[...], split_s[...])
        if first is not None:
            first[...] = y.astype(bf)
        target[...] = y[0:ROWS, :]

    def sort_rest(source, target):
        for i in range(1, 3):
            split_s[0:n, :] = split3(source[...])[i]
            target[...] += dot_nn(perm[0:ROWS, :], split_s[...])

    loads[0].wait()
    sort_first(out, res, low)
    code = lax.broadcasted_iota(jnp.int32, (128, WIDE_ROWS), 0).astype(f32)
    for i in range(2):
        row = rows_s[2 + i:3 + i, :]
        one = dot_nt(perm[...], jnp.where(code == row, 1.0, 0.0).astype(bf)).astype(bf)
        ob[:, 128 * i:128 * (i + 1)] = one
        ob4[:, 256 * i:256 * i + 128] = one
        ob4[:, 256 * i + 128:256 * i + 256] = one
    ws[...] = jnp.zeros_like(ws)
    for i in range(3):
        loads[1 + i].wait()
        ws[i, 0:width, :] = gat[i * width:(i + 1) * width, :].astype(bf)
    q_s[...] = ((dot_nt(low[...], ws[0]) + vec_s[7:8, 0:256]).astype(bf) * SCORE_SCALE).astype(bf)
    k_s[...] = dot_nt(low[...], ws[1]).astype(bf)
    v_s[...] = (dot_nt(low[...], ws[2]) + vec_s[8:9, 0:256]).astype(bf)
    wo[...] = jnp.zeros_like(wo)
    loads[4].wait()
    wo[0:width, :] = gat[3 * width:4 * width, :].astype(bf)
    row_o = exact_dot(to[...], so[...], ((1,), (0,)))
    row_xy = (exact_dot(tx[...], sxy[...], ((1,), (0,))), exact_dot(ty[...], sxy[...], ((1,), (0,))))
    for h in range(heads):
        base[h] = pltpu.roll(jnp.broadcast_to(row_o[h:h + 1, :], (128, 1280)), 0, 1, stride=1, stride_axis=0)
        for i in range(2):
            table = pltpu.roll(jnp.broadcast_to(row_xy[i][h:h + 1, :], (128, 256)), 0, 1, stride=1, stride_axis=0)
            pairs[h, i] = jnp.concatenate(split2(table[:, 0:128]), axis=1)
    line.ready(bits)

    def blocks(body, start=0):
        full = ROWS // BLOCK

        def step(m, carry):
            body(m, BLOCK)
            return carry
        lax.fori_loop(start, full, step, 0)
        if ROWS % BLOCK:
            body(full, ROWS % BLOCK)

    def sends(m, rows, order):
        for p in pieces_of(m, rows):
            line.slot(p, order, closing[p] if order == 2 and isinstance(p, int) else None)

    def attend(m, rows):
        r = block_rows(m, rows)
        mixed = None
        for h in range(heads):
            qh = jnp.where(lanes_of(h, (rows, 256)), q_s[r, :], jnp.zeros((), bf))
            bias = jnp.concatenate([dot_nn(ob[r, 128 * i:128 * (i + 1)], pairs[h, i]).astype(bf) for i in range(2)], axis=1)
            s = dot_nt(qh, k_s[...]) + dot_nt(bias, ob4[...]) + base[h, 0:rows, block_window(m)]
            s = jnp.where(lax.broadcasted_iota(jnp.int32, s.shape, 1) < n, s, -1e30)
            e = jnp.exp(s - jnp.max(s, axis=1, keepdims=True))
            p = e / jnp.sum(e, axis=1, keepdims=True)
            prob[h, r, :] = p
            pv = dot_nn(p.astype(bf), v_s[...])
            mixed = pv if h == 0 else jnp.where(lanes_of(h, (rows, 256)), pv, mixed)
        mixed = mixed.astype(bf)
        att[r, :] = mixed
        part[r, :] = dot_nn(mixed, wo[...])
        sends(m, rows, 0)
        if rows == BLOCK:
            pl.when(m == 1)(early_one)
            pl.when(m == 2)(early_two)

    def early_one():
        sort_rest(out, res)

    def early_two():
        loads[5].wait()
        wi[...] = gwi[...].astype(bf)
        loads[6].wait()
        wd[...] = gwd[...].astype(bf)
        sm[...] = jnp.zeros_like(sm)
    blocks(attend)

    def open_block(m, rows):
        for p in pieces_of(m, rows):
            line.want(p)
        for p in pieces_of(m, rows):
            line.free_part(p)

    def forward(m, rows):
        r = block_rows(m, rows)
        open_block(m, rows)
        one = res[r, :] + (tot[r, :] + b_out)
        res[r, :] = one
        c, _ = centre(one)
        hidden = c * g1 + b1
        hid[r, :] = hidden
        hl = hidden.astype(bf)
        hlow[r, :] = hl
        u = dot_nn(hl, wi[...]) + b_in
        pre[r, :] = u
        a = (u * normal_cdf(u)).astype(bf)
        act[r, :] = a
        part[r, :] = dot_nn(a, wd[...])
        sends(m, rows, 1)
        if rows == BLOCK:
            pl.when(m == 0)(late_one)
            pl.when(m == 1)(late_two)
            pl.when(m == 2)(late_three)

    def late_one():
        loads[7].wait()
        sort_first(gin, cotp, None)

    def late_two():
        sort_rest(gin, cotp)

    def late_three():
        for i in range(2):
            row = rows_s[2 + i:3 + i, :]
            obf[:, 128 * i:128 * (i + 1)] = dot_nt(perm[...], jnp.where(127.0 - code == row, 1.0, 0.0).astype(bf)).astype(bf)
        outp[...] = jnp.zeros_like(outp)
        qt[...] = jnp.transpose(q_s[...])
        dkt[...] = jnp.zeros_like(dkt)
        dvt[...] = jnp.zeros_like(dvt)
        base[...] = jnp.zeros_like(base)
        gacc[...] = jnp.zeros_like(gacc)
        ga[...] = jnp.zeros_like(ga)
        dq[...] = jnp.zeros_like(dq)
        gat[3 * width:4 * width, :] = jnp.zeros((width, gat.shape[1]), f32)
    blocks(forward)

    def add_row(i, value):
        sm[i:i + 1, :] += jnp.sum(value, axis=0, keepdims=True)

    def put_back(r, y):
        total = outp[...]
        for piece in split3(y):
            total = total + dot_tn(perm[r, :], piece)
        outp[...] = total

    def back(m, rows):
        r = block_rows(m, rows)
        open_block(m, rows)
        two = hid[r, :] + (tot[r, :] + b_down)
        c, rs = centre(two)
        g = cotp[r, :]
        add_row(0, g * c)
        add_row(1, g)
        gradient = norm_back(g, c, rs, g2)
        hid[r, :] = gradient
        gl = gradient.astype(bf)
        gff[r, :] = gl
        add_row(2, gl.astype(f32))
        slope_in = dot_nt(gl, wd[...])
        u = pre[r, :]
        slope = normal_cdf(u) + u * (jnp.exp(-0.5 * u * u) * (1.0 / math.sqrt(2.0 * math.pi)))
        gp = (slope_in * slope).astype(bf)
        gpre[r, :] = gp
        add_row(3, gp.astype(f32))
        part[r, :] = dot_nt(gp, wi[...])
        sends(m, rows, 2)
        put_back(r, c * g2 + b2)

    def attend_back(m, rows):
        r = block_rows(m, rows)
        for p in pieces_of(m, rows):
            line.want(p)
        g = hid[r, :] + tot[r, :]
        c, rs = centre(res[r, :])
        add_row(4, g * c)
        add_row(5, g)
        gradient = norm_back(g, c, rs, g1)
        hid[r, :] = gradient
        gb = gradient.astype(bf)
        add_row(6, gb.astype(f32))
        gat[3 * width:4 * width, :] += dot_tn(att[r, :], gb)[0:width, :]
        gab = dot_nt(gb, wo[...]).astype(bf)
        ga[0:rows, :] = gab
        gt[...] = jnp.transpose(ga[...])
        cols = pl.ds(pl.multiple_of(m * BLOCK, BLOCK), rows)
        query_grad = None
        for h in range(heads):
            gh = jnp.where(lanes_of(h, (rows, 256)), gab, jnp.zeros((), bf))
            dp = dot_nt(gh, v_s[...])
            p = prob[h, r, :]
            inner = jnp.sum(p * dp, axis=1, keepdims=True)
            ds = (p * (dp - inner)).astype(bf)
            dqh = dot_nn(ds, k_s[...])
            query_grad = dqh if h == 0 else jnp.where(lanes_of(h, (rows, 256)), dqh, query_grad)
            base[h, 0:rows, block_window(m)] += ds.astype(f32)
            hr = pl.ds(h * HEAD_DIM, HEAD_DIM)
            dkt[hr, :] += dot_nn(qt[hr, cols], ds)
            dvt[hr, :] += dot_nn(gt[hr, 0:rows], p.astype(bf))
            u = jnp.concatenate(split2(dot_nn(ds, ob[...])), axis=1)
            gg = dot_tn(obf[r, :], u)
            for i in range(2):
                b = 128 * i
                gacc[h, i] += gg[b:b + 128, b:b + 128] + gg[b:b + 128, 256 + b:384 + b]
        dq[r, :] = jnp.where(lax.broadcasted_iota(jnp.int32, (rows, 256), 1) < width, query_grad * SCORE_SCALE, 0.0).astype(bf)

    def back_step(m, carry):
        back(m, BLOCK)

        @pl.when(m == ROWS // BLOCK - 1)
        def _():
            attend_back(0, BLOCK)
        return carry
    lax.fori_loop(0, ROWS // BLOCK, back_step, 0)
    back(ROWS // BLOCK, ROWS % BLOCK)

    gwd[...] = dot_tn(act[...], gff[...])
    cube[1].step(0)
    gwi[...] = dot_tn(hlow[...], gpre[...])
    cube[0].step(0)
    line.last([pieces - 2, pieces - 1])

    def late_step(m, carry):
        attend_back(m, BLOCK)

        @pl.when(m == 1)
        def _():
            cube[1].step(1)

        @pl.when(m == 2)
        def _():
            cube[0].step(1)
        return carry
    lax.fori_loop(1, ROWS // BLOCK, late_step, 0)
    out[...] = outp[0:n, :]
    outp[...] = jnp.zeros_like(outp)
    attend_back(ROWS // BLOCK, ROWS % BLOCK)
    dk[...] = jnp.transpose(dkt[...]).astype(bf)
    dv[...] = jnp.transpose(dvt[...]).astype(bf)

    def produce(m, rows):
        r = block_rows(m, rows)
        for p in pieces_of(m, rows):
            line.free_part(p)
        part[r, :] = dot_nn(dq[r, :], ws[0]) + dot_nn(dk[r, :], ws[1]) + dot_nn(dv[r, :], ws[2])
        for p in pieces_of(m, rows):
            line.send_end(p)
    blocks(produce)

    def table_sums(h):
        for i in range(2):
            both = jnp.concatenate([gacc[h, i], jnp.zeros((128, 128), f32)], axis=1)
            line_sum = jnp.sum(pltpu.roll(both, 0, 1, stride=1, stride_axis=0), axis=0, keepdims=True)
            sm[10 + heads * (i + 1) + h:11 + heads * (i + 1) + h, 0:BINS2] = exact_dot(line_sum, sgxy[...], ((1,), (1,)))
        flip = (lax.broadcasted_iota(jnp.int32, (128, 128), 0) + lax.broadcasted_iota(jnp.int32, (128, 128), 1)) == 127
        flip = jnp.where(flip, 1.0, 0.0).astype(bf)
        hi, lo = split2(base[h])
        turned = dot_nn(flip, hi) + dot_nn(flip, lo)
        line_sum = jnp.sum(pltpu.roll(turned, 0, 1, stride=1, stride_axis=0), axis=0, keepdims=True)
        sm[10 + h:11 + h, 0:BINS1] = exact_dot(line_sum, sgo[...], ((1,), (1,)))

    def bias_sums(_):
        sm[8:9, 0:256] = jnp.sum(dq[...].astype(f32), axis=0, keepdims=True)
        sm[9:10, 0:256] = jnp.sum(dv[...].astype(f32), axis=0, keepdims=True)

    bit_to = cube[0].to

    def small_copy(i):
        return pltpu.make_async_remote_copy(sm, rxs.at[i], ss.at[i], sr.at[i], device_id=bit_to[i], device_id_type=MESH)

    def small_step(i):
        if i > 0:
            small_copy(i - 1).wait()
            sm[...] += rxs[i - 1]
        if i < bits:
            small_copy(i).start()

    def weight_grad(i):
        gat[i * width:(i + 1) * width, :] = dot_tn((dq, dk, dv)[i][...], low[...])[0:width, :]

    def consume(m):
        rows = min(BLOCK, ROWS - m * BLOCK)
        for p in pieces_of(m, rows):
            line.want(p)
        r = slice(m * BLOCK, m * BLOCK + rows)
        put_back(r, hid[r, :] + tot[r, :])

    jobs = {1: [(bias_sums, 0), (table_sums, 0)], 2: [(table_sums, 1)], 3: [(cube[1].step, 3), (cube[0].step, 3)], 5: [(table_sums, 2)], 6: [(cube[2].step, 1), (small_step, 0)], 7: [(cube[1].step, 4), (cube[0].step, 4)], 9: [(small_step, 1)], 10: [(cube[2].step, 2)], 11: [(consume, 0)], 12: [(small_step, 2)], 13: [(consume, 1)], 14: [(cube[2].step, 3)], 15: [(small_step, 3)], 16: [(cube[1].step, 5), (cube[0].step, 5)]}
    cube[1].step(2)
    cube[0].step(2)
    for i in range(3):
        weight_grad(i)
    cube[2].step(0)
    ending = {p: [p - LAG] for p in range(LAG, pieces - 4)}
    ending.update({pieces - 4: [pieces - 8, pieces - 7], pieces - 3: [pieces - 6], pieces - 2: [pieces - 5, pieces - 4],
                   pieces - 1: [pieces - 3, pieces - 2]})
    for p in range(pieces):
        line.slot_mid(p, ending.get(p, ()))
        for job, arg in jobs.get(p, ()):
            job(arg)
    line.last([pieces - 1])
    for i in range(4, bits + 1):
        small_step(i)
    cube[2].step(4)
    consume(2)
    cube[2].step(5)
    consume(3)
    consume(4)
    for c in cube:
        c.step(6)
    gin[...] = outp[0:n, :]
    line.drain()


def layer(bits, tok, cot, wq, wk, wv, wo, wi, wd, *small_args):
    f32, bf = jnp.float32, jnp.bfloat16
    d = tok.shape[1]
    f = wi.shape[1]
    width = wo.shape[0]
    heads = small_args[12].shape[0]
    sd = jax.ShapeDtypeStruct
    W, R = WIDE_ROWS, ROWS
    pieces = R // BLOCK * BLOCK // PC + R % BLOCK // END_PC
    more = max(bits - 3, 1)
    vm, hbm = pl.BlockSpec(memory_space=pltpu.VMEM), pl.BlockSpec(memory_space=pl.ANY)
    v_ = pltpu.VMEM
    shapes = (v_((PAGE, d), f32), v_((PAGE, d), f32), v_((4 * width, d), f32), v_((d, f), f32), v_((f, d), f32), v_((24, d), f32))
    scratch = [v_((R, d), f32)] * 7 + [v_((R, f), f32), v_((R, f), bf), v_((R, d), bf), v_((R, d), bf), v_((R, f), bf)]
    scratch += [v_((W, d), bf), v_((W, W), bf)] + [v_((W, 256), bf)] * 3 + [v_((heads, R, W), f32)] + [v_((W, 256), bf)] * 3
    scratch += [v_((heads, 2, 128, 256), bf), v_((W, 512), bf), v_((W, d), bf), v_((heads, 128, 1280), f32)]
    scratch += [v_((BLOCK, 256), bf), v_((256, BLOCK), bf), v_((256, W), bf), v_((256, W), f32), v_((256, W), f32)]
    scratch += [v_((W, 256), bf)] * 3 + [v_((heads, 2, 128, 128), f32)]
    scratch += [v_((3, 256, d), bf), v_((256, d), bf), v_((d, f), bf), v_((f, d), bf), v_((W, d), f32), v_((8, W), f32), v_((16, d), f32)]
    scratch += [v_((2, d // 2, d), f32), v_((2, 2, d // 8, d), f32), v_((2, 2, d // 16, d), f32), v_((2, 2, d // 16, d), f32), v_((bits, 24, d), f32)]
    scratch += [pltpu.SemaphoreType.DMA((pieces,))] * 4 + [pltpu.SemaphoreType.DMA((3, 10 + 2 * more))] * 2
    scratch += [pltpu.SemaphoreType.REGULAR((3, max(bits, 3)))] + [pltpu.SemaphoreType.DMA((bits,))] * 2 + [pltpu.SemaphoreType.DMA((8,))]
    return pl.pallas_call(
        functools.partial(layer_kernel, bits), out_shape=shapes, in_specs=[hbm] * 8 + [vm] * 19, out_specs=[vm] * 6,
        scratch_shapes=scratch,
        compiler_params=pltpu.CompilerParams(collective_id=0, has_side_effects=True, vmem_limit_bytes=52 << 20),
        cost_estimate=pl.CostEstimate(flops=3 * 10 ** 10, bytes_accessed=20 << 20, transcendentals=heads * R * W),
    )(tok, cot, wq, wk, wv, wo, wi, wd, *small_args)


def finish_kernel(out_in, gin_in, gat_in, gwi_in, gwd_in, sm, out, gin, gwq, gwk, gwv, gwo, gwi, gwd, *rest):
    vectors, sem = rest[:12], rest[12]
    width = gwo.shape[0]
    heads = vectors[9].shape[0]
    pairs = [(out_in, out), (gin_in, gin), (gwi_in, gwi), (gwd_in, gwd)]
    pairs += [(gat_in.at[pl.ds(i * width, width)], g) for i, g in enumerate((gwq, gwk, gwv, gwo))]
    copies = [pltpu.make_async_copy(a, b, sem.at[i]) for i, (a, b) in enumerate(pairs)]
    for c in copies:
        c.start()
    for i in range(7):
        vectors[i][...] = sm[i, :]
    vectors[7][...] = sm[8, 0:width]
    vectors[8][...] = sm[9, 0:width]
    vectors[9][...] = sm[10:10 + heads, 0:BINS1]
    vectors[10][...] = sm[10 + heads:10 + 2 * heads, 0:BINS2]
    vectors[11][...] = sm[10 + 2 * heads:10 + 3 * heads, 0:BINS2]
    for c in copies:
        c.wait()


def finish(heads, width, out, gin, gat, gwi, gwd, sm):
    f32 = jnp.float32
    sd = jax.ShapeDtypeStruct
    d = gat.shape[1]
    like = lambda x: sd(x.shape, f32)
    shapes = (like(out), like(gin)) + (sd((width, d), f32),) * 4 + (like(gwi), like(gwd)) + (sd((d,), f32),) * 7 \
        + (sd((width,), f32),) * 2 + (sd((heads, BINS1), f32), sd((heads, BINS2), f32), sd((heads, BINS2), f32))
    vm, hbm = pl.BlockSpec(memory_space=pltpu.VMEM), pl.BlockSpec(memory_space=pl.ANY)
    return pl.pallas_call(
        finish_kernel, out_shape=shapes, in_specs=[vm] * 6, out_specs=[hbm] * 8 + [vm] * 12,
        scratch_shapes=[pltpu.SemaphoreType.DMA((8,))],
        compiler_params=pltpu.CompilerParams(vmem_limit_bytes=4 << 20),
    )(*(pltpu.with_memory_space_constraint(x, pltpu.VMEM) for x in (out, gin, gat, gwi, gwd, sm)))


def local(
    bits,
    tokens,
    region,
    order_rank,
    box_coords,
    w_query,
    b_query,
    w_key,
    w_value,
    b_value,
    w_out,
    b_out,
    ln1_gain,
    ln1_bias,
    w_in,
    b_in,
    w_down,
    b_down,
    ln2_gain,
    ln2_bias,
    rel_order,
    rel_x,
    rel_y,
    cotangent,
):
    so = choose_matrix([i - 512 if i < 1152 else i - 1792 for i in range(1280)], BINS1, MAX_ORDER)
    sxy = choose_matrix([i if i < 128 else i - 256 for i in range(256)], BINS2, MAX_LAYOUT)
    sgo = choose_matrix([i - 639 for i in range(1280)], BINS1, MAX_ORDER)
    sgxy = choose_matrix([i - 127 for i in range(256)], BINS2, MAX_LAYOUT)
    width = w_out.shape[0]
    heads = rel_order.shape[0]
    output, gin, gat, gwi, gwd, sm = layer(
        bits, tokens, cotangent, w_query.T, w_key.T, w_value.T, w_out, w_in, w_down, region, order_rank, box_coords, b_query, b_value,
        b_out, ln1_gain, ln1_bias, b_in, b_down, ln2_gain, ln2_bias, rel_order, rel_x, rel_y, so, sxy, sgo, sgxy)
    (output, gin, gwq, gwk, gwv, gwo, gwi, gwd, l2g, l2b, bd, bi, l1g, l1b, bo, gbq, gbv, ro, rx, ry) = finish(
        heads, width, output, gin, gat, gwi, gwd, sm)
    return (output, gin, gwq.T, gbq, gwk.T, gwv.T, gbv, gwo, bo, l1g, l1b, gwi, bi,
            gwd, bd, l2g, l2b, ro, rx, ry)


def solution(mesh):
    in_specs = (
        P("wide", None),
        P("wide"),
        P("wide"),
        P(None, "wide"),
        P(None, "narrow"),
        P("narrow"),
        P(None, "narrow"),
        P(None, "narrow"),
        P("narrow"),
        P("narrow", None),
        P(),
        P(),
        P(),
        P(None, "narrow"),
        P("narrow"),
        P("narrow", None),
        P(),
        P(),
        P(),
        P("narrow", None),
        P("narrow", None),
        P("narrow", None),
        P("wide", None),
    )
    out_specs = (
        P("wide", None),
        P("wide", None),
        P(None, "narrow"),
        P("narrow"),
        P(None, "narrow"),
        P(None, "narrow"),
        P("narrow"),
        P("narrow", None),
        P(),
        P(),
        P(),
        P(None, "narrow"),
        P("narrow"),
        P("narrow", None),
        P(),
        P(),
        P(),
        P("narrow", None),
        P("narrow", None),
        P("narrow", None),
    )
    bits = mesh.shape["wide"].bit_length() - 1
    return jax.shard_map(functools.partial(local, bits), mesh=mesh, in_specs=in_specs, out_specs=out_specs, check_vma=False)
```

```python
import functools
import math

import jax
import jax.numpy as jnp
import numpy as np
from jax import lax
from jax.experimental import pallas as pl
from jax.experimental.pallas import tpu as pltpu
from jax.sharding import PartitionSpec as P

HEAD_DIM = 64
BINS1 = 32
BINS2 = 64
MAX_ORDER = 128
MAX_LAYOUT = 256
PAGE = 561


HIGHEST = lax.Precision.HIGHEST
EPSILON = 1e-05
SCORE_SCALE = 0.125

def bucket_steps(bins, reach):
    halfway = bins // 2
    exact = halfway // 2
    steps = []
    for level in range(1, halfway):
        if level < exact:
            steps.append(level)
        else:
            found = reach + 1
            for count in range(exact, reach + 2):
                value = exact + int(
                    math.log(count / exact) / math.log(reach / exact) * (halfway - exact)
                )
                if min(value, halfway - 1) >= level:
                    found = count
                    break
            steps.append(found)
    return steps


MESH = pl.DeviceIdType.MESH
BLOCK = 128
PC = 32
END_PC = 32
SENT = -(-PAGE // 8) * 8
LAG = 4


def erf_of(x):
    x = jnp.clip(x, -3.832506856900711, 3.832506856900711)
    s = x * x
    top = -2.72614225801306e-10
    for term in (2.77068142495902e-08, -2.10102402082508e-06, -5.69250639462346e-05,
                 -7.34990630326855e-04, -2.95459980854025e-03, -1.60960333262415e-02):
        top = top * s + term
    low = -1.45660718464996e-05
    for term in (-2.13374055278905e-04, -1.68282697438203e-03, -7.37332916720468e-03,
                 -1.42647390514189e-02):
        low = low * s + term
    return x * top / low


def normal_cdf(x):
    return 0.5 + 0.5 * erf_of(x * math.sqrt(0.5))


def centre(values):
    c = values - jnp.mean(values, axis=-1, keepdims=True)
    r = lax.rsqrt(jnp.mean(c * c, axis=-1, keepdims=True) + EPSILON)
    return c * r, r


def norm_back(g, n, r, gain):
    m = g * gain
    return r * (m - jnp.mean(m, axis=-1, keepdims=True) - n * jnp.mean(m * n, axis=-1, keepdims=True))


def dot_nn(a, b):
    return lax.dot_general(a, b, (((1,), (0,)), ((), ())), preferred_element_type=jnp.float32)


def dot_nt(a, b):
    return lax.dot_general(a, b, (((1,), (1,)), ((), ())), preferred_element_type=jnp.float32)


def dot_tn(a, b):
    return lax.dot_general(a, b, (((0,), (0,)), ((), ())), preferred_element_type=jnp.float32)


class LineSum:
    def __init__(self, part, rx_in, rx_mid, tot, s_in, s_mid, r_in, r_mid):
        self.part, self.rx_in, self.rx_mid, self.tot = part, rx_in, rx_mid, tot
        self.s_in, self.s_mid, self.r_in, self.r_mid = s_in, s_mid, r_in, r_mid
        w, n = lax.axis_index("wide"), lax.axis_index("narrow")
        self.end = (n == 0) | (n == 3)
        self.mid = jnp.logical_not(self.end)
        self.side = (w, n + 1 - 2 * lax.rem(n, 2))
        self.across = (w, 3 - n)
        self.body = part.shape[0] // BLOCK * BLOCK // PC
        self.pieces = self.body + part.shape[0] % BLOCK // END_PC

    def rows(self, p):
        if not isinstance(p, int):
            return pl.ds(pl.multiple_of(p * PC, PC), PC)
        if p < self.body:
            return pl.ds(p * PC, PC)
        start = self.body * PC + (p - self.body) * END_PC
        return pl.ds(start, min(END_PC, SENT - start))

    def copy_a(self, p):
        return pltpu.make_async_remote_copy(self.part.at[self.rows(p)], self.rx_in.at[self.rows(p)],
            self.s_in.at[p], self.r_in.at[p], device_id=self.side, device_id_type=MESH)

    def copy_b(self, p):
        return pltpu.make_async_remote_copy(self.part.at[self.rows(p)], self.rx_mid.at[self.rows(p)],
            self.s_mid.at[p], self.r_mid.at[p], device_id=self.across, device_id_type=MESH)

    def copy_t(self, p):
        return pltpu.make_async_remote_copy(self.tot.at[self.rows(p)], self.tot.at[self.rows(p)],
            self.s_in.at[p], self.r_in.at[p], device_id=self.side, device_id_type=MESH)

    def signal(self):
        bar = pltpu.get_barrier_semaphore()
        pl.semaphore_signal(bar, inc=1, device_id=self.side, device_id_type=MESH)

        @pl.when(self.mid)
        def _():
            pl.semaphore_signal(bar, inc=1, device_id=self.across, device_id_type=MESH)

    def ready(self, others):
        bar = pltpu.get_barrier_semaphore()

        @pl.when(self.end)
        def _():
            pl.semaphore_wait(bar, 1 + others)

        @pl.when(self.mid)
        def _():
            pl.semaphore_wait(bar, 2 + others)

    def free_part(self, p):
        @pl.when(self.end)
        def _():
            self.copy_a(p).wait_send()

        @pl.when(self.mid)
        def _():
            self.copy_b(p).wait_send()

    def finish(self, p, first):
        self.copy_b(p).wait_recv()
        if not first:
            self.copy_t(p).wait_send()
        self.tot[self.rows(p), :] = self.part[self.rows(p), :] + self.rx_mid[self.rows(p), :]
        self.copy_t(p).start()

    def slot(self, p, order, done=None):
        @pl.when(self.end)
        def _():
            self.copy_a(p).start()

        @pl.when(self.mid)
        def _():
            self.copy_a(p).wait_recv()
            self.part[self.rows(p), :] += self.rx_in[self.rows(p), :]
            self.copy_b(p).start()

            if done is not None:
                for q in done:
                    self.finish(q, order == 0)
                return

            if isinstance(p, int):
                self.finish(p - LAG, order == 0)
                return

            @pl.when(p >= LAG)
            def _():
                self.finish(p - LAG, order == 0)

            if order > 0:
                @pl.when(p < LAG - 1)
                def _():
                    self.finish(p + self.pieces - LAG, order == 1)

                @pl.when(p == LAG - 1)
                def _():
                    self.finish(self.pieces - 1, order == 1)

    def send_end(self, p):
        @pl.when(self.end)
        def _():
            self.copy_a(p).start()

    def slot_mid(self, p, done):
        @pl.when(self.mid)
        def _():
            self.copy_a(p).wait_recv()
            self.part[self.rows(p), :] += self.rx_in[self.rows(p), :]
            self.copy_b(p).start()
            for q in done:
                self.finish(q, False)

    def last(self, pieces):
        @pl.when(self.mid)
        def _():
            for q in pieces:
                self.finish(q, False)

    def want(self, p):
        @pl.when(self.end)
        def _():
            self.copy_t(p).wait_recv()

    def drain(self):
        def one(p, c):
            self.free_part(p)

            @pl.when(self.mid)
            def _():
                self.copy_t(p).wait_send()
            return c
        lax.fori_loop(0, self.body, one, 0)
        for p in range(self.body, self.pieces):
            one(p, 0)


WIDE_ROWS = 640
ROWS = 576


def bucket_number(offset, bins, reach):
    halfway = bins // 2
    steps = bucket_steps(bins, reach)
    return (halfway if offset > 0 else 0) + sum(1 for s in steps if abs(offset) >= s)


def choose_matrix(offsets, bins, reach):
    out = np.zeros((bins, len(offsets)), np.float32)
    for place, offset in enumerate(offsets):
        out[bucket_number(offset, bins, reach), place] = 1.0
    return out


def split3(x):
    hi = x.astype(jnp.bfloat16)
    rest = x - hi.astype(jnp.float32)
    mid = rest.astype(jnp.bfloat16)
    return hi, mid, (rest - mid.astype(jnp.float32)).astype(jnp.bfloat16)


def split2(x):
    hi = x.astype(jnp.bfloat16)
    return hi, (x - hi.astype(jnp.float32)).astype(jnp.bfloat16)


def exact_dot(a, b, dims):
    return lax.dot_general(a, b, (dims, ((), ())), precision=HIGHEST, preferred_element_type=jnp.float32)


def lanes_of(h, shape):
    lane = lax.broadcasted_iota(jnp.int32, shape, 1)
    return (lane >= h * HEAD_DIM) & (lane < (h + 1) * HEAD_DIM)


def block_rows(m, n):
    return pl.ds(m * BLOCK, n) if isinstance(m, int) else pl.ds(pl.multiple_of(m * BLOCK, BLOCK), n)


def block_window(m):
    start = 512 - m * BLOCK
    return pl.ds(start if isinstance(m, int) else pl.multiple_of(start, 128), WIDE_ROWS)


class CubeSum:
    def __init__(self, ref, rx1, rx2, rx3, rxb, ssem, rsem, free, bits):
        self.ref, self.rx1, self.rx2, self.rx3, self.rxb = ref, rx1, rx2, rx3, rxb
        self.ssem, self.rsem, self.free = ssem, rsem, free
        w, n = lax.axis_index("wide"), lax.axis_index("narrow")
        self.bit = [lax.rem(lax.div(w, 2 ** i), 2) for i in range(bits)]
        self.to = [(w + 2 ** i * (1 - 2 * self.bit[i]), n) for i in range(bits)]
        self.rows = ref.shape[0]
        half = self.rows // 2
        self.half, self.stream, self.eighth, self.piece = half, half // 2, half // 4, half // 8
        self.own = self.bit[0] * half
        self.axes = ((1, 2), (2, 1))
        self.extra = range(3, bits)

    def at(self, start, size):
        return pl.ds(pl.multiple_of(start, self.piece), size)

    def base1(self, s, other):
        b = self.bit[self.axes[s][0]]
        b = 1 - b if other else b
        return self.own + s * self.stream + b * self.eighth

    def base2(self, s, other):
        b = self.bit[self.axes[s][1]]
        b = 1 - b if other else b
        return self.base1(s, False) + b * self.piece

    def copy(self, src, dst, i, axis):
        return pltpu.make_async_remote_copy(src, dst, self.ssem.at[i], self.rsem.at[i], device_id=self.to[axis],
                                            device_id_type=MESH)

    def core_out(self):
        return self.copy(self.ref.at[self.at((1 - self.bit[0]) * self.half, self.half)], self.rx1, 0, 0)

    def first(self, s):
        return self.copy(self.ref.at[self.at(self.base1(s, True), self.eighth)], self.rx2[s], 1 + s, self.axes[s][0])

    def second(self, s):
        return self.copy(self.ref.at[self.at(self.base2(s, True), self.piece)], self.rx3[s], 3 + s, self.axes[s][1])

    def back2(self, s):
        r = self.at(self.base2(s, False), self.piece)
        return self.copy(self.ref.at[r], self.rxb[s], 5 + s, self.axes[s][1])

    def back1(self, s):
        r = self.at(self.base1(s, False), self.eighth)
        return self.copy(self.ref.at[r], self.ref.at[r], 7 + s, self.axes[s][0])

    def core_back(self):
        r = self.at(self.own, self.half)
        return self.copy(self.ref.at[r], self.ref.at[r], 9, 0)

    def spare(self, e, s):
        return pl.ds((2 * (e - 3) + s) * self.piece, self.piece)

    def more(self, e, s):
        return self.copy(self.ref.at[self.at(self.base2(s, False), self.piece)], self.rx1.at[self.spare(e, s)],
                         10 + 2 * (e - 3) + s, e)

    def release(self, i, axis):
        pl.semaphore_signal(self.free.at[i], inc=1, device_id=self.to[axis], device_id_type=MESH)

    def step(self, i):
        if i == 0:
            self.core_out().start()
        if i == 1:
            self.core_out().wait_recv()
            self.ref[self.at(self.own, self.half), :] += self.rx1[...]
            for s in range(2):
                self.first(s).start()
            self.core_out().wait_send()
            self.release(0, 0)
            for e in self.extra:
                self.release(e, e)
        if i == 2:
            for s in range(2):
                self.first(s).wait()
                self.release(1 + s, self.axes[s][0])
                self.ref[self.at(self.base1(s, False), self.eighth), :] += self.rx2[s][...]
                self.second(s).start()
        if i == 3:
            for s in range(2):
                self.second(s).wait()
                self.ref[self.at(self.base2(s, False), self.piece), :] += self.rx3[s][...]
            for e in self.extra:
                pl.semaphore_wait(self.free.at[e], 1)
                for s in range(2):
                    self.more(e, s).start()
                for s in range(2):
                    self.more(e, s).wait()
                    self.ref[self.at(self.base2(s, False), self.piece), :] += self.rx1[self.spare(e, s), :]
            for s in range(2):
                self.back2(s).start()
        if i == 4:
            for s in range(2):
                self.back2(s).wait_recv()
                self.ref[self.at(self.base2(s, True), self.piece), :] = self.rxb[s][...]
                pl.semaphore_wait(self.free.at[1 + s], 1)
                self.back1(s).start()
        if i == 5:
            for s in range(2):
                self.back1(s).wait_recv()
            pl.semaphore_wait(self.free.at[0], 1)
            self.core_back().start()
        if i == 6:
            self.core_back().wait()
            for s in range(2):
                self.back2(s).wait_send()
                self.back1(s).wait_send()


def layer_kernel(bits, tok_h, cot_h, wq_h, wk_h, wv_h, wo_h, wi_h, wd_h, reg, rank, box, bq, bv, bo_r, g1_r, b1_r, bi_r, bd_r, g2_r, b2_r,
                 to, tx, ty, so, sxy, sgo, sgxy,
                 out, gin, gat, gwi, gwd, sm,
                 part, rx_in, rx_mid, tot, res, cotp, hid, pre, act, gff, hlow, gpre, low, perm,
                 q_s, k_s, v_s, prob, att, ob, obf, pairs, ob4, split_s, base, ga, gt, qt, dkt, dvt, dqkv, gacc, trow,
                 ws, wo, wi, wd, outp, rows_s, vec_s, rx1, rx2, rx3, rxb, rxs,
                 s_in, s_mid, r_in, r_mid, cs, cr, cf, ss, sr, ls):
    f32, bf = jnp.float32, jnp.bfloat16
    n = PAGE
    width = wo_h.shape[0]
    heads = to.shape[0]
    block_pieces = BLOCK // PC
    dq, dk, dv = (dqkv.at[i] for i in range(3))
    tail_pieces = ROWS % BLOCK // END_PC

    def pieces_of(m, rows):
        return [m * block_pieces + j for j in range(block_pieces if rows == BLOCK else tail_pieces)]
    line = LineSum(part, rx_in, rx_mid, tot, s_in, s_mid, r_in, r_mid)
    pieces = line.pieces
    closing = {pieces - 2: [pieces - 6, pieces - 5], pieces - 1: [pieces - 4, pieces - 3]}
    rest1, rest2, rest3, restb = pre.at[pl.ds(0, 384)], pre.at[pl.ds(384, 192)], cotp.at[pl.ds(0, 96)], cotp.at[pl.ds(96, 96)]
    cube = [CubeSum(gwi, rx1.at[0], [rx2.at[0, s] for s in range(2)], [rx3.at[0, s] for s in range(2)],
                    [rxb.at[0, s] for s in range(2)], cs.at[0], cr.at[0], cf.at[0], bits),
            CubeSum(gwd, rx1.at[1], [rx2.at[1, s] for s in range(2)], [rx3.at[1, s] for s in range(2)],
                    [rxb.at[1, s] for s in range(2)], cs.at[1], cr.at[1], cf.at[1], bits),
            CubeSum(gat, rest1, [pre.at[pl.ds(384 + 96 * s, 96)] for s in range(2)],
                    [cotp.at[pl.ds(48 * s, 48)] for s in range(2)],
                    [cotp.at[pl.ds(96 + 48 * s, 48)] for s in range(2)], cs.at[2], cr.at[2], cf.at[2], bits)]

    def load(i, src, dst):
        return pltpu.make_async_copy(src, dst, ls.at[i])
    loads = [load(0, tok_h, out)]
    loads += [load(1 + i, src, gat.at[pl.ds(i * width, width)]) for i, src in enumerate((wq_h, wk_h, wv_h, wo_h))]
    loads += [load(5, wi_h, gwi), load(6, wd_h, gwd), load(7, cot_h, gin)]
    for c in loads:
        c.start()
    bar = pltpu.get_barrier_semaphore()
    for peer in cube[0].to:
        pl.semaphore_signal(bar, inc=1, device_id=peer, device_id_type=MESH)
    line.signal()
    tot[SENT:ROWS, :] = jnp.zeros((ROWS - SENT, tot.shape[1]), f32)

    rows_s[...] = jnp.full(rows_s.shape, 1e4, f32)
    rows_s[0, 0:n] = reg[...].astype(f32)
    rows_s[1, 0:n] = rank[...].astype(f32)
    rows_s[2:4, 0:n] = box[...].astype(f32)
    region_row, rank_row = rows_s[0:1, :], rows_s[1:2, :]
    i0 = lax.broadcasted_iota(jnp.int32, (WIDE_ROWS, WIDE_ROWS), 0)
    i1 = lax.broadcasted_iota(jnp.int32, (WIDE_ROWS, WIDE_ROWS), 1)
    region_col = jnp.sum(jnp.where(i0 == i1, region_row, 0.0), axis=1, keepdims=True)
    place = jnp.sum(jnp.where(region_col < region_row, 1.0, 0.0), axis=0, keepdims=True) + rank_row
    perm[...] = jnp.where(i0.astype(f32) == place, 1.0, 0.0).astype(bf)
    split_s[...] = jnp.zeros_like(split_s)
    for i, vector in enumerate((bo_r, g1_r, b1_r, bi_r, bd_r, g2_r, b2_r)):
        vec_s[i, :] = vector[...]
    vec_s[7:9, :] = jnp.zeros((2, vec_s.shape[1]), f32)
    vec_s[7, 0:width] = bq[...]
    vec_s[8, 0:width] = bv[...]
    b_out, g1, b1, b_in, b_down, g2, b2 = (vec_s[i:i + 1, :] for i in range(7))

    def sort_first(source, target, first):
        split_s[0:n, :] = source[...].astype(bf)
        y = dot_nn(perm[...], split_s[...])
        if first is not None:
            first[...] = y.astype(bf)
        target[...] = y[0:ROWS, :]

    def sort_rest(source, target):
        for i in range(1, 3):
            split_s[0:n, :] = split3(source[...])[i]
            target[...] += dot_nn(perm[0:ROWS, :], split_s[...])

    loads[0].wait()
    sort_first(out, res, low)
    code = lax.broadcasted_iota(jnp.int32, (128, WIDE_ROWS), 0).astype(f32)
    for i in range(2):
        row = rows_s[2 + i:3 + i, :]
        one = dot_nt(perm[...], jnp.where(code == row, 1.0, 0.0).astype(bf)).astype(bf)
        ob[:, 128 * i:128 * (i + 1)] = one
        ob4[:, 256 * i:256 * i + 128] = one
        ob4[:, 256 * i + 128:256 * i + 256] = one
    ws[...] = jnp.zeros_like(ws)
    for i in range(3):
        loads[1 + i].wait()
        ws[i, 0:width, :] = gat[i * width:(i + 1) * width, :].astype(bf)
    q_s[...] = ((dot_nt(low[...], ws[0]) + vec_s[7:8, 0:256]).astype(bf) * SCORE_SCALE).astype(bf)
    k_s[...] = dot_nt(low[...], ws[1]).astype(bf)
    v_s[...] = (dot_nt(low[...], ws[2]) + vec_s[8:9, 0:256]).astype(bf)
    wo[...] = jnp.zeros_like(wo)
    loads[4].wait()
    wo[0:width, :] = gat[3 * width:4 * width, :].astype(bf)
    row_o = exact_dot(to[...], so[...], ((1,), (0,)))
    row_xy = (exact_dot(tx[...], sxy[...], ((1,), (0,))), exact_dot(ty[...], sxy[...], ((1,), (0,))))
    for h in range(heads):
        base[h] = pltpu.roll(jnp.broadcast_to(row_o[h:h + 1, :], (128, 1280)), 0, 1, stride=1, stride_axis=0)
        for i in range(2):
            table = pltpu.roll(jnp.broadcast_to(row_xy[i][h:h + 1, :], (128, 256)), 0, 1, stride=1, stride_axis=0)
            pairs[h, i] = jnp.concatenate(split2(table[:, 0:128]), axis=1)
    line.ready(bits)

    def blocks(body, start=0):
        full = ROWS // BLOCK

        def step(m, carry):
            body(m, BLOCK)
            return carry
        lax.fori_loop(start, full, step, 0)
        if ROWS % BLOCK:
            body(full, ROWS % BLOCK)

    def sends(m, rows, order):
        if rows == BLOCK:
            def one_slot(j, carry):
                line.slot(m * block_pieces + j, order)
                return carry
            lax.fori_loop(0, block_pieces, one_slot, 0)
            return
        for p in pieces_of(m, rows):
            line.slot(p, order, closing[p] if order == 2 and isinstance(p, int) else None)

    def attend(m, rows):
        r = block_rows(m, rows)
        mixed = None
        for h in range(heads):
            qh = jnp.where(lanes_of(h, (rows, 256)), q_s[r, :], jnp.zeros((), bf))
            bias = jnp.concatenate([dot_nn(ob[r, 128 * i:128 * (i + 1)], pairs[h, i]).astype(bf) for i in range(2)], axis=1)
            s = dot_nt(qh, k_s[...]) + dot_nt(bias, ob4[...]) + base[h, 0:rows, block_window(m)]
            s = jnp.where(lax.broadcasted_iota(jnp.int32, s.shape, 1) < n, s, -1e30)
            e = jnp.exp(s - jnp.max(s, axis=1, keepdims=True))
            p = e / jnp.sum(e, axis=1, keepdims=True)
            prob[h, r, :] = p
            pv = dot_nn(p.astype(bf), v_s[...])
            mixed = pv if h == 0 else jnp.where(lanes_of(h, (rows, 256)), pv, mixed)
        mixed = mixed.astype(bf)
        att[r, :] = mixed
        part[r, :] = dot_nn(mixed, wo[...])
        sends(m, rows, 0)
        if rows == BLOCK:
            pl.when(m == 1)(early_one)
            pl.when(m == 2)(early_two)

    def early_one():
        sort_rest(out, res)

    def early_two():
        loads[5].wait()
        wi[...] = gwi[...].astype(bf)
        loads[6].wait()
        wd[...] = gwd[...].astype(bf)
        sm[...] = jnp.zeros_like(sm)
    blocks(attend)

    def open_block(m, rows):
        for p in pieces_of(m, rows):
            line.want(p)
        for p in pieces_of(m, rows):
            line.free_part(p)

    def forward(m, rows):
        r = block_rows(m, rows)
        open_block(m, rows)
        one = res[r, :] + (tot[r, :] + b_out)
        res[r, :] = one
        c, _ = centre(one)
        hidden = c * g1 + b1
        hid[r, :] = hidden
        hl = hidden.astype(bf)
        hlow[r, :] = hl
        u = dot_nn(hl, wi[...]) + b_in
        pre[r, :] = u
        a = (u * normal_cdf(u)).astype(bf)
        act[r, :] = a
        part[r, :] = dot_nn(a, wd[...])
        sends(m, rows, 1)
        if rows == BLOCK:
            pl.when(m == 0)(late_one)
            pl.when(m == 1)(late_two)
            pl.when(m == 2)(late_three)

    def late_one():
        loads[7].wait()
        sort_first(gin, cotp, None)

    def late_two():
        sort_rest(gin, cotp)

    def late_three():
        for i in range(2):
            row = rows_s[2 + i:3 + i, :]
            obf[:, 128 * i:128 * (i + 1)] = dot_nt(perm[...], jnp.where(127.0 - code == row, 1.0, 0.0).astype(bf)).astype(bf)
        outp[...] = jnp.zeros_like(outp)
        qt[...] = jnp.transpose(q_s[...])
        dkt[...] = jnp.zeros_like(dkt)
        dvt[...] = jnp.zeros_like(dvt)
        base[...] = jnp.zeros_like(base)
        gacc[...] = jnp.zeros_like(gacc)
        ga[...] = jnp.zeros_like(ga)
        dq[...] = jnp.zeros_like(dq)
        gat[3 * width:4 * width, :] = jnp.zeros((width, gat.shape[1]), f32)
    blocks(forward)

    def add_row(i, value):
        sm[i:i + 1, :] += jnp.sum(value, axis=0, keepdims=True)

    def put_back(r, y):
        total = outp[...]
        for piece in split3(y):
            total = total + dot_tn(perm[r, :], piece)
        outp[...] = total

    def back(m, rows):
        r = block_rows(m, rows)
        open_block(m, rows)
        two = hid[r, :] + (tot[r, :] + b_down)
        c, rs = centre(two)
        g = cotp[r, :]
        add_row(0, g * c)
        add_row(1, g)
        gradient = norm_back(g, c, rs, g2)
        hid[r, :] = gradient
        gl = gradient.astype(bf)
        gff[r, :] = gl
        add_row(2, gl.astype(f32))
        slope_in = dot_nt(gl, wd[...])
        u = pre[r, :]
        slope = normal_cdf(u) + u * (jnp.exp(-0.5 * u * u) * (1.0 / math.sqrt(2.0 * math.pi)))
        gp = (slope_in * slope).astype(bf)
        gpre[r, :] = gp
        add_row(3, gp.astype(f32))
        part[r, :] = dot_nt(gp, wi[...])
        sends(m, rows, 2)
        put_back(r, c * g2 + b2)

    def attend_back(m, rows):
        r = block_rows(m, rows)
        for p in pieces_of(m, rows):
            line.want(p)
        g = hid[r, :] + tot[r, :]
        c, rs = centre(res[r, :])
        add_row(4, g * c)
        add_row(5, g)
        gradient = norm_back(g, c, rs, g1)
        hid[r, :] = gradient
        gb = gradient.astype(bf)
        add_row(6, gb.astype(f32))
        gat[3 * width:4 * width, :] += dot_tn(att[r, :], gb)[0:width, :]
        gab = dot_nt(gb, wo[...]).astype(bf)
        ga[0:rows, :] = gab
        gt[...] = jnp.transpose(ga[...])
        cols = pl.ds(pl.multiple_of(m * BLOCK, BLOCK), rows)
        query_grad = None
        for h in range(heads):
            gh = jnp.where(lanes_of(h, (rows, 256)), gab, jnp.zeros((), bf))
            dp = dot_nt(gh, v_s[...])
            p = prob[h, r, :]
            inner = jnp.sum(p * dp, axis=1, keepdims=True)
            ds = (p * (dp - inner)).astype(bf)
            dqh = dot_nn(ds, k_s[...])
            query_grad = dqh if h == 0 else jnp.where(lanes_of(h, (rows, 256)), dqh, query_grad)
            base[h, 0:rows, block_window(m)] += ds.astype(f32)
            hr = pl.ds(h * HEAD_DIM, HEAD_DIM)
            dkt[hr, :] += dot_nn(qt[hr, cols], ds)
            dvt[hr, :] += dot_nn(gt[hr, 0:rows], p.astype(bf))
            u = jnp.concatenate(split2(dot_nn(ds, ob[...])), axis=1)
            gg = dot_tn(obf[r, :], u)
            for i in range(2):
                b = 128 * i
                gacc[h, i] += gg[b:b + 128, b:b + 128] + gg[b:b + 128, 256 + b:384 + b]
        dq[r, :] = jnp.where(lax.broadcasted_iota(jnp.int32, (rows, 256), 1) < width, query_grad * SCORE_SCALE, 0.0).astype(bf)

    def back_step(m, carry):
        back(m, BLOCK)

        @pl.when(m == ROWS // BLOCK - 1)
        def _():
            attend_back(0, BLOCK)
        return carry
    lax.fori_loop(0, ROWS // BLOCK, back_step, 0)
    back(ROWS // BLOCK, ROWS % BLOCK)

    gwd[...] = dot_tn(act[...], gff[...])
    cube[1].step(0)
    gwi[...] = dot_tn(hlow[...], gpre[...])
    cube[0].step(0)
    line.last([pieces - 2, pieces - 1])

    def late_step(m, carry):
        attend_back(m, BLOCK)

        @pl.when(m == 1)
        def _():
            cube[1].step(1)

        @pl.when(m == 2)
        def _():
            cube[0].step(1)
        return carry
    lax.fori_loop(1, ROWS // BLOCK, late_step, 0)
    out[...] = outp[0:n, :]
    outp[...] = jnp.zeros_like(outp)
    attend_back(ROWS // BLOCK, ROWS % BLOCK)
    dk[...] = jnp.transpose(dkt[...]).astype(bf)
    dv[...] = jnp.transpose(dvt[...]).astype(bf)

    def produce(m, rows):
        r = block_rows(m, rows)
        for p in pieces_of(m, rows):
            line.free_part(p)
        part[r, :] = dot_nn(dq[r, :], ws[0]) + dot_nn(dk[r, :], ws[1]) + dot_nn(dv[r, :], ws[2])
        for p in pieces_of(m, rows):
            line.send_end(p)
    blocks(produce)

    def table_sums(_):
        flip = (lax.broadcasted_iota(jnp.int32, (128, 128), 0) + lax.broadcasted_iota(jnp.int32, (128, 128), 1)) == 127
        flip = jnp.where(flip, 1.0, 0.0).astype(bf)

        def one(h, carry):
            for i in range(2):
                both = jnp.concatenate([gacc[h, i], jnp.zeros((128, 128), f32)], axis=1)
                line_sum = jnp.sum(pltpu.roll(both, 0, 1, stride=1, stride_axis=0), axis=0, keepdims=True)
                trow[h, i + 1:i + 2, 0:BINS2] = exact_dot(line_sum, sgxy[...], ((1,), (1,)))
            hi, lo = split2(base[h])
            turned = dot_nn(flip, hi) + dot_nn(flip, lo)
            line_sum = jnp.sum(pltpu.roll(turned, 0, 1, stride=1, stride_axis=0), axis=0, keepdims=True)
            trow[h, 0:1, 0:BINS1] = exact_dot(line_sum, sgo[...], ((1,), (1,)))
            return carry
        lax.fori_loop(0, heads, one, 0)
        for h in range(heads):
            for i, bins in enumerate((BINS1, BINS2, BINS2)):
                sm[10 + heads * i + h:11 + heads * i + h, 0:bins] = trow[h, i:i + 1, 0:bins]

    def bias_sums(_):
        sm[8:9, 0:256] = jnp.sum(dq[...].astype(f32), axis=0, keepdims=True)
        sm[9:10, 0:256] = jnp.sum(dv[...].astype(f32), axis=0, keepdims=True)

    bit_to = cube[0].to

    def small_copy(i):
        return pltpu.make_async_remote_copy(sm, rxs.at[i], ss.at[i], sr.at[i], device_id=bit_to[i], device_id_type=MESH)

    def small_step(i):
        if i > 0:
            small_copy(i - 1).wait()
            sm[...] += rxs[i - 1]
        if i < bits:
            small_copy(i).start()

    def weight_grads():
        def one(i, carry):
            gat[pl.ds(pl.multiple_of(i * width, HEAD_DIM), width), :] = dot_tn(dqkv[i], low[...])[0:width, :]
            return carry
        lax.fori_loop(0, 3, one, 0)

    def consume(m):
        rows = min(BLOCK, ROWS - m * BLOCK)
        for p in pieces_of(m, rows):
            line.want(p)
        r = slice(m * BLOCK, m * BLOCK + rows)
        put_back(r, hid[r, :] + tot[r, :])

    jobs = {1: [(bias_sums, 0), (table_sums, 0)], 2: [], 3: [(cube[1].step, 3), (cube[0].step, 3)], 5: [], 6: [(cube[2].step, 1), (small_step, 0)], 7: [(cube[1].step, 4), (cube[0].step, 4)], 9: [(small_step, 1)], 10: [(cube[2].step, 2)], 11: [(consume, 0)], 12: [(small_step, 2)], 13: [(consume, 1)], 14: [(cube[2].step, 3)], 15: [(small_step, 3)], 16: [(cube[1].step, 5), (cube[0].step, 5)]}
    cube[1].step(2)
    cube[0].step(2)
    weight_grads()
    cube[2].step(0)
    ending = {p: [p - LAG] for p in range(LAG, pieces - 4)}
    ending.update({pieces - 4: [pieces - 8, pieces - 7], pieces - 3: [pieces - 6], pieces - 2: [pieces - 5, pieces - 4],
                   pieces - 1: [pieces - 3, pieces - 2]})
    for p in range(pieces):
        line.slot_mid(p, ending.get(p, ()))
        for job, arg in jobs.get(p, ()):
            job(arg)
    line.last([pieces - 1])
    for i in range(4, bits + 1):
        small_step(i)
    cube[2].step(4)
    consume(2)
    cube[2].step(5)
    consume(3)
    consume(4)
    for c in cube:
        c.step(6)
    gin[...] = outp[0:n, :]
    line.drain()


def layer(bits, tok, cot, wq, wk, wv, wo, wi, wd, *small_args):
    f32, bf = jnp.float32, jnp.bfloat16
    d = tok.shape[1]
    f = wi.shape[1]
    width = wo.shape[0]
    heads = small_args[12].shape[0]
    sd = jax.ShapeDtypeStruct
    W, R = WIDE_ROWS, ROWS
    pieces = R // BLOCK * BLOCK // PC + R % BLOCK // END_PC
    more = max(bits - 3, 1)
    vm, hbm = pl.BlockSpec(memory_space=pltpu.VMEM), pl.BlockSpec(memory_space=pl.ANY)
    v_ = pltpu.VMEM
    shapes = (v_((PAGE, d), f32), v_((PAGE, d), f32), v_((4 * width, d), f32), v_((d, f), f32), v_((f, d), f32), v_((24, d), f32))
    scratch = [v_((R, d), f32)] * 7 + [v_((R, f), f32), v_((R, f), bf), v_((R, d), bf), v_((R, d), bf), v_((R, f), bf)]
    scratch += [v_((W, d), bf), v_((W, W), bf)] + [v_((W, 256), bf)] * 3 + [v_((heads, R, W), f32)] + [v_((W, 256), bf)] * 3
    scratch += [v_((heads, 2, 128, 256), bf), v_((W, 512), bf), v_((W, d), bf), v_((heads, 128, 1280), f32)]
    scratch += [v_((BLOCK, 256), bf), v_((256, BLOCK), bf), v_((256, W), bf), v_((256, W), f32), v_((256, W), f32)]
    scratch += [v_((3, W, 256), bf), v_((heads, 2, 128, 128), f32), v_((heads, 8, 128), f32)]
    scratch += [v_((3, 256, d), bf), v_((256, d), bf), v_((d, f), bf), v_((f, d), bf), v_((W, d), f32), v_((8, W), f32), v_((16, d), f32)]
    scratch += [v_((2, d // 2, d), f32), v_((2, 2, d // 8, d), f32), v_((2, 2, d // 16, d), f32), v_((2, 2, d // 16, d), f32), v_((bits, 24, d), f32)]
    scratch += [pltpu.SemaphoreType.DMA((pieces,))] * 4 + [pltpu.SemaphoreType.DMA((3, 10 + 2 * more))] * 2
    scratch += [pltpu.SemaphoreType.REGULAR((3, max(bits, 3)))] + [pltpu.SemaphoreType.DMA((bits,))] * 2 + [pltpu.SemaphoreType.DMA((8,))]
    return pl.pallas_call(
        functools.partial(layer_kernel, bits), out_shape=shapes, in_specs=[hbm] * 8 + [vm] * 19, out_specs=[vm] * 6,
        scratch_shapes=scratch,
        compiler_params=pltpu.CompilerParams(collective_id=0, has_side_effects=True, vmem_limit_bytes=52 << 20),
        cost_estimate=pl.CostEstimate(flops=3 * 10 ** 10, bytes_accessed=20 << 20, transcendentals=heads * R * W),
    )(tok, cot, wq, wk, wv, wo, wi, wd, *small_args)


def finish_kernel(out_in, gin_in, gat_in, gwi_in, gwd_in, sm, out, gin, gwq, gwk, gwv, gwo, gwi, gwd, *rest):
    vectors, sem = rest[:12], rest[12]
    width = gwo.shape[0]
    heads = vectors[9].shape[0]
    pairs = [(out_in, out), (gin_in, gin), (gwi_in, gwi), (gwd_in, gwd)]
    pairs += [(gat_in.at[pl.ds(i * width, width)], g) for i, g in enumerate((gwq, gwk, gwv, gwo))]
    copies = [pltpu.make_async_copy(a, b, sem.at[i]) for i, (a, b) in enumerate(pairs)]
    for c in copies:
        c.start()
    for i in range(7):
        vectors[i][...] = sm[i, :]
    vectors[7][...] = sm[8, 0:width]
    vectors[8][...] = sm[9, 0:width]
    vectors[9][...] = sm[10:10 + heads, 0:BINS1]
    vectors[10][...] = sm[10 + heads:10 + 2 * heads, 0:BINS2]
    vectors[11][...] = sm[10 + 2 * heads:10 + 3 * heads, 0:BINS2]
    for c in copies:
        c.wait()


def finish(heads, width, out, gin, gat, gwi, gwd, sm):
    f32 = jnp.float32
    sd = jax.ShapeDtypeStruct
    d = gat.shape[1]
    like = lambda x: sd(x.shape, f32)
    shapes = (like(out), like(gin)) + (sd((width, d), f32),) * 4 + (like(gwi), like(gwd)) + (sd((d,), f32),) * 7 \
        + (sd((width,), f32),) * 2 + (sd((heads, BINS1), f32), sd((heads, BINS2), f32), sd((heads, BINS2), f32))
    vm, hbm = pl.BlockSpec(memory_space=pltpu.VMEM), pl.BlockSpec(memory_space=pl.ANY)
    return pl.pallas_call(
        finish_kernel, out_shape=shapes, in_specs=[vm] * 6, out_specs=[hbm] * 8 + [vm] * 12,
        scratch_shapes=[pltpu.SemaphoreType.DMA((8,))],
        compiler_params=pltpu.CompilerParams(vmem_limit_bytes=4 << 20),
    )(*(pltpu.with_memory_space_constraint(x, pltpu.VMEM) for x in (out, gin, gat, gwi, gwd, sm)))


def local(
    bits,
    tokens,
    region,
    order_rank,
    box_coords,
    w_query,
    b_query,
    w_key,
    w_value,
    b_value,
    w_out,
    b_out,
    ln1_gain,
    ln1_bias,
    w_in,
    b_in,
    w_down,
    b_down,
    ln2_gain,
    ln2_bias,
    rel_order,
    rel_x,
    rel_y,
    cotangent,
):
    so = choose_matrix([i - 512 if i < 1152 else i - 1792 for i in range(1280)], BINS1, MAX_ORDER)
    sxy = choose_matrix([i if i < 128 else i - 256 for i in range(256)], BINS2, MAX_LAYOUT)
    sgo = choose_matrix([i - 639 for i in range(1280)], BINS1, MAX_ORDER)
    sgxy = choose_matrix([i - 127 for i in range(256)], BINS2, MAX_LAYOUT)
    width = w_out.shape[0]
    heads = rel_order.shape[0]
    output, gin, gat, gwi, gwd, sm = layer(
        bits, tokens, cotangent, w_query.T, w_key.T, w_value.T, w_out, w_in, w_down, region, order_rank, box_coords, b_query, b_value,
        b_out, ln1_gain, ln1_bias, b_in, b_down, ln2_gain, ln2_bias, rel_order, rel_x, rel_y, so, sxy, sgo, sgxy)
    (output, gin, gwq, gwk, gwv, gwo, gwi, gwd, l2g, l2b, bd, bi, l1g, l1b, bo, gbq, gbv, ro, rx, ry) = finish(
        heads, width, output, gin, gat, gwi, gwd, sm)
    return (output, gin, gwq.T, gbq, gwk.T, gwv.T, gbv, gwo, bo, l1g, l1b, gwi, bi,
            gwd, bd, l2g, l2b, ro, rx, ry)


def solution(mesh):
    in_specs = (
        P("wide", None),
        P("wide"),
        P("wide"),
        P(None, "wide"),
        P(None, "narrow"),
        P("narrow"),
        P(None, "narrow"),
        P(None, "narrow"),
        P("narrow"),
        P("narrow", None),
        P(),
        P(),
        P(),
        P(None, "narrow"),
        P("narrow"),
        P("narrow", None),
        P(),
        P(),
        P(),
        P("narrow", None),
        P("narrow", None),
        P("narrow", None),
        P("wide", None),
    )
    out_specs = (
        P("wide", None),
        P("wide", None),
        P(None, "narrow"),
        P("narrow"),
        P(None, "narrow"),
        P(None, "narrow"),
        P("narrow"),
        P("narrow", None),
        P(),
        P(),
        P(),
        P(None, "narrow"),
        P("narrow"),
        P("narrow", None),
        P(),
        P(),
        P(),
        P("narrow", None),
        P("narrow", None),
        P("narrow", None),
    )
    bits = mesh.shape["wide"].bit_length() - 1
    return jax.shard_map(functools.partial(local, bits), mesh=mesh, in_specs=in_specs, out_specs=out_specs, check_vma=False)
```

```python
import functools
import math

import jax
import jax.numpy as jnp
import numpy as np
from jax import lax
from jax.experimental import pallas as pl
from jax.experimental.pallas import tpu as pltpu
from jax.sharding import PartitionSpec as P

HEAD_DIM = 64
BINS1 = 32
BINS2 = 64
MAX_ORDER = 128
MAX_LAYOUT = 256
PAGE = 561


HIGHEST = lax.Precision.HIGHEST
EPSILON = 1e-05
SCORE_SCALE = 0.125

def bucket_steps(bins, reach):
    halfway = bins // 2
    exact = halfway // 2
    steps = []
    for level in range(1, halfway):
        if level < exact:
            steps.append(level)
        else:
            found = reach + 1
            for count in range(exact, reach + 2):
                value = exact + int(
                    math.log(count / exact) / math.log(reach / exact) * (halfway - exact)
                )
                if min(value, halfway - 1) >= level:
                    found = count
                    break
            steps.append(found)
    return steps


MESH = pl.DeviceIdType.MESH
BLOCK = 128
PC = 32
END_PC = 32
SENT = -(-PAGE // 8) * 8
LAG = 4


def erf_of(x):
    x = jnp.clip(x, -3.832506856900711, 3.832506856900711)
    s = x * x
    top = -2.72614225801306e-10
    for term in (2.77068142495902e-08, -2.10102402082508e-06, -5.69250639462346e-05,
                 -7.34990630326855e-04, -2.95459980854025e-03, -1.60960333262415e-02):
        top = top * s + term
    low = -1.45660718464996e-05
    for term in (-2.13374055278905e-04, -1.68282697438203e-03, -7.37332916720468e-03,
                 -1.42647390514189e-02):
        low = low * s + term
    return x * top / low


def normal_cdf(x):
    return 0.5 + 0.5 * erf_of(x * math.sqrt(0.5))


def centre(values):
    c = values - jnp.mean(values, axis=-1, keepdims=True)
    r = lax.rsqrt(jnp.mean(c * c, axis=-1, keepdims=True) + EPSILON)
    return c * r, r


def norm_back(g, n, r, gain):
    m = g * gain
    return r * (m - jnp.mean(m, axis=-1, keepdims=True) - n * jnp.mean(m * n, axis=-1, keepdims=True))


def dot_nn(a, b):
    return lax.dot_general(a, b, (((1,), (0,)), ((), ())), preferred_element_type=jnp.float32)


def dot_nt(a, b):
    return lax.dot_general(a, b, (((1,), (1,)), ((), ())), preferred_element_type=jnp.float32)


def dot_tn(a, b):
    return lax.dot_general(a, b, (((0,), (0,)), ((), ())), preferred_element_type=jnp.float32)


class LineSum:
    def __init__(self, part, rx_in, rx_mid, tot, s_in, s_mid, r_in, r_mid):
        self.part, self.rx_in, self.rx_mid, self.tot = part, rx_in, rx_mid, tot
        self.s_in, self.s_mid, self.r_in, self.r_mid = s_in, s_mid, r_in, r_mid
        w, n = lax.axis_index("wide"), lax.axis_index("narrow")
        self.end = (n == 0) | (n == 3)
        self.mid = jnp.logical_not(self.end)
        self.side = (w, n + 1 - 2 * lax.rem(n, 2))
        self.across = (w, 3 - n)
        self.body = part.shape[0] // BLOCK * BLOCK // PC
        self.pieces = self.body + part.shape[0] % BLOCK // END_PC

    def rows(self, p):
        if not isinstance(p, int):
            return pl.ds(pl.multiple_of(p * PC, PC), PC)
        if p < self.body:
            return pl.ds(p * PC, PC)
        start = self.body * PC + (p - self.body) * END_PC
        return pl.ds(start, min(END_PC, SENT - start))

    def copy_a(self, p):
        return pltpu.make_async_remote_copy(self.part.at[self.rows(p)], self.rx_in.at[self.rows(p)],
            self.s_in.at[p], self.r_in.at[p], device_id=self.side, device_id_type=MESH)

    def copy_b(self, p):
        return pltpu.make_async_remote_copy(self.part.at[self.rows(p)], self.rx_mid.at[self.rows(p)],
            self.s_mid.at[p], self.r_mid.at[p], device_id=self.across, device_id_type=MESH)

    def copy_t(self, p):
        return pltpu.make_async_remote_copy(self.tot.at[self.rows(p)], self.tot.at[self.rows(p)],
            self.s_in.at[p], self.r_in.at[p], device_id=self.side, device_id_type=MESH)

    def signal(self):
        bar = pltpu.get_barrier_semaphore()
        pl.semaphore_signal(bar, inc=1, device_id=self.side, device_id_type=MESH)

        @pl.when(self.mid)
        def _():
            pl.semaphore_signal(bar, inc=1, device_id=self.across, device_id_type=MESH)

    def ready(self, others):
        bar = pltpu.get_barrier_semaphore()

        @pl.when(self.end)
        def _():
            pl.semaphore_wait(bar, 1 + others)

        @pl.when(self.mid)
        def _():
            pl.semaphore_wait(bar, 2 + others)

    def free_part(self, p):
        @pl.when(self.end)
        def _():
            self.copy_a(p).wait_send()

        @pl.when(self.mid)
        def _():
            self.copy_b(p).wait_send()

    def finish(self, p, first):
        self.copy_b(p).wait_recv()
        if not first:
            self.copy_t(p).wait_send()
        self.tot[self.rows(p), :] = self.part[self.rows(p), :] + self.rx_mid[self.rows(p), :]
        self.copy_t(p).start()

    def slot(self, p, order, done=None):
        @pl.when(self.end)
        def _():
            self.copy_a(p).start()

        @pl.when(self.mid)
        def _():
            self.copy_a(p).wait_recv()
            self.part[self.rows(p), :] += self.rx_in[self.rows(p), :]
            self.copy_b(p).start()

            if done is not None:
                for q in done:
                    self.finish(q, order == 0)
                return

            if isinstance(p, int):
                self.finish(p - LAG, order == 0)
                return

            @pl.when(p >= LAG)
            def _():
                self.finish(p - LAG, order == 0)

            if order > 0:
                @pl.when(p < LAG - 1)
                def _():
                    self.finish(p + self.pieces - LAG, order == 1)

                @pl.when(p == LAG - 1)
                def _():
                    self.finish(self.pieces - 1, order == 1)

    def send_end(self, p):
        @pl.when(self.end)
        def _():
            self.copy_a(p).start()

    def slot_mid(self, p, done):
        @pl.when(self.mid)
        def _():
            self.copy_a(p).wait_recv()
            self.part[self.rows(p), :] += self.rx_in[self.rows(p), :]
            self.copy_b(p).start()
            for q in done:
                self.finish(q, False)

    def last(self, pieces):
        @pl.when(self.mid)
        def _():
            for q in pieces:
                self.finish(q, False)

    def want(self, p):
        @pl.when(self.end)
        def _():
            self.copy_t(p).wait_recv()

    def drain(self):
        def one(p, c):
            self.free_part(p)

            @pl.when(self.mid)
            def _():
                self.copy_t(p).wait_send()
            return c
        lax.fori_loop(0, self.body, one, 0)
        for p in range(self.body, self.pieces):
            one(p, 0)


WIDE_ROWS = 640
ROWS = 576


def bucket_number(offset, bins, reach):
    halfway = bins // 2
    steps = bucket_steps(bins, reach)
    return (halfway if offset > 0 else 0) + sum(1 for s in steps if abs(offset) >= s)


def choose_matrix(offsets, bins, reach):
    out = np.zeros((bins, len(offsets)), np.float32)
    for place, offset in enumerate(offsets):
        out[bucket_number(offset, bins, reach), place] = 1.0
    return out


def split3(x):
    hi = x.astype(jnp.bfloat16)
    rest = x - hi.astype(jnp.float32)
    mid = rest.astype(jnp.bfloat16)
    return hi, mid, (rest - mid.astype(jnp.float32)).astype(jnp.bfloat16)


def split2(x):
    hi = x.astype(jnp.bfloat16)
    return hi, (x - hi.astype(jnp.float32)).astype(jnp.bfloat16)


def exact_dot(a, b, dims):
    return lax.dot_general(a, b, (dims, ((), ())), precision=HIGHEST, preferred_element_type=jnp.float32)


def lanes_of(h, shape):
    lane = lax.broadcasted_iota(jnp.int32, shape, 1)
    return (lane >= h * HEAD_DIM) & (lane < (h + 1) * HEAD_DIM)


def block_rows(m, n):
    return pl.ds(m * BLOCK, n) if isinstance(m, int) else pl.ds(pl.multiple_of(m * BLOCK, BLOCK), n)


def block_window(m):
    start = 512 - m * BLOCK
    return pl.ds(start if isinstance(m, int) else pl.multiple_of(start, 128), WIDE_ROWS)


class CubeSum:
    def __init__(self, ref, rx1, rx2, rx3, rxb, ssem, rsem, free, bits):
        self.ref, self.rx1, self.rx2, self.rx3, self.rxb = ref, rx1, rx2, rx3, rxb
        self.ssem, self.rsem, self.free = ssem, rsem, free
        w, n = lax.axis_index("wide"), lax.axis_index("narrow")
        self.bit = [lax.rem(lax.div(w, 2 ** i), 2) for i in range(bits)]
        self.to = [(w + 2 ** i * (1 - 2 * self.bit[i]), n) for i in range(bits)]
        self.rows = ref.shape[0]
        half = self.rows // 2
        self.half, self.stream, self.eighth, self.piece = half, half // 2, half // 4, half // 8
        self.own = self.bit[0] * half
        self.axes = ((1, 2), (2, 1))
        self.extra = range(3, bits)

    def at(self, start, size):
        return pl.ds(pl.multiple_of(start, self.piece), size)

    def base1(self, s, other):
        b = self.bit[self.axes[s][0]]
        b = 1 - b if other else b
        return self.own + s * self.stream + b * self.eighth

    def base2(self, s, other):
        b = self.bit[self.axes[s][1]]
        b = 1 - b if other else b
        return self.base1(s, False) + b * self.piece

    def copy(self, src, dst, i, axis):
        return pltpu.make_async_remote_copy(src, dst, self.ssem.at[i], self.rsem.at[i], device_id=self.to[axis],
                                            device_id_type=MESH)

    def core_out(self):
        return self.copy(self.ref.at[self.at((1 - self.bit[0]) * self.half, self.half)], self.rx1, 0, 0)

    def first(self, s):
        return self.copy(self.ref.at[self.at(self.base1(s, True), self.eighth)], self.rx2[s], 1 + s, self.axes[s][0])

    def second(self, s):
        return self.copy(self.ref.at[self.at(self.base2(s, True), self.piece)], self.rx3[s], 3 + s, self.axes[s][1])

    def back2(self, s):
        r = self.at(self.base2(s, False), self.piece)
        return self.copy(self.ref.at[r], self.rxb[s], 5 + s, self.axes[s][1])

    def back1(self, s):
        r = self.at(self.base1(s, False), self.eighth)
        return self.copy(self.ref.at[r], self.ref.at[r], 7 + s, self.axes[s][0])

    def core_back(self):
        r = self.at(self.own, self.half)
        return self.copy(self.ref.at[r], self.ref.at[r], 9, 0)

    def spare(self, e, s):
        return pl.ds((2 * (e - 3) + s) * self.piece, self.piece)

    def more(self, e, s):
        return self.copy(self.ref.at[self.at(self.base2(s, False), self.piece)], self.rx1.at[self.spare(e, s)],
                         10 + 2 * (e - 3) + s, e)

    def release(self, i, axis):
        pl.semaphore_signal(self.free.at[i], inc=1, device_id=self.to[axis], device_id_type=MESH)

    def step(self, i):
        if i == 0:
            self.core_out().start()
        if i == 1:
            self.core_out().wait_recv()
            self.ref[self.at(self.own, self.half), :] += self.rx1[...]
            for s in range(2):
                self.first(s).start()
            self.core_out().wait_send()
            self.release(0, 0)
            for e in self.extra:
                self.release(e, e)
        if i == 2:
            for s in range(2):
                self.first(s).wait()
                self.release(1 + s, self.axes[s][0])
                self.ref[self.at(self.base1(s, False), self.eighth), :] += self.rx2[s][...]
                self.second(s).start()
        if i == 3:
            for s in range(2):
                self.second(s).wait()
                self.ref[self.at(self.base2(s, False), self.piece), :] += self.rx3[s][...]
            for e in self.extra:
                pl.semaphore_wait(self.free.at[e], 1)
                for s in range(2):
                    self.more(e, s).start()
                for s in range(2):
                    self.more(e, s).wait()
                    self.ref[self.at(self.base2(s, False), self.piece), :] += self.rx1[self.spare(e, s), :]
            for s in range(2):
                self.back2(s).start()
        if i == 4:
            for s in range(2):
                self.back2(s).wait_recv()
                self.ref[self.at(self.base2(s, True), self.piece), :] = self.rxb[s][...]
                pl.semaphore_wait(self.free.at[1 + s], 1)
                self.back1(s).start()
        if i == 5:
            for s in range(2):
                self.back1(s).wait_recv()
            pl.semaphore_wait(self.free.at[0], 1)
            self.core_back().start()
        if i == 6:
            self.core_back().wait()
            for s in range(2):
                self.back2(s).wait_send()
                self.back1(s).wait_send()


def layer_kernel(bits, tok_h, cot_h, wq_h, wk_h, wv_h, wo_h, wi_h, wd_h, reg, rank, box, bq, bv, bo_r, g1_r, b1_r, bi_r, bd_r, g2_r, b2_r,
                 to, tx, ty, so, sxy, sgo, sgxy,
                 out, gin, gat, gwi, gwd, sm,
                 part, rx_in, rx_mid, tot, res, cotp, hid, pre, act, gff, hlow, gpre, low, perm,
                 q_s, k_s, v_s, prob, att, ob, obf, pairs, ob4, split_s, base, ga, gt, qt, dkt, dvt, dqkv, gacc, trow,
                 ws, wo, wi, wd, outp, rows_s, vec_s, rx1, rx2, rx3, rxb, rxs,
                 s_in, s_mid, r_in, r_mid, cs, cr, cf, ss, sr, ls):
    f32, bf = jnp.float32, jnp.bfloat16
    n = PAGE
    width = wo_h.shape[0]
    heads = to.shape[0]
    block_pieces = BLOCK // PC
    dq, dk, dv = (dqkv.at[i] for i in range(3))
    tail_pieces = ROWS % BLOCK // END_PC

    def pieces_of(m, rows):
        return [m * block_pieces + j for j in range(block_pieces if rows == BLOCK else tail_pieces)]
    line = LineSum(part, rx_in, rx_mid, tot, s_in, s_mid, r_in, r_mid)
    pieces = line.pieces
    closing = {pieces - 2: [pieces - 6, pieces - 5], pieces - 1: [pieces - 4, pieces - 3]}
    rest1, rest2, rest3, restb = pre.at[pl.ds(0, 384)], pre.at[pl.ds(384, 192)], cotp.at[pl.ds(0, 96)], cotp.at[pl.ds(96, 96)]
    cube = [CubeSum(gwi, rx1.at[0], [rx2.at[0, s] for s in range(2)], [rx3.at[0, s] for s in range(2)],
                    [rxb.at[0, s] for s in range(2)], cs.at[0], cr.at[0], cf.at[0], bits),
            CubeSum(gwd, rx1.at[1], [rx2.at[1, s] for s in range(2)], [rx3.at[1, s] for s in range(2)],
                    [rxb.at[1, s] for s in range(2)], cs.at[1], cr.at[1], cf.at[1], bits),
            CubeSum(gat, rest1, [pre.at[pl.ds(384 + 96 * s, 96)] for s in range(2)],
                    [cotp.at[pl.ds(48 * s, 48)] for s in range(2)],
                    [cotp.at[pl.ds(96 + 48 * s, 48)] for s in range(2)], cs.at[2], cr.at[2], cf.at[2], bits)]

    def load(i, src, dst):
        return pltpu.make_async_copy(src, dst, ls.at[i])
    loads = [load(0, tok_h, out)]
    loads += [load(1 + i, src, gat.at[pl.ds(i * width, width)]) for i, src in enumerate((wq_h, wk_h, wv_h, wo_h))]
    loads += [load(5, wi_h, gwi), load(6, wd_h, gwd), load(7, cot_h, gin)]
    for c in loads:
        c.start()
    bar = pltpu.get_barrier_semaphore()
    for peer in cube[0].to:
        pl.semaphore_signal(bar, inc=1, device_id=peer, device_id_type=MESH)
    line.signal()
    tot[SENT:ROWS, :] = jnp.zeros((ROWS - SENT, tot.shape[1]), f32)

    rows_s[...] = jnp.full(rows_s.shape, 1e4, f32)
    rows_s[0, 0:n] = reg[...].astype(f32)
    rows_s[1, 0:n] = rank[...].astype(f32)
    rows_s[2:4, 0:n] = box[...].astype(f32)
    region_row, rank_row = rows_s[0:1, :], rows_s[1:2, :]
    i0 = lax.broadcasted_iota(jnp.int32, (WIDE_ROWS, WIDE_ROWS), 0)
    i1 = lax.broadcasted_iota(jnp.int32, (WIDE_ROWS, WIDE_ROWS), 1)
    region_col = jnp.sum(jnp.where(i0 == i1, region_row, 0.0), axis=1, keepdims=True)
    place = jnp.sum(jnp.where(region_col < region_row, 1.0, 0.0), axis=0, keepdims=True) + rank_row
    perm[...] = jnp.where(i0.astype(f32) == place, 1.0, 0.0).astype(bf)
    split_s[...] = jnp.zeros_like(split_s)
    for i, vector in enumerate((bo_r, g1_r, b1_r, bi_r, bd_r, g2_r, b2_r)):
        vec_s[i, :] = vector[...]
    vec_s[7:9, :] = jnp.zeros((2, vec_s.shape[1]), f32)
    vec_s[7, 0:width] = bq[...]
    vec_s[8, 0:width] = bv[...]
    b_out, g1, b1, b_in, b_down, g2, b2 = (vec_s[i:i + 1, :] for i in range(7))

    def sort_first(source, target, first):
        split_s[0:n, :] = source[...].astype(bf)
        y = dot_nn(perm[...], split_s[...])
        if first is not None:
            first[...] = y.astype(bf)
        target[...] = y[0:ROWS, :]

    def sort_rest(source, target):
        for i in range(1, 3):
            split_s[0:n, :] = split3(source[...])[i]
            target[...] += dot_nn(perm[0:ROWS, :], split_s[...])

    loads[0].wait()
    sort_first(out, res, low)
    code = lax.broadcasted_iota(jnp.int32, (128, WIDE_ROWS), 0).astype(f32)
    for i in range(2):
        row = rows_s[2 + i:3 + i, :]
        one = dot_nt(perm[...], jnp.where(code == row, 1.0, 0.0).astype(bf)).astype(bf)
        ob[:, 128 * i:128 * (i + 1)] = one
        ob4[:, 256 * i:256 * i + 128] = one
        ob4[:, 256 * i + 128:256 * i + 256] = one
    ws[...] = jnp.zeros_like(ws)
    for i in range(3):
        loads[1 + i].wait()
        ws[i, 0:width, :] = gat[i * width:(i + 1) * width, :].astype(bf)
    q_s[...] = ((dot_nt(low[...], ws[0]) + vec_s[7:8, 0:256]).astype(bf) * SCORE_SCALE).astype(bf)
    k_s[...] = dot_nt(low[...], ws[1]).astype(bf)
    v_s[...] = (dot_nt(low[...], ws[2]) + vec_s[8:9, 0:256]).astype(bf)
    wo[...] = jnp.zeros_like(wo)
    loads[4].wait()
    wo[0:width, :] = gat[3 * width:4 * width, :].astype(bf)
    row_o = exact_dot(to[...], so[...], ((1,), (0,)))
    row_xy = (exact_dot(tx[...], sxy[...], ((1,), (0,))), exact_dot(ty[...], sxy[...], ((1,), (0,))))
    for h in range(heads):
        base[h] = pltpu.roll(jnp.broadcast_to(row_o[h:h + 1, :], (128, 1280)), 0, 1, stride=1, stride_axis=0)
        for i in range(2):
            table = pltpu.roll(jnp.broadcast_to(row_xy[i][h:h + 1, :], (128, 256)), 0, 1, stride=1, stride_axis=0)
            pairs[h, i] = jnp.concatenate(split2(table[:, 0:128]), axis=1)
    line.ready(bits)

    def blocks(body, start=0):
        full = ROWS // BLOCK

        def step(m, carry):
            body(m, BLOCK)
            return carry
        lax.fori_loop(start, full, step, 0)
        if ROWS % BLOCK:
            body(full, ROWS % BLOCK)

    def sends(m, rows, order):
        if rows == BLOCK:
            def one_slot(j, carry):
                line.slot(m * block_pieces + j, order)
                return carry
            lax.fori_loop(0, block_pieces, one_slot, 0)
            return
        for p in pieces_of(m, rows):
            line.slot(p, order, closing[p] if order == 2 and isinstance(p, int) else None)

    def attend(m, rows):
        r = block_rows(m, rows)
        mixed = None
        for h in range(heads):
            qh = jnp.where(lanes_of(h, (rows, 256)), q_s[r, :], jnp.zeros((), bf))
            bias = jnp.concatenate([dot_nn(ob[r, 128 * i:128 * (i + 1)], pairs[h, i]).astype(bf) for i in range(2)], axis=1)
            s = dot_nt(qh, k_s[...]) + dot_nt(bias, ob4[...]) + base[h, 0:rows, block_window(m)]
            s = jnp.where(lax.broadcasted_iota(jnp.int32, s.shape, 1) < n, s, -1e30)
            e = jnp.exp(s - jnp.max(s, axis=1, keepdims=True))
            p = e / jnp.sum(e, axis=1, keepdims=True)
            prob[h, r, :] = p
            pv = dot_nn(p.astype(bf), v_s[...])
            mixed = pv if h == 0 else jnp.where(lanes_of(h, (rows, 256)), pv, mixed)
        mixed = mixed.astype(bf)
        att[r, :] = mixed
        part[r, :] = dot_nn(mixed, wo[...])
        sends(m, rows, 0)
        if rows == BLOCK:
            pl.when(m == 1)(early_one)
            pl.when(m == 2)(early_two)

    def early_one():
        sort_rest(out, res)

    def early_two():
        loads[5].wait()
        wi[...] = gwi[...].astype(bf)
        loads[6].wait()
        wd[...] = gwd[...].astype(bf)
        sm[...] = jnp.zeros_like(sm)
    blocks(attend)

    def open_block(m, rows):
        for p in pieces_of(m, rows):
            line.want(p)
        for p in pieces_of(m, rows):
            line.free_part(p)

    def forward(m, rows):
        r = block_rows(m, rows)
        open_block(m, rows)
        one = res[r, :] + (tot[r, :] + b_out)
        res[r, :] = one
        c, _ = centre(one)
        hidden = c * g1 + b1
        hid[r, :] = hidden
        hl = hidden.astype(bf)
        hlow[r, :] = hl
        u = dot_nn(hl, wi[...]) + b_in
        pre[r, :] = u
        a = (u * normal_cdf(u)).astype(bf)
        act[r, :] = a
        part[r, :] = dot_nn(a, wd[...])
        sends(m, rows, 1)
        if rows == BLOCK:
            pl.when(m == 0)(late_one)
            pl.when(m == 1)(late_two)
            pl.when(m == 2)(late_three)

    def late_one():
        loads[7].wait()
        sort_first(gin, cotp, None)

    def late_two():
        sort_rest(gin, cotp)

    def late_three():
        for i in range(2):
            row = rows_s[2 + i:3 + i, :]
            obf[:, 128 * i:128 * (i + 1)] = dot_nt(perm[...], jnp.where(127.0 - code == row, 1.0, 0.0).astype(bf)).astype(bf)
        outp[...] = jnp.zeros_like(outp)
        qt[...] = jnp.transpose(q_s[...])
        dkt[...] = jnp.zeros_like(dkt)
        dvt[...] = jnp.zeros_like(dvt)
        base[...] = jnp.zeros_like(base)
        gacc[...] = jnp.zeros_like(gacc)
        ga[...] = jnp.zeros_like(ga)
        dq[...] = jnp.zeros_like(dq)
        gat[3 * width:4 * width, :] = jnp.zeros((width, gat.shape[1]), f32)
    blocks(forward)

    def add_row(i, value):
        sm[i:i + 1, :] += jnp.sum(value, axis=0, keepdims=True)

    def put_back(r, y):
        total = outp[...]
        for piece in split3(y):
            total = total + dot_tn(perm[r, :], piece)
        outp[...] = total

    def back(m, rows):
        r = block_rows(m, rows)
        open_block(m, rows)
        two = hid[r, :] + (tot[r, :] + b_down)
        c, rs = centre(two)
        g = cotp[r, :]
        add_row(0, g * c)
        add_row(1, g)
        gradient = norm_back(g, c, rs, g2)
        hid[r, :] = gradient
        gl = gradient.astype(bf)
        gff[r, :] = gl
        add_row(2, gl.astype(f32))
        slope_in = dot_nt(gl, wd[...])
        u = pre[r, :]
        slope = normal_cdf(u) + u * (jnp.exp(-0.5 * u * u) * (1.0 / math.sqrt(2.0 * math.pi)))
        gp = (slope_in * slope).astype(bf)
        gpre[r, :] = gp
        add_row(3, gp.astype(f32))
        part[r, :] = dot_nt(gp, wi[...])
        sends(m, rows, 2)
        put_back(r, c * g2 + b2)

    def attend_back(m, rows):
        r = block_rows(m, rows)
        for p in pieces_of(m, rows):
            line.want(p)
        g = hid[r, :] + tot[r, :]
        c, rs = centre(res[r, :])
        add_row(4, g * c)
        add_row(5, g)
        gradient = norm_back(g, c, rs, g1)
        hid[r, :] = gradient
        gb = gradient.astype(bf)
        add_row(6, gb.astype(f32))
        gat[3 * width:4 * width, :] += dot_tn(att[r, :], gb)[0:width, :]
        gab = dot_nt(gb, wo[...]).astype(bf)
        ga[0:rows, :] = gab
        gt[...] = jnp.transpose(ga[...])
        cols = pl.ds(pl.multiple_of(m * BLOCK, BLOCK), rows)
        query_grad = None
        for h in range(heads):
            gh = jnp.where(lanes_of(h, (rows, 256)), gab, jnp.zeros((), bf))
            dp = dot_nt(gh, v_s[...])
            p = prob[h, r, :]
            inner = jnp.sum(p * dp, axis=1, keepdims=True)
            ds = (p * (dp - inner)).astype(bf)
            dqh = dot_nn(ds, k_s[...])
            query_grad = dqh if h == 0 else jnp.where(lanes_of(h, (rows, 256)), dqh, query_grad)
            base[h, 0:rows, block_window(m)] += ds.astype(f32)
            hr = pl.ds(h * HEAD_DIM, HEAD_DIM)
            dkt[hr, :] += dot_nn(qt[hr, cols], ds)
            dvt[hr, :] += dot_nn(gt[hr, 0:rows], p.astype(bf))
            u = jnp.concatenate(split2(dot_nn(ds, ob[...])), axis=1)
            gg = dot_tn(obf[r, :], u)
            for i in range(2):
                b = 128 * i
                gacc[h, i] += gg[b:b + 128, b:b + 128] + gg[b:b + 128, 256 + b:384 + b]
        dq[r, :] = jnp.where(lax.broadcasted_iota(jnp.int32, (rows, 256), 1) < width, query_grad * SCORE_SCALE, 0.0).astype(bf)

    def back_step(m, carry):
        back(m, BLOCK)

        @pl.when(m == ROWS // BLOCK - 1)
        def _():
            attend_back(0, BLOCK)
        return carry
    lax.fori_loop(0, ROWS // BLOCK, back_step, 0)
    back(ROWS // BLOCK, ROWS % BLOCK)

    gwd[...] = dot_tn(act[...], gff[...])
    cube[1].step(0)
    gwi[...] = dot_tn(hlow[...], gpre[...])
    cube[0].step(0)
    line.last([pieces - 2, pieces - 1])

    def late_step(m, carry):
        attend_back(m, BLOCK)

        @pl.when(m == 1)
        def _():
            cube[1].step(1)

        @pl.when(m == 2)
        def _():
            cube[0].step(1)
        return carry
    lax.fori_loop(1, ROWS // BLOCK, late_step, 0)
    out[...] = outp[0:n, :]
    outp[...] = jnp.zeros_like(outp)
    attend_back(ROWS // BLOCK, ROWS % BLOCK)
    dk[...] = jnp.transpose(dkt[...]).astype(bf)
    dv[...] = jnp.transpose(dvt[...]).astype(bf)

    def produce(m, rows):
        r = block_rows(m, rows)
        for p in pieces_of(m, rows):
            line.free_part(p)
        part[r, :] = dot_nn(dq[r, :], ws[0]) + dot_nn(dk[r, :], ws[1]) + dot_nn(dv[r, :], ws[2])
        for p in pieces_of(m, rows):
            line.send_end(p)
    blocks(produce)

    def table_sums(_):
        flip = (lax.broadcasted_iota(jnp.int32, (128, 128), 0) + lax.broadcasted_iota(jnp.int32, (128, 128), 1)) == 127
        flip = jnp.where(flip, 1.0, 0.0).astype(bf)

        def one(h, carry):
            for i in range(2):
                both = jnp.concatenate([gacc[h, i], jnp.zeros((128, 128), f32)], axis=1)
                line_sum = jnp.sum(pltpu.roll(both, 0, 1, stride=1, stride_axis=0), axis=0, keepdims=True)
                trow[h, i + 1:i + 2, 0:BINS2] = exact_dot(line_sum, sgxy[...], ((1,), (1,)))
            hi, lo = split2(base[h])
            turned = dot_nn(flip, hi) + dot_nn(flip, lo)
            line_sum = jnp.sum(pltpu.roll(turned, 0, 1, stride=1, stride_axis=0), axis=0, keepdims=True)
            trow[h, 0:1, 0:BINS1] = exact_dot(line_sum, sgo[...], ((1,), (1,)))
            return carry
        lax.fori_loop(0, heads, one, 0)
        for h in range(heads):
            for i, bins in enumerate((BINS1, BINS2, BINS2)):
                sm[10 + heads * i + h:11 + heads * i + h, 0:bins] = trow[h, i:i + 1, 0:bins]

    def bias_sums(_):
        sm[8:9, 0:256] = jnp.sum(dq[...].astype(f32), axis=0, keepdims=True)
        sm[9:10, 0:256] = jnp.sum(dv[...].astype(f32), axis=0, keepdims=True)

    bit_to = cube[0].to

    def small_copy(i):
        return pltpu.make_async_remote_copy(sm, rxs.at[i], ss.at[i], sr.at[i], device_id=bit_to[i], device_id_type=MESH)

    def small_step(i):
        if i > 0:
            small_copy(i - 1).wait()
            sm[...] += rxs[i - 1]
        if i < bits:
            small_copy(i).start()

    def weight_grads():
        def one(i, carry):
            gat[pl.ds(pl.multiple_of(i * width, HEAD_DIM), width), :] = dot_tn(dqkv[i], low[...])[0:width, :]
            return carry
        lax.fori_loop(0, 3, one, 0)

    def consume(m):
        rows = min(BLOCK, ROWS - m * BLOCK)
        for p in pieces_of(m, rows):
            line.want(p)
        r = slice(m * BLOCK, m * BLOCK + rows)
        put_back(r, hid[r, :] + tot[r, :])

    jobs = {1: [(bias_sums, 0), (table_sums, 0)], 2: [], 3: [(cube[1].step, 3), (cube[0].step, 3)], 5: [], 6: [(cube[2].step, 1), (small_step, 0)], 7: [(cube[1].step, 4), (cube[0].step, 4)], 9: [(small_step, 1)], 10: [(cube[2].step, 2)], 11: [(consume, 0)], 12: [(small_step, 2)], 13: [(consume, 1)], 14: [(cube[2].step, 3)], 15: [(small_step, 3)], 17: [(cube[1].step, 5), (cube[0].step, 5)]}
    cube[1].step(2)
    cube[0].step(2)
    weight_grads()
    cube[2].step(0)
    ending = {p: [p - LAG] for p in range(LAG, pieces - 4)}
    ending.update({pieces - 4: [pieces - 8, pieces - 7], pieces - 3: [pieces - 6], pieces - 2: [pieces - 5, pieces - 4],
                   pieces - 1: [pieces - 3, pieces - 2]})
    for p in range(pieces):
        line.slot_mid(p, ending.get(p, ()))
        for job, arg in jobs.get(p, ()):
            job(arg)
    line.last([pieces - 1])
    for i in range(4, bits + 1):
        small_step(i)
    cube[2].step(4)
    consume(2)
    cube[2].step(5)
    consume(3)
    consume(4)
    for c in cube:
        c.step(6)
    gin[...] = outp[0:n, :]
    line.drain()


def layer(bits, tok, cot, wq, wk, wv, wo, wi, wd, *small_args):
    f32, bf = jnp.float32, jnp.bfloat16
    d = tok.shape[1]
    f = wi.shape[1]
    width = wo.shape[0]
    heads = small_args[12].shape[0]
    sd = jax.ShapeDtypeStruct
    W, R = WIDE_ROWS, ROWS
    pieces = R // BLOCK * BLOCK // PC + R % BLOCK // END_PC
    more = max(bits - 3, 1)
    vm, hbm = pl.BlockSpec(memory_space=pltpu.VMEM), pl.BlockSpec(memory_space=pl.ANY)
    v_ = pltpu.VMEM
    shapes = (v_((PAGE, d), f32), v_((PAGE, d), f32), v_((4 * width, d), f32), v_((d, f), f32), v_((f, d), f32), v_((24, d), f32))
    scratch = [v_((R, d), f32)] * 7 + [v_((R, f), f32), v_((R, f), bf), v_((R, d), bf), v_((R, d), bf), v_((R, f), bf)]
    scratch += [v_((W, d), bf), v_((W, W), bf)] + [v_((W, 256), bf)] * 3 + [v_((heads, R, W), f32)] + [v_((W, 256), bf)] * 3
    scratch += [v_((heads, 2, 128, 256), bf), v_((W, 512), bf), v_((W, d), bf), v_((heads, 128, 1280), f32)]
    scratch += [v_((BLOCK, 256), bf), v_((256, BLOCK), bf), v_((256, W), bf), v_((256, W), f32), v_((256, W), f32)]
    scratch += [v_((3, W, 256), bf), v_((heads, 2, 128, 128), f32), v_((heads, 8, 128), f32)]
    scratch += [v_((3, 256, d), bf), v_((256, d), bf), v_((d, f), bf), v_((f, d), bf), v_((W, d), f32), v_((8, W), f32), v_((16, d), f32)]
    scratch += [v_((2, d // 2, d), f32), v_((2, 2, d // 8, d), f32), v_((2, 2, d // 16, d), f32), v_((2, 2, d // 16, d), f32), v_((bits, 24, d), f32)]
    scratch += [pltpu.SemaphoreType.DMA((pieces,))] * 4 + [pltpu.SemaphoreType.DMA((3, 10 + 2 * more))] * 2
    scratch += [pltpu.SemaphoreType.REGULAR((3, max(bits, 3)))] + [pltpu.SemaphoreType.DMA((bits,))] * 2 + [pltpu.SemaphoreType.DMA((8,))]
    return pl.pallas_call(
        functools.partial(layer_kernel, bits), out_shape=shapes, in_specs=[hbm] * 8 + [vm] * 19, out_specs=[vm] * 6,
        scratch_shapes=scratch,
        compiler_params=pltpu.CompilerParams(collective_id=0, has_side_effects=True, vmem_limit_bytes=52 << 20),
        cost_estimate=pl.CostEstimate(flops=3 * 10 ** 10, bytes_accessed=20 << 20, transcendentals=heads * R * W),
    )(tok, cot, wq, wk, wv, wo, wi, wd, *small_args)


def finish_kernel(out_in, gin_in, gat_in, gwi_in, gwd_in, sm, out, gin, gwq, gwk, gwv, gwo, gwi, gwd, *rest):
    vectors, sem = rest[:12], rest[12]
    width = gwo.shape[0]
    heads = vectors[9].shape[0]
    pairs = [(out_in, out), (gin_in, gin), (gwi_in, gwi), (gwd_in, gwd)]
    pairs += [(gat_in.at[pl.ds(i * width, width)], g) for i, g in enumerate((gwq, gwk, gwv, gwo))]
    copies = [pltpu.make_async_copy(a, b, sem.at[i]) for i, (a, b) in enumerate(pairs)]
    for c in copies:
        c.start()
    for i in range(7):
        vectors[i][...] = sm[i, :]
    vectors[7][...] = sm[8, 0:width]
    vectors[8][...] = sm[9, 0:width]
    vectors[9][...] = sm[10:10 + heads, 0:BINS1]
    vectors[10][...] = sm[10 + heads:10 + 2 * heads, 0:BINS2]
    vectors[11][...] = sm[10 + 2 * heads:10 + 3 * heads, 0:BINS2]
    for c in copies:
        c.wait()


def finish(heads, width, out, gin, gat, gwi, gwd, sm):
    f32 = jnp.float32
    sd = jax.ShapeDtypeStruct
    d = gat.shape[1]
    like = lambda x: sd(x.shape, f32)
    shapes = (like(out), like(gin)) + (sd((width, d), f32),) * 4 + (like(gwi), like(gwd)) + (sd((d,), f32),) * 7 \
        + (sd((width,), f32),) * 2 + (sd((heads, BINS1), f32), sd((heads, BINS2), f32), sd((heads, BINS2), f32))
    vm, hbm = pl.BlockSpec(memory_space=pltpu.VMEM), pl.BlockSpec(memory_space=pl.ANY)
    return pl.pallas_call(
        finish_kernel, out_shape=shapes, in_specs=[vm] * 6, out_specs=[hbm] * 8 + [vm] * 12,
        scratch_shapes=[pltpu.SemaphoreType.DMA((8,))],
        compiler_params=pltpu.CompilerParams(vmem_limit_bytes=4 << 20),
    )(*(pltpu.with_memory_space_constraint(x, pltpu.VMEM) for x in (out, gin, gat, gwi, gwd, sm)))


def local(
    bits,
    tokens,
    region,
    order_rank,
    box_coords,
    w_query,
    b_query,
    w_key,
    w_value,
    b_value,
    w_out,
    b_out,
    ln1_gain,
    ln1_bias,
    w_in,
    b_in,
    w_down,
    b_down,
    ln2_gain,
    ln2_bias,
    rel_order,
    rel_x,
    rel_y,
    cotangent,
):
    so = choose_matrix([i - 512 if i < 1152 else i - 1792 for i in range(1280)], BINS1, MAX_ORDER)
    sxy = choose_matrix([i if i < 128 else i - 256 for i in range(256)], BINS2, MAX_LAYOUT)
    sgo = choose_matrix([i - 639 for i in range(1280)], BINS1, MAX_ORDER)
    sgxy = choose_matrix([i - 127 for i in range(256)], BINS2, MAX_LAYOUT)
    width = w_out.shape[0]
    heads = rel_order.shape[0]
    output, gin, gat, gwi, gwd, sm = layer(
        bits, tokens, cotangent, w_query.T, w_key.T, w_value.T, w_out, w_in, w_down, region, order_rank, box_coords, b_query, b_value,
        b_out, ln1_gain, ln1_bias, b_in, b_down, ln2_gain, ln2_bias, rel_order, rel_x, rel_y, so, sxy, sgo, sgxy)
    (output, gin, gwq, gwk, gwv, gwo, gwi, gwd, l2g, l2b, bd, bi, l1g, l1b, bo, gbq, gbv, ro, rx, ry) = finish(
        heads, width, output, gin, gat, gwi, gwd, sm)
    return (output, gin, gwq.T, gbq, gwk.T, gwv.T, gbv, gwo, bo, l1g, l1b, gwi, bi,
            gwd, bd, l2g, l2b, ro, rx, ry)


def solution(mesh):
    in_specs = (
        P("wide", None),
        P("wide"),
        P("wide"),
        P(None, "wide"),
        P(None, "narrow"),
        P("narrow"),
        P(None, "narrow"),
        P(None, "narrow"),
        P("narrow"),
        P("narrow", None),
        P(),
        P(),
        P(),
        P(None, "narrow"),
        P("narrow"),
        P("narrow", None),
        P(),
        P(),
        P(),
        P("narrow", None),
        P("narrow", None),
        P("narrow", None),
        P("wide", None),
    )
    out_specs = (
        P("wide", None),
        P("wide", None),
        P(None, "narrow"),
        P("narrow"),
        P(None, "narrow"),
        P(None, "narrow"),
        P("narrow"),
        P("narrow", None),
        P(),
        P(),
        P(),
        P(None, "narrow"),
        P("narrow"),
        P("narrow", None),
        P(),
        P(),
        P(),
        P("narrow", None),
        P("narrow", None),
        P("narrow", None),
    )
    bits = mesh.shape["wide"].bit_length() - 1
    return jax.shard_map(functools.partial(local, bits), mesh=mesh, in_specs=in_specs, out_specs=out_specs, check_vma=False)
```
